32 devices in a mesh: req: 8 (over z, y), tp: 4 (over x, core).
Axes of the slice: x: 2, y: 2, z: 4, core: 2. Of those that a mesh axis runs over, the one named last changes fastest.
Arguments:
- tokens: bfloat16 [4096, 2048], P('req')
- token_request_number: int32 [8, 512], P('req'), may hold values from 0 to 7, never falling along the last dimension, each value on 1 to 256 neighbouring positions
- request_adapter_position: int32 [8, 8], P('req'), may hold values from 0 to 15
- adapters_in_use: int32 [16], replicated, may hold values from 0 to 15, as said below
- adapter_storage_slot: int32 [16], replicated, may hold values from 0 to 15, each once
- input_norm_gain: bfloat16 [2048], replicated, may hold values from 0.5 to 1.5
- query_weight: bfloat16 [2048, 2048], P('req', 'tp')
- key_weight: bfloat16 [2048, 2048], P('req', 'tp')
- value_weight: bfloat16 [2048, 2048], P('req', 'tp'), may hold values from -0.125 to 0.125
- output_weight: bfloat16 [2048, 2048], P('tp', 'req'), may hold values from -0.125 to 0.125
- adapter_down_weight: bfloat16 [16, 2, 16, 2048], P('req'), may hold values from -0.125 to 0.125
- adapter_up_weight: bfloat16 [16, 2, 16, 2048], P('req', None, None, 'tp'), may hold values from -0.75 to 0.75
Outputs:
- layer_out: bfloat16 [4096, 2048], P('req', 'tp')
The draws below stay inside these ranges and needn't reach their ends.
Inputs may be any that keep to these rules, and one draw needn't show every extreme that they name: `adapters_in_use`: 16 different adapter numbers; 0 and 15 are always among them. `token_request_number`: the 512 tokens of each index of req form exactly 8 requests in order, each of 1 to 256 tokens, and one of exactly 256.
All inputs are finite; a program needn't handle non-finite values.
Results may differ from the reference program's by a relative error of at most 0.01.
Values may be sent and summed in bfloat16 or wider, within the bound.
A program may use at most 64 MiB of HBM per device.

```python
import math
import jax
import jax.numpy as jnp
import numpy as np
from jax import lax

MODEL_WIDTH = 2048
ATTENTION_HEADS = 32
HEAD_WIDTH = 64
ADAPTER_RANK = 16
ACTIVE = 16
PROMPT_TOKENS = 512
REQ_DEV = 8
MOST_LEN = 256
TOKENS = 4096
STORED_ADAPTERS = 16
N_REQ = 8


def shared_query(key):
    return jax.random.normal(jax.random.fold_in(key, 11), (MODEL_WIDTH, MODEL_WIDTH), jnp.float32) * MODEL_WIDTH ** (-0.5)


def draw_query_weight(key, part):
    return shared_query(key).astype(jnp.bfloat16)


def draw_key_weight(key, part):
    own_part = jax.random.normal(jax.random.fold_in(key, 12), (MODEL_WIDTH, MODEL_WIDTH), jnp.float32) * MODEL_WIDTH ** (-0.5)
    return own_part.astype(jnp.bfloat16)


def draw_tokens(key, part):
    base = jax.random.normal(jax.random.fold_in(key, 21), (TOKENS, MODEL_WIDTH), jnp.float32)
    return jnp.clip(base, -6.0, 6.0).astype(jnp.bfloat16)


def draw_adapters_in_use(key, part):
    middle = jax.random.permutation(jax.random.fold_in(key, 31), STORED_ADAPTERS - 2).astype(jnp.int32) + 1
    chosen = jnp.concatenate([jnp.array([0, STORED_ADAPTERS - 1], jnp.int32), middle[:ACTIVE - 2]])
    return jax.random.permutation(jax.random.fold_in(key, 32), chosen).astype(jnp.int32)


def set_ends(drawn, stream_key, least, largest):
    longest = drawn.shape.index(max(drawn.shape))
    spots = []
    for shift in (0, 1):
        where = [jax.random.randint(jax.random.fold_in(stream_key, axis), (), 0, length) for axis, length in enumerate(drawn.shape)]
        where[longest] = (where[longest] + shift) % drawn.shape[longest]
        spots.append(tuple(where))
    return drawn.at[spots[0]].set(least).at[spots[1]].set(largest)


def levels(stream_key, shape, shards, least, top_value):
    level, own = 1.0, jax.random.fold_in(stream_key, 6)
    for dim, shards_of in shards:
        heights = jnp.exp(jax.random.uniform(jax.random.fold_in(own, dim), (shards_of,), jnp.float32, least / len(shards), top_value / len(shards)))
        level = level * jnp.repeat(heights, shape[dim] // shards_of).reshape([-1 if axis == dim else 1 for axis in range(len(shape))])
    return level


def split_up(amount, total, limit, skew):
    portions = [(1 << 20) // math.isqrt(grade ** skew) + 1 for grade in range(2, amount + 1)]
    spare, holding = total - limit - (amount - 1), [1] * (amount - 1)
    while spare > 0:
        candidates = [i for i in range(amount - 1) if holding[i] < limit]
        pool, left = sum([portions[i] for i in candidates]), spare
        for i in candidates:
            more = min(limit - holding[i], max(1, left * portions[i] // pool), spare)
            holding[i] = holding[i] + more
            spare = spare - more
    return np.array([limit] + holding)


def uneven(own_key, number_of, total, most, lean):
    if number_of == 2:
        one = jax.random.randint(own_key, (), max(1, total - most), min(most, total - 1) + 1)
        return jnp.stack([one, total - one])
    lengths = jnp.asarray(split_up(number_of, total, most, lean), jnp.int32)
    twos = (number_of - 1) // 2
    giver, taker = lengths[1:1 + 2 * twos:2], lengths[2:2 + 2 * twos:2]
    slack = jnp.minimum(giver - 1, most - taker)
    shifted = jax.random.randint(jax.random.fold_in(own_key, 1), (twos,), 0, 1 << 20) % (slack + 1)
    lengths = lengths.at[1:1 + 2 * twos:2].set(giver - shifted).at[2:2 + 2 * twos:2].set(taker + shifted)
    return lengths[jax.random.permutation(jax.random.fold_in(own_key, 2), number_of)]


def bell_draw(rng, dims, scale, reach, pieces=(), kind=jnp.bfloat16):
    factor_of = levels(rng, dims, pieces, -0.22, 0.18) if pieces else 1.0
    drawn = jax.random.normal(rng, dims, jnp.float32) * scale * factor_of
    return jnp.minimum(jnp.maximum(drawn, -reach), reach).astype(kind)


def setup_inputs(seed: int = 0) -> dict:
    key_list = jax.random.split(jax.random.key(seed), 13)
    return {
        "tokens": draw_tokens(jax.random.fold_in(key_list[12], 71), 0),
        "token_request_number": jax.vmap(lambda own: jnp.searchsorted(jnp.cumsum(uneven(own, REQ_DEV, PROMPT_TOKENS, MOST_LEN, 2)), jnp.arange(PROMPT_TOKENS), side="right"))(jax.random.split(key_list[1], N_REQ)).reshape((N_REQ, PROMPT_TOKENS)).astype(jnp.int32),
        "request_adapter_position": set_ends(jax.random.randint(key_list[2], (N_REQ, REQ_DEV), 0, ACTIVE), jax.random.fold_in(key_list[2], 1), 0, ACTIVE - 1).astype(jnp.int32),
        "adapters_in_use": draw_adapters_in_use(jax.random.fold_in(key_list[12], 71), 0),
        "adapter_storage_slot": jax.random.permutation(key_list[4], STORED_ADAPTERS).astype(jnp.int32),
        "input_norm_gain": jnp.clip(jax.random.uniform(key_list[5], (MODEL_WIDTH,), jnp.float32, 0.5, 1.5), 0.5, 1.5).astype(jnp.bfloat16),
        "query_weight": draw_query_weight(jax.random.fold_in(key_list[12], 71), 0),
        "key_weight": draw_key_weight(jax.random.fold_in(key_list[12], 71), 0),
        "value_weight": bell_draw(key_list[8], (MODEL_WIDTH, MODEL_WIDTH), MODEL_WIDTH ** -0.5, 0.125, ((0, 8), (1, 4))),
        "output_weight": bell_draw(key_list[9], (MODEL_WIDTH, MODEL_WIDTH), MODEL_WIDTH ** -0.5, 0.125, ((0, 4), (1, 8))),
        "adapter_down_weight": bell_draw(key_list[10], (STORED_ADAPTERS, 2, ADAPTER_RANK, MODEL_WIDTH), MODEL_WIDTH ** -0.5, 0.125, ((0, 8),)),
        "adapter_up_weight": bell_draw(key_list[11], (STORED_ADAPTERS, 2, ADAPTER_RANK, MODEL_WIDTH), (4 * ADAPTER_RANK) ** -0.5, 0.75, ((0, 8), (3, 4))),
    }


norm_eps = 1e-05
rope_base = 130000.0
adapter_scale = 2.0

def positions_of(segment):
    ordinal = jnp.arange(segment.shape[0], dtype=jnp.int32)
    starts = jnp.concatenate([jnp.ones((1,), jnp.bool_), segment[1:] != segment[:-1]])
    segment_start = lax.cummax(jnp.where(starts, ordinal, jnp.zeros_like(ordinal)), axis=0)
    return ordinal - segment_start

def apply_rotation(values, token_positions):
    half_dim = HEAD_WIDTH // 2
    frequency = rope_base ** (-(jnp.arange(half_dim, dtype=jnp.float32) * 2.0 / HEAD_WIDTH))
    angles = token_positions.astype(jnp.float32)[:, None] * frequency[None, :]
    cosine = jnp.cos(angles)[:, None, :]
    sine_part = jnp.sin(angles)[:, None, :]
    first_half = values[..., :half_dim]
    second_half = values[..., half_dim:]
    return jnp.concatenate([first_half * cosine - second_half * sine_part, second_half * cosine + first_half * sine_part], axis=-1)

def attend(query_per_head, key_heads, value_per_head, segment):
    scores = jnp.einsum('qhd,khd->hqk', query_per_head.astype(jnp.float32), key_heads.astype(jnp.float32)) * 0.125
    ordinal = jnp.arange(segment.shape[0], dtype=jnp.int32)
    allowed = (segment[:, None] == segment[None, :]) & (ordinal[None, :] <= ordinal[:, None])
    scores = jnp.where(allowed[None], scores, jnp.float32(-1e+30))
    row_peak = lax.optimization_barrier(jnp.max(scores, axis=-1, keepdims=True))
    exponent = jnp.where(allowed[None], jnp.exp(scores - row_peak), jnp.float32(0.0))
    weights = (exponent / lax.optimization_barrier(jnp.sum(exponent, axis=-1, keepdims=True))).astype(jnp.bfloat16)
    return jnp.einsum('hqk,khd->qhd', weights.astype(jnp.float32), value_per_head.astype(jnp.float32)).astype(jnp.bfloat16)

def reference(tokens, token_request_number, request_adapter_position, adapters_in_use, adapter_storage_slot, input_norm_gain, query_weight, key_weight, value_weight, output_weight, adapter_down_weight, adapter_up_weight):
    storage_slots = jnp.take(adapter_storage_slot, adapters_in_use, axis=0).astype(jnp.int32)
    in_use_down = jnp.take(adapter_down_weight, storage_slots, axis=0)
    in_use_up = jnp.take(adapter_up_weight, storage_slots, axis=0)
    down_matrix = in_use_down.reshape(ACTIVE * 2 * ADAPTER_RANK, MODEL_WIDTH)
    blocks = tokens.reshape(N_REQ, PROMPT_TOKENS, MODEL_WIDTH)

    def one_block(block):
        rows, segment, request_adapters = block
        floats = rows.astype(jnp.float32)
        normed = (floats * lax.rsqrt(lax.optimization_barrier(jnp.mean(floats * floats, axis=-1, keepdims=True)) + norm_eps) * input_norm_gain.astype(jnp.float32)).astype(jnp.bfloat16)
        query_plain = jnp.dot(normed, query_weight, preferred_element_type=jnp.float32)
        key_base = jnp.dot(normed, key_weight, preferred_element_type=jnp.float32)
        value_plain = jnp.dot(normed, value_weight, preferred_element_type=jnp.float32)
        member = segment[:, None] == jnp.arange(REQ_DEV, dtype=jnp.int32)[None, :]
        token_adapter = lax.optimization_barrier(jnp.sum(jnp.where(member, request_adapters[None, :], jnp.zeros_like(request_adapters)[None, :]), axis=1))
        select = token_adapter[:, None] == jnp.arange(ACTIVE, dtype=jnp.int32)[None, :]
        shrunk_all = lax.dot_general(normed, down_matrix, (((1,), (1,)), ((), ())), preferred_element_type=jnp.float32).reshape(PROMPT_TOKENS, ACTIVE, 2, ADAPTER_RANK)
        shrunk = lax.optimization_barrier(jnp.sum(jnp.where(select[:, :, None, None], shrunk_all, jnp.float32(0.0)), axis=1)).astype(jnp.bfloat16)
        spread = jnp.where(select[:, :, None, None], shrunk[:, None, :, :], jnp.zeros((), jnp.bfloat16))
        query_change = jnp.dot(spread[:, :, 0, :].reshape(PROMPT_TOKENS, ACTIVE * ADAPTER_RANK), in_use_up[:, 0].reshape(ACTIVE * ADAPTER_RANK, MODEL_WIDTH), preferred_element_type=jnp.float32)
        value_change = jnp.dot(spread[:, :, 1, :].reshape(PROMPT_TOKENS, ACTIVE * ADAPTER_RANK), in_use_up[:, 1].reshape(ACTIVE * ADAPTER_RANK, MODEL_WIDTH), preferred_element_type=jnp.float32)
        token_positions = positions_of(segment)
        query_per_head = apply_rotation((query_plain + adapter_scale * query_change).reshape(PROMPT_TOKENS, ATTENTION_HEADS, HEAD_WIDTH), token_positions).astype(jnp.bfloat16)
        key_heads = apply_rotation(key_base.reshape(PROMPT_TOKENS, ATTENTION_HEADS, HEAD_WIDTH), token_positions).astype(jnp.bfloat16)
        value_per_head = (value_plain + adapter_scale * value_change).astype(jnp.bfloat16).reshape(PROMPT_TOKENS, ATTENTION_HEADS, HEAD_WIDTH)
        attended = attend(query_per_head, key_heads, value_per_head, segment).reshape(PROMPT_TOKENS, MODEL_WIDTH)
        return (floats + jnp.dot(attended, output_weight, preferred_element_type=jnp.float32)).astype(jnp.bfloat16)
    outputs = lax.map(one_block, (blocks, token_request_number, request_adapter_position))
    return outputs.reshape(N_REQ * PROMPT_TOKENS, MODEL_WIDTH)
```

```python
import functools

import jax
import jax.numpy as jnp
import numpy as np
from jax import lax
from jax.experimental import pallas as pl
from jax.experimental.pallas import tpu as pltpu
from jax.sharding import PartitionSpec as P

HEAD_WIDTH = 64


norm_eps = 1e-05
rope_base = 130000.0
adapter_scale = 2.0

MESH = pl.DeviceIdType.MESH
DOWN, QUERY, KEY, VALUE, UP, OUTPUT = range(6)
SPAN = 128
PLACES = 16
RANK = 16
REACH = 256
FAR = 3.0e38
NEVER = -1.0e30
NT = (((1,), (1,)), ((), ()))
TN = (((0,), (0,)), ((), ()))


def rotation_tables():
    half = HEAD_WIDTH // 2
    lane = np.arange(128)
    frequency = np.float32(rope_base) ** (-(np.arange(half, dtype=np.float32) * 2.0 / HEAD_WIDTH))
    angles = np.arange(REACH, dtype=np.float32)[:, None] * frequency.astype(np.float32)[None, lane % half]
    angles = angles.astype(np.float64)
    sign = np.where(lane % HEAD_WIDTH < half, -1.0, 1.0)
    table = np.concatenate([np.cos(angles), np.sin(angles) * sign], axis=1).astype(np.float32)
    high = table.astype(jnp.bfloat16)
    low = (table - high.astype(np.float32)).astype(jnp.bfloat16)
    return np.stack([high, low])


def layer_kernel(
    tokens, segment_in, request_position, in_use, slots, gain, table,
    down, query_weight, key_weight, value_weight, up, output_weight,
    out,
    tok, normed, info, limit, rotation,
    down_all, query_all, key_all, value_all, up_all, output_all,
    shrunk_all, query_heads, key_heads, value_heads, attended,
    sent_core, got_core, sent_second, got_second, kept_second, sent_third, got_third, kept_third,
    token_sems, send_sems, recv_sems, local_sems,
    spread_send, spread_recv, info_sems, shrunk_send, shrunk_recv, reduce_send, reduce_recv,
):
    me = lax.axis_index("req")
    part = lax.axis_index("tp")
    z, y = me // 2, me % 2
    x, core = part // 2, part % 2
    mine = z % 2
    other = 1 - mine
    z_mate = 2 * (z + 1 - 2 * mine) + y
    y_mate = 2 * z + 1 - y
    core_mate = 2 * x + 1 - core
    x_mate = 2 * (1 - x) + core
    sources = (down, query_weight, key_weight, value_weight, up, output_weight)
    gathered = (down_all, query_all, key_all, value_all, up_all, output_all)

    def piece(index, half):
        if index == DOWN:
            rows = pl.ds(pl.multiple_of(part * 16, 16), 16)
            return down.at[rows, pl.ds(pl.multiple_of(half * 1024, 1024), 1024)]
        if index == OUTPUT:
            return output_weight.at[pl.ds(pl.multiple_of(half * 256, 256), 256), :]
        return sources[index].at[:, pl.ds(pl.multiple_of(half * 256, 256), 256)]

    def remote(source, target, send, recv, req=None, tp=None):
        return pltpu.make_async_remote_copy(
            src_ref=source,
            dst_ref=target,
            send_sem=send,
            recv_sem=recv,
            device_id={
                "req": me if req is None else req,
                "tp": part if tp is None else tp,
            },
            device_id_type=MESH,
        )

    def along(index, hop):
        there = lax.rem(z + hop, 4)
        return remote(
            piece(index, there % 2),
            gathered[index].at[me],
            send_sems.at[index, hop],
            recv_sems.at[index, me],
            req=2 * there + y,
        )

    def across(index):
        return remote(
            piece(index, mine),
            gathered[index].at[me],
            send_sems.at[index, 0],
            recv_sems.at[index, me],
            req=y_mate,
        )

    def onward(index, hop):
        origin = 2 * lax.rem(z + hop, 4) + y
        block = gathered[index].at[origin]
        return remote(
            block, block, send_sems.at[index, 3 + hop], recv_sems.at[index, origin], req=y_mate
        )

    def keep(index):
        return pltpu.make_async_copy(
            piece(index, mine), gathered[index].at[me], local_sems.at[index]
        )

    def arrived(index, origin):
        block = gathered[index].at[origin]
        remote(
            block, block, send_sems.at[index, 0], recv_sems.at[index, origin], req=y_mate
        ).wait_recv()

    def begin(index):
        for hop in (1, 3, 2):
            along(index, hop).start()
        across(index).start()
        keep(index).start()

    def pump(index):
        for hop in (1, 3, 2):
            arrived(index, 2 * lax.rem(z + hop, 4) + y)
            onward(index, hop).start()

    def complete(index):
        for hop in (0, 1, 3, 2):
            arrived(index, 2 * lax.rem(z + hop, 4) + 1 - y)
        keep(index).wait()

    def load_tokens(quarter):
        rows = pl.ds(pl.multiple_of(quarter * SPAN, SPAN), SPAN)
        return pltpu.make_async_copy(tokens.at[rows, :], tok.at[rows, :], token_sems.at[quarter])

    def quarters(which, quarter):
        return normed.at[which, pl.ds(pl.multiple_of(quarter * SPAN, SPAN), SPAN), :]

    def share_tokens():
        block = quarters(mine, part)
        return remote(block, block, spread_send.at[0], spread_recv.at[part], req=z_mate)

    def spread_tokens(hop):
        block = quarters(other, part)
        return remote(
            block, block, spread_send.at[hop], spread_recv.at[part], tp=lax.rem(part + hop, 4)
        )

    def tokens_arrived(quarter):
        block = quarters(other, quarter)
        remote(block, block, spread_send.at[0], spread_recv.at[quarter], req=z_mate).wait_recv()

    def share_info():
        block = info.at[mine]
        return remote(block, block, info_sems.at[0], info_sems.at[1], req=z_mate)

    def share_shrunk(to_mate, hop):
        slot = 4 * to_mate + hop
        block = shrunk_all.at[2 * part + mine]
        return remote(
            block,
            block,
            shrunk_send.at[slot],
            shrunk_recv.at[2 * part + mine],
            req=z_mate if to_mate else me,
            tp=lax.rem(part + hop, 4),
        )

    shrunk_hops = [(0, 1), (0, 2), (0, 3), (1, 0), (1, 1), (1, 2), (1, 3)]

    for step in range(4):
        load_tokens(lax.rem(part + step, 4)).start()

    barrier = pltpu.get_barrier_semaphore()

    def greet(req, tp):
        pl.semaphore_signal(
            barrier, inc=1, device_id={"req": req, "tp": tp}, device_id_type=MESH
        )

    for hop in (1, 2, 3):
        greet(2 * lax.rem(z + hop, 4) + y, part)
    greet(y_mate, part)
    for hop in (1, 2, 3):
        greet(me, lax.rem(part + hop, 4))
        greet(z_mate, lax.rem(part + hop, 4))
    pl.semaphore_wait(barrier, 10)

    begin(DOWN)
    begin(QUERY)

    gains = gain[...].astype(jnp.float32)

    def normalise(quarter):
        load_tokens(quarter).wait()

        def some(step, carry):
            rows = pl.ds(pl.multiple_of(quarter * SPAN + step * 32, 32), 32)
            floats = tok[rows, :].astype(jnp.float32)
            mean = jnp.mean(floats * floats, axis=-1, keepdims=True)
            normed[mine, rows, :] = (floats * lax.rsqrt(mean + norm_eps) * gains).astype(
                jnp.bfloat16
            )
            return carry

        lax.fori_loop(0, SPAN // 32, some, 0)

    normalise(part)
    share_tokens().start()

    segment = segment_in[...].astype(jnp.float32)
    ordinal = lax.broadcasted_iota(jnp.int32, segment.shape, 1).astype(jnp.float32)
    place = jnp.zeros_like(segment)
    start = jnp.zeros_like(segment)
    for request in range(request_position.shape[1]):
        slot = slots[in_use[request_position[0, request]]]
        here = segment == float(request)
        place = jnp.where(here, slot.astype(jnp.float32), place)
        before = jnp.sum(jnp.where(segment < float(request), 1.0, 0.0), axis=1, keepdims=True)
        start = jnp.where(here, before, start)
    info[mine] = jnp.concatenate(
        [segment, place, ordinal - start, jnp.zeros((5, segment.shape[1]), jnp.float32)], axis=0
    )
    share_info().start()
    begin(KEY)
    begin(UP)
    begin(VALUE)
    begin(OUTPUT)

    for step in range(1, 4):
        normalise(lax.rem(part + step, 4))

    pump(DOWN)

    share_info().wait_recv()

    def prepare(which, carry):
        facts = info[which]
        columns = facts.T
        for block in range(4):
            first = max(0, block - 2) * SPAN
            width = min(block + 1, 3) * SPAN
            query_segment = columns[block * SPAN : (block + 1) * SPAN, 0:1]
            key_segment = facts[0:1, first : first + width]
            query_order = block * SPAN + lax.broadcasted_iota(jnp.int32, (SPAN, width), 0)
            key_order = first + lax.broadcasted_iota(jnp.int32, (SPAN, width), 1)
            allowed = (query_segment == key_segment) & (key_order <= query_order)
            limit[which, pl.ds(block * SPAN, SPAN), pl.ds(0, width)] = jnp.where(
                allowed, FAR, NEVER
            )
        lane = lax.broadcasted_iota(jnp.int32, (4 * SPAN, REACH), 1).astype(jnp.float32)
        chosen = jnp.where(columns[:, 2:3] == lane, 1.0, 0.0).astype(jnp.bfloat16)
        rotation[which] = jnp.dot(
            chosen, table[0], preferred_element_type=jnp.float32
        ) + jnp.dot(chosen, table[1], preferred_element_type=jnp.float32)
        return carry

    lax.fori_loop(0, 2, prepare, 0)

    tokens_arrived(part)
    for hop in (1, 2, 3):
        spread_tokens(hop).start()
    pump(QUERY)
    complete(DOWN)
    for hop in (1, 2, 3):
        tokens_arrived(lax.rem(part + hop, 4))

    def shrink(which, carry):
        columns = pl.ds(pl.multiple_of(mine * 1024, 1024), 1024)
        product = lax.dot_general(
            down_all[...].reshape(8 * RANK, 1024),
            normed[which, :, columns],
            NT,
            preferred_element_type=jnp.float32,
        )
        places = info[which][1:2, :]
        total = jnp.zeros((RANK, product.shape[1]), jnp.float32)
        for origin in range(8):
            wanted = (2 * origin + x).astype(jnp.float32)
            total = total + jnp.where(
                places == wanted, product[origin * RANK : (origin + 1) * RANK], 0.0
            )
        at = pl.ds(pl.multiple_of(which * 512, 512), 512)
        shrunk_all[2 * part + mine, :, at] = total.astype(jnp.bfloat16)
        return carry

    lax.fori_loop(0, 2, shrink, 0)
    for to_mate, hop in shrunk_hops:
        share_shrunk(to_mate, hop).start()

    def projected(which, index):
        return jnp.dot(
            normed[which],
            gathered[index][...].reshape(8 * 256, 256),
            preferred_element_type=jnp.float32,
        )

    def shrunk_of(which, kind):
        at = pl.ds(pl.multiple_of(which * 512, 512), 512)
        total = jnp.zeros((RANK, 512), jnp.float32)
        for slot in range(2):
            for half in range(2):
                total = total + shrunk_all[2 * (2 * slot + kind) + half, :, at].astype(jnp.float32)
        return total

    def change(which, kind):
        columns = info[which].T
        compact = shrunk_of(which, kind)
        padded = jnp.concatenate(
            [compact, jnp.zeros((128 - RANK, compact.shape[1]), jnp.float32)], axis=0
        ).T
        lane = lax.broadcasted_iota(jnp.int32, (128, PLACES * RANK), 1)
        row = lax.broadcasted_iota(jnp.int32, (128, PLACES * RANK), 0)
        tile = jnp.where(lane % RANK == row, 1.0, 0.0).astype(jnp.bfloat16)
        tiled = jnp.dot(
            padded.astype(jnp.bfloat16), tile, preferred_element_type=jnp.float32
        )
        lanes = lax.broadcasted_iota(jnp.int32, tiled.shape, 1) // RANK
        laid = jnp.where(columns[:, 1:2] == lanes.astype(jnp.float32), tiled, 0.0)
        ups = up_all[...].reshape(8, 2, 2, RANK, 256)[:, :, kind].reshape(PLACES * RANK, 256)
        return adapter_scale * jnp.dot(
            laid.astype(jnp.bfloat16), ups, preferred_element_type=jnp.float32
        )

    def rotated(which, values):
        half = HEAD_WIDTH // 2
        cosine = rotation[which, :, 0:128]
        sine = rotation[which, :, 128:256]
        low = lax.broadcasted_iota(jnp.int32, (512, 128), 1) % HEAD_WIDTH < half
        parts = []
        for pair in range(2):
            value = values[:, pair * 128 : (pair + 1) * 128]
            swapped = jnp.where(
                low, pltpu.roll(value, 128 - half, 1), pltpu.roll(value, half, 1)
            )
            parts.append(value * cosine + swapped * sine)
        return jnp.concatenate(parts, axis=1)

    pump(UP)
    complete(QUERY)
    pump(KEY)
    complete(UP)
    for to_mate, hop in shrunk_hops:
        origin_part = lax.rem(part + hop, 4)
        at = shrunk_all.at[2 * origin_part + (other if to_mate else mine)]
        remote(
            at, at, shrunk_send.at[0],
            shrunk_recv.at[2 * origin_part + (other if to_mate else mine)], req=z_mate,
        ).wait_recv()

    def make_query(which, carry):
        query = projected(which, QUERY) + change(which, 0)
        query_heads[which] = (rotated(which, query) * 0.125).astype(jnp.bfloat16)
        return carry

    lax.fori_loop(0, 2, make_query, 0)
    complete(KEY)
    pump(VALUE)

    def make_key(which, carry):
        key_heads[which] = rotated(which, projected(which, KEY)).astype(jnp.bfloat16)
        return carry

    lax.fori_loop(0, 2, make_key, 0)
    complete(VALUE)

    def make_value(which, carry):
        value_heads[which] = (projected(which, VALUE) + change(which, 1)).astype(jnp.bfloat16)
        return carry

    lax.fori_loop(0, 2, make_value, 0)

    def attend(which):
        def one(pair, carry):
            lanes = pl.ds(pl.multiple_of(pair * 128, 128), 128)
            left = lax.broadcasted_iota(jnp.int32, (SPAN, 128), 1) < HEAD_WIDTH
            for block in range(4):
                first = max(0, block - 2) * SPAN
                width = min(block + 1, 3) * SPAN
                rows = pl.ds(block * SPAN, SPAN)
                query = query_heads[which, rows, lanes]
                keys = key_heads[which, pl.ds(first, width), lanes]
                values = value_heads[which, pl.ds(first, width), lanes]
                results = []
                for head in range(2):
                    own = left if head == 0 else jnp.logical_not(left)
                    masked = jnp.where(own, query, jnp.zeros_like(query))
                    scores = lax.dot_general(
                        masked, keys, NT, preferred_element_type=jnp.float32
                    )
                    scores = jnp.minimum(scores, limit[which, rows, pl.ds(0, width)])
                    peak = jnp.max(scores, axis=-1, keepdims=True)
                    exponent = jnp.exp(scores - peak)
                    total = jnp.sum(exponent, axis=-1, keepdims=True)
                    weighed = jnp.dot(
                        exponent.astype(jnp.bfloat16), values, preferred_element_type=jnp.float32
                    )
                    results.append(weighed / total)
                attended[which, rows, lanes] = jnp.where(left, results[0], results[1]).astype(
                    jnp.bfloat16
                )
            return carry

        lax.fori_loop(0, 2, one, 0)

    attend(other)
    for hop in (1, 3):
        arrived(OUTPUT, 2 * lax.rem(z + hop, 4) + y)
        onward(OUTPUT, hop).start()
    attend(mine)
    arrived(OUTPUT, 2 * lax.rem(z + 2, 4) + y)
    onward(OUTPUT, 2).start()
    keep(OUTPUT).wait()

    chunks = sent_core.shape[1]
    rows_of = sent_core.shape[3]

    def product(target, side, which, chunk):
        return jnp.dot(
            attended[which, pl.ds(pl.multiple_of(chunk * rows_of, rows_of), rows_of), :],
            output_all[2 * target + side],
            preferred_element_type=jnp.float32,
        )

    def core_copy(phase, chunk):
        return remote(
            sent_core.at[phase, chunk], got_core.at[phase, chunk],
            reduce_send.at[0, phase, chunk], reduce_recv.at[0, phase, chunk], tp=core_mate,
        )

    def second_copy(phase, chunk):
        to = {"tp": x_mate} if phase == 0 else {"req": z_mate}
        return remote(
            sent_second.at[phase, chunk], got_second.at[phase, chunk],
            reduce_send.at[1, phase, chunk], reduce_recv.at[1, phase, chunk], **to,
        )

    def third_copy(phase, chunk):
        to = {"req": z_mate} if phase == 0 else {"tp": x_mate}
        return remote(
            sent_third.at[phase, chunk], got_third.at[phase, chunk],
            reduce_send.at[2, phase, chunk], reduce_recv.at[2, phase, chunk], **to,
        )

    def side_of(phase):
        return y if phase == 0 else 1 - y

    for phase in range(2):
        if phase == 1:
            for hop in (0, 1, 3, 2):
                arrived(OUTPUT, 2 * lax.rem(z + hop, 4) + 1 - y)
        side = side_of(phase)

        def first(chunk, carry):
            for column in range(2):
                for which in range(2):
                    sent_core[phase, chunk, 2 * column + which] = product(
                        2 * column + 1 - core, side, which, chunk
                    ).astype(jnp.bfloat16)
            core_copy(phase, chunk).start()
            return carry

        lax.fori_loop(0, chunks, first, 0)

    for phase in range(2):
        side = side_of(phase)

        def second(chunk, carry):
            core_copy(phase, chunk).wait_recv()
            for step in range(2):
                column, which = (1 - x, step) if phase == 0 else (step, other)
                sent_second[phase, chunk, step] = (
                    product(2 * column + core, side, which, chunk)
                    + got_core[phase, chunk, 2 * column + which].astype(jnp.float32)
                ).astype(jnp.bfloat16)
            second_copy(phase, chunk).start()
            for step in range(2):
                column, which = (x, step) if phase == 0 else (step, mine)
                kept_second[phase, chunk, step] = product(
                    2 * column + core, side, which, chunk
                ) + got_core[phase, chunk, 2 * column + which].astype(jnp.float32)
            return carry

        lax.fori_loop(0, chunks, second, 0)

    for phase in range(2):

        def third(chunk, carry):
            second_copy(phase, chunk).wait_recv()
            sent, held = (other, mine) if phase == 0 else (1 - x, x)
            sent_third[phase, chunk] = (
                kept_second[phase, chunk, sent]
                + got_second[phase, chunk, sent].astype(jnp.float32)
            ).astype(jnp.bfloat16)
            third_copy(phase, chunk).start()
            kept_third[phase, chunk] = kept_second[phase, chunk, held] + got_second[
                phase, chunk, held
            ].astype(jnp.float32)
            return carry

        lax.fori_loop(0, chunks, third, 0)

    for phase in range(2):
        side = side_of(phase)

        def last(chunk, carry):
            third_copy(phase, chunk).wait_recv()
            rows = pl.ds(pl.multiple_of(chunk * rows_of, rows_of), rows_of)
            residual = tok[rows, pl.ds(pl.multiple_of(part * 512 + side * 256, 256), 256)]
            out[rows, pl.ds(pl.multiple_of(side * 256, 256), 256)] = (
                kept_third[phase, chunk]
                + got_third[phase, chunk].astype(jnp.float32)
                + residual.astype(jnp.float32)
            ).astype(jnp.bfloat16)
            return carry

        lax.fori_loop(0, chunks, last, 0)

    for index in range(6):
        for hop in (1, 2, 3):
            along(index, hop).wait_send()
            onward(index, hop).wait_send()
        across(index).wait_send()
    share_tokens().wait_send()
    for hop in (1, 2, 3):
        spread_tokens(hop).wait_send()
    share_info().wait_send()
    for to_mate, hop in shrunk_hops:
        share_shrunk(to_mate, hop).wait_send()
    for phase in range(2):
        for chunk in range(chunks):
            core_copy(phase, chunk).wait_send()
            second_copy(phase, chunk).wait_send()
            third_copy(phase, chunk).wait_send()


def fused_layer(
    tokens, segment, request_position, in_use, slots, gain,
    query_weight, key_weight, value_weight, output_weight, down, up,
):
    bf16, f32 = jnp.bfloat16, jnp.float32
    rows, width = tokens.shape
    chunks = 4
    piece = rows // chunks
    hbm = pl.BlockSpec(memory_space=pltpu.HBM)
    vmem = pl.BlockSpec(memory_space=pltpu.VMEM)
    smem = pl.BlockSpec(memory_space=pltpu.SMEM)
    dma = pltpu.SemaphoreType.DMA
    return pl.pallas_call(
        layer_kernel,
        out_shape=jax.ShapeDtypeStruct((rows, 512), bf16),
        in_specs=[hbm, vmem, smem, smem, smem, vmem, vmem] + [hbm] * 6,
        out_specs=vmem,
        scratch_shapes=[
            pltpu.VMEM((rows, width), bf16),
            pltpu.VMEM((2, rows, width), bf16),
            pltpu.VMEM((2, 8, rows), f32),
            pltpu.VMEM((2, rows, 3 * SPAN), f32),
            pltpu.VMEM((2, rows, 256), f32),
            pltpu.VMEM((8, RANK, 1024), bf16),
            pltpu.VMEM((8, 256, 256), bf16),
            pltpu.VMEM((8, 256, 256), bf16),
            pltpu.VMEM((8, 256, 256), bf16),
            pltpu.VMEM((8, 64, 256), bf16),
            pltpu.VMEM((8, 256, 256), bf16),
            pltpu.VMEM((8, RANK, 2 * rows), bf16),
            pltpu.VMEM((2, rows, 256), bf16),
            pltpu.VMEM((2, rows, 256), bf16),
            pltpu.VMEM((2, rows, 256), bf16),
            pltpu.VMEM((2, rows, 256), bf16),
            pltpu.VMEM((2, chunks, 4, piece, 256), bf16),
            pltpu.VMEM((2, chunks, 4, piece, 256), bf16),
            pltpu.VMEM((2, chunks, 2, piece, 256), bf16),
            pltpu.VMEM((2, chunks, 2, piece, 256), bf16),
            pltpu.VMEM((2, chunks, 2, piece, 256), f32),
            pltpu.VMEM((2, chunks, piece, 256), bf16),
            pltpu.VMEM((2, chunks, piece, 256), bf16),
            pltpu.VMEM((2, chunks, piece, 256), f32),
            dma((4,)),
            dma((6, 7)),
            dma((6, 8)),
            dma((6,)),
            dma((4,)),
            dma((4,)),
            dma((2,)),
            dma((8,)),
            dma((8,)),
            dma((3, 2, chunks)),
            dma((3, 2, chunks)),
        ],
        compiler_params=pltpu.CompilerParams(
            collective_id=0, has_side_effects=True, vmem_limit_bytes=56 * 1024 * 1024
        ),
    )(
        tokens, segment, request_position, in_use, slots, gain[None, :],
        jnp.asarray(rotation_tables()),
        down.reshape(-1, width), query_weight, key_weight, value_weight,
        up.reshape(-1, up.shape[3]), output_weight,
    )


def active_rows(stored, active_slots):
    slot_total = stored.shape[0]
    held = lax.axis_index("req") * slot_total + jnp.arange(slot_total, dtype=jnp.int32)
    chosen = (active_slots[:, None] == held[None, :]).astype(stored.dtype)
    rows = jnp.einsum(
        "as,srd->ard", chosen, stored, preferred_element_type=jnp.float32
    ).astype(stored.dtype)
    return lax.psum(rows, "req").reshape(-1, stored.shape[2])


def positions_of(segment):
    ordinal = jnp.arange(segment.shape[0], dtype=jnp.int32)
    before = segment[None, :] < segment[:, None]
    return ordinal - jnp.sum(before.astype(jnp.int32), axis=1)


def apply_rotation(values, token_positions):
    half_dim = HEAD_WIDTH // 2
    frequency = rope_base ** (-(jnp.arange(half_dim, dtype=jnp.float32) * 2.0 / HEAD_WIDTH))
    angles = token_positions.astype(jnp.float32)[:, None] * frequency[None, :]
    cosine = jnp.cos(angles)[:, None, :]
    sine_part = jnp.sin(angles)[:, None, :]
    first_half = values[..., :half_dim]
    second_half = values[..., half_dim:]
    return jnp.concatenate(
        [
            first_half * cosine - second_half * sine_part,
            second_half * cosine + first_half * sine_part,
        ],
        axis=-1,
    )


def attend(query_per_head, key_heads, value_per_head, segment):
    scores = (
        jnp.einsum("qhd,khd->hqk", query_per_head, key_heads, preferred_element_type=jnp.float32)
        * 0.125
    )
    ordinal = jnp.arange(segment.shape[0], dtype=jnp.int32)
    allowed = (segment[:, None] == segment[None, :]) & (ordinal[None, :] <= ordinal[:, None])
    scores = jnp.where(allowed[None], scores, jnp.float32(-1e30))
    row_peak = jnp.max(scores, axis=-1, keepdims=True)
    exponent = jnp.where(allowed[None], jnp.exp(scores - row_peak), jnp.float32(0.0))
    weights = (exponent / jnp.sum(exponent, axis=-1, keepdims=True)).astype(jnp.bfloat16)
    return jnp.einsum(
        "hqk,khd->qhd", weights, value_per_head, preferred_element_type=jnp.float32
    ).astype(jnp.bfloat16)


def local(
    tokens,
    token_request_number,
    request_adapter_position,
    adapters_in_use,
    adapter_storage_slot,
    input_norm_gain,
    query_weight,
    key_weight,
    value_weight,
    output_weight,
    adapter_down_weight,
    adapter_up_weight,
):
    if (
        lax.axis_size("req") == 8
        and lax.axis_size("tp") == 4
        and tokens.shape == (512, 2048)
        and adapter_down_weight.shape == (2, 2, 16, 2048)
    ):
        return fused_layer(
            tokens,
            token_request_number,
            request_adapter_position,
            adapters_in_use,
            adapter_storage_slot,
            input_norm_gain,
            query_weight,
            key_weight,
            value_weight,
            output_weight,
            adapter_down_weight,
            adapter_up_weight,
        )
    row_total, model_width = tokens.shape
    local_width = query_weight.shape[1]
    reduced_rows = adapter_down_weight.shape[2]
    slot_total = adapter_down_weight.shape[0]
    segment = token_request_number[0]
    request_adapters = request_adapter_position[0]
    tp_total = lax.axis_size("tp")
    req_total = lax.axis_size("req")
    part_rows = reduced_rows // tp_total
    share = 2 * part_rows
    down_part = lax.dynamic_slice_in_dim(
        adapter_down_weight, lax.axis_index("tp") * part_rows, part_rows, 2
    ).reshape(slot_total, share, model_width)
    up_part = adapter_up_weight.reshape(slot_total, 2 * reduced_rows, local_width)
    active_slots = jnp.take(adapter_storage_slot, adapters_in_use, axis=0)
    place_total = active_slots.shape[0]
    request_places = request_adapters
    member = segment[:, None] == jnp.arange(request_adapters.shape[0], dtype=jnp.int32)[None, :]
    token_place = jnp.sum(
        jnp.where(member, request_places[None, :], jnp.zeros_like(request_places)[None, :]),
        axis=1,
    )
    column = jnp.arange(place_total * share, dtype=jnp.int32)
    mask = (token_place[:, None] == (column // share)[None, :]).astype(jnp.bfloat16)
    lanes = max(128, tp_total * share)
    fold = (lax.axis_index("tp") * share + column % share)[:, None] == jnp.arange(
        lanes, dtype=jnp.int32
    )[None, :]
    fold = fold.astype(jnp.bfloat16)
    floats = tokens.astype(jnp.float32)
    normed = (
        floats
        * lax.rsqrt(jnp.mean(floats * floats, axis=-1, keepdims=True) + norm_eps)
        * input_norm_gain.astype(jnp.float32)
    ).astype(jnp.bfloat16)
    down_all = active_rows(down_part, active_slots)
    up_all = active_rows(up_part, active_slots)
    output_full = lax.all_gather(output_weight, "req", axis=1, tiled=True)
    query_plain, key_base, value_plain = [
        jnp.dot(
            normed,
            lax.all_gather(weight, "req", axis=0, tiled=True),
            preferred_element_type=jnp.float32,
        )
        for weight in (query_weight, key_weight, value_weight)
    ]
    shrunk_all = lax.dot_general(
        normed, down_all, (((1,), (1,)), ((), ())), preferred_element_type=jnp.float32
    ).astype(jnp.bfloat16)
    shrunk = lax.psum(
        jnp.dot(shrunk_all * mask, fold, preferred_element_type=jnp.float32), "tp"
    ).astype(jnp.bfloat16)
    shrunk = shrunk[:, : tp_total * share]
    source = jnp.arange(tp_total * share, dtype=jnp.int32)
    source_kind = (source % share) // part_rows
    source_rank = (source // share) * part_rows + source % part_rows
    target = jnp.arange(place_total * reduced_rows, dtype=jnp.int32)
    mine = token_place[:, None] == (target // reduced_rows)[None, :]
    up_all = up_all.reshape(place_total, 2, reduced_rows, local_width)

    def change_of(kind):
        spread_map = (source_kind == kind)[:, None] & (
            source_rank[:, None] == (target % reduced_rows)[None, :]
        )
        spread = jnp.dot(
            shrunk, spread_map.astype(jnp.bfloat16), preferred_element_type=jnp.float32
        ).astype(jnp.bfloat16)
        spread = jnp.where(mine, spread, jnp.zeros((), jnp.bfloat16))
        return jnp.dot(
            spread,
            up_all[:, kind].reshape(place_total * reduced_rows, local_width),
            preferred_element_type=jnp.float32,
        )

    query_change = change_of(0)
    value_change = change_of(1)
    head_total = local_width // HEAD_WIDTH
    token_positions = positions_of(segment)
    query_per_head = apply_rotation(
        (query_plain + adapter_scale * query_change).reshape(row_total, head_total, HEAD_WIDTH),
        token_positions,
    ).astype(jnp.bfloat16)
    key_heads = apply_rotation(
        key_base.reshape(row_total, head_total, HEAD_WIDTH), token_positions
    ).astype(jnp.bfloat16)
    value_per_head = (
        (value_plain + adapter_scale * value_change)
        .astype(jnp.bfloat16)
        .reshape(row_total, head_total, HEAD_WIDTH)
    )
    attended = attend(query_per_head, key_heads, value_per_head, segment).reshape(
        row_total, local_width
    )
    share_width = model_width // tp_total
    residual_part = lax.dynamic_slice_in_dim(
        tokens, lax.axis_index("tp") * share_width, share_width, 1
    )
    partial_out = jnp.dot(attended, output_full, preferred_element_type=jnp.float32)
    summed = lax.psum_scatter(
        partial_out.astype(jnp.bfloat16), "tp", scatter_dimension=1, tiled=True
    ).astype(jnp.float32)
    return (summed + residual_part.astype(jnp.float32)).astype(jnp.bfloat16)


def solution(mesh):
    in_specs = (
        P("req", None),
        P("req", None),
        P("req", None),
        P(),
        P(),
        P(),
        P("req", "tp"),
        P("req", "tp"),
        P("req", "tp"),
        P("tp", "req"),
        P("req", None, None, None),
        P("req", None, None, "tp"),
    )
    out_specs = P("req", "tp")
    return jax.shard_map(local, mesh=mesh, in_specs=in_specs, out_specs=out_specs, check_vma=False)
```

```python
import functools

import jax
import jax.numpy as jnp
import numpy as np
from jax import lax
from jax.experimental import pallas as pl
from jax.experimental.pallas import tpu as pltpu
from jax.sharding import PartitionSpec as P

HEAD_WIDTH = 64


norm_eps = 1e-05
rope_base = 130000.0
adapter_scale = 2.0

MESH = pl.DeviceIdType.MESH
DOWN, QUERY_0, KEY_0, UP, VALUE_0, QUERY_1, KEY_1, VALUE_1, OUTPUT_0, OUTPUT_1 = range(10)
PIECES = 10
AHEAD = 2
SPAN = 128
PLACES = 16
RANK = 16
REACH = 256
FAR = 3.0e38
NEVER = -1.0e30
NT = (((1,), (1,)), ((), ()))
TN = (((0,), (0,)), ((), ()))


def rotation_tables():
    half = HEAD_WIDTH // 2
    lane = np.arange(128)
    frequency = np.float32(rope_base) ** (-(np.arange(half, dtype=np.float32) * 2.0 / HEAD_WIDTH))
    angles = np.arange(REACH, dtype=np.float32)[:, None] * frequency.astype(np.float32)[None, lane % half]
    angles = angles.astype(np.float64)
    sign = np.where(lane % HEAD_WIDTH < half, -1.0, 1.0)
    table = np.concatenate([np.cos(angles), np.sin(angles) * sign], axis=1).astype(np.float32)
    high = table.astype(jnp.bfloat16)
    low = (table - high.astype(np.float32)).astype(jnp.bfloat16)
    return np.stack([high, low])


def layer_kernel(
    tokens, segment_in, request_position, in_use, slots, gain, table,
    down, query_weight, key_weight, value_weight, up, output_weight,
    out,
    tok, normed, info, limit, rotation,
    down_all, weight_all, up_all, output_all,
    shrunk_all, laid, query_heads, key_heads, value_heads, attended,
    sent_core, got_core, sent_second, got_second, kept_second, sent_third, got_third, kept_third,
    token_sems, send_sems, recv_sems, local_sems,
    spread_send, spread_recv, info_sems, shrunk_send, shrunk_recv, reduce_send, reduce_recv,
):
    me = lax.axis_index("req")
    part = lax.axis_index("tp")
    z, y = me // 2, me % 2
    x, core = part // 2, part % 2
    mine = z % 2
    other = 1 - mine
    z_mate = 2 * (z + 1 - 2 * mine) + y
    y_mate = 2 * z + 1 - y
    core_mate = 2 * x + 1 - core
    x_mate = 2 * (1 - x) + core
    weights = {
        QUERY_0: (query_weight, 0), KEY_0: (key_weight, 0), VALUE_0: (value_weight, 0),
        QUERY_1: (query_weight, 1), KEY_1: (key_weight, 1), VALUE_1: (value_weight, 1),
    }
    weight_slot = {name: slot for slot, name in enumerate(weights)}

    def piece(index, half):
        if index == DOWN:
            rows = pl.ds(pl.multiple_of(part * 16, 16), 16)
            return down.at[rows, pl.ds(pl.multiple_of(half * 1024, 1024), 1024)]
        if index == UP:
            return up.at[:, pl.ds(pl.multiple_of(half * 256, 256), 256)]
        if index in weights:
            weight, pair = weights[index]
            return weight.at[:, pl.ds(pl.multiple_of(half * 256 + pair * 128, 128), 128)]
        first = half * 256 + (index - OUTPUT_0) * 128
        return output_weight.at[pl.ds(pl.multiple_of(first, 128), 128), :]

    def block(index, origin):
        if index == DOWN:
            return down_all.at[origin]
        if index == UP:
            return up_all.at[origin]
        if index in weights:
            return weight_all.at[weight_slot[index], origin]
        return output_all.at[origin, pl.ds((index - OUTPUT_0) * 128, 128), :]

    def remote(source, target, send, recv, req=None, tp=None):
        return pltpu.make_async_remote_copy(
            src_ref=source,
            dst_ref=target,
            send_sem=send,
            recv_sem=recv,
            device_id={
                "req": me if req is None else req,
                "tp": part if tp is None else tp,
            },
            device_id_type=MESH,
        )

    def along(index, hop):
        there = lax.rem(z + hop, 4)
        return remote(
            piece(index, there % 2),
            block(index, me),
            send_sems.at[index, hop],
            recv_sems.at[index, me],
            req=2 * there + y,
        )

    def across(index):
        return remote(
            piece(index, mine),
            block(index, me),
            send_sems.at[index, 0],
            recv_sems.at[index, me],
            req=y_mate,
        )

    def onward(index, hop):
        origin = 2 * lax.rem(z + hop, 4) + y
        held = block(index, origin)
        return remote(
            held, held, send_sems.at[index, 3 + hop], recv_sems.at[index, origin], req=y_mate
        )

    def keep(index):
        return pltpu.make_async_copy(piece(index, mine), block(index, me), local_sems.at[index])

    def arrived(index, origin):
        held = block(index, origin)
        remote(
            held, held, send_sems.at[index, 0], recv_sems.at[index, origin], req=y_mate
        ).wait_recv()

    def pump(index):
        for hop in (1, 3, 2):
            arrived(index, 2 * lax.rem(z + hop, 4) + y)
            onward(index, hop).start()
            if index + AHEAD < PIECES:
                along(index + AHEAD, hop).start()

    def complete(index):
        for hop in (0, 1, 3, 2):
            arrived(index, 2 * lax.rem(z + hop, 4) + 1 - y)
        keep(index).wait()

    def load_tokens(quarter):
        rows = pl.ds(pl.multiple_of(quarter * SPAN, SPAN), SPAN)
        return pltpu.make_async_copy(tokens.at[rows, :], tok.at[rows, :], token_sems.at[quarter])

    def quarters(which, quarter):
        return normed.at[which, pl.ds(pl.multiple_of(quarter * SPAN, SPAN), SPAN), :]

    def share_tokens():
        held = quarters(mine, part)
        return remote(held, held, spread_send.at[0], spread_recv.at[part], req=z_mate)

    def spread_tokens(slot):
        quarter = x_mate if slot == 2 else part
        held = quarters(other, quarter)
        return remote(
            held, held, spread_send.at[1 + slot], spread_recv.at[quarter],
            tp=x_mate if slot == 0 else core_mate,
        )

    def tokens_arrived(quarter):
        held = quarters(other, quarter)
        remote(held, held, spread_send.at[0], spread_recv.at[quarter], req=z_mate).wait_recv()

    def share_info():
        held = info.at[mine]
        return remote(held, held, info_sems.at[0], info_sems.at[1], req=z_mate)

    def share_shrunk(to_mate, hop):
        slot = 4 * to_mate + hop
        held = shrunk_all.at[2 * part + mine]
        return remote(
            held,
            held,
            shrunk_send.at[slot],
            shrunk_recv.at[2 * part + mine],
            req=z_mate if to_mate else me,
            tp=lax.rem(part + hop, 4),
        )

    shrunk_hops = [(0, 1), (0, 2), (0, 3), (1, 0), (1, 1), (1, 2), (1, 3)]

    for step in range(4):
        load_tokens(lax.rem(part + step, 4)).start()

    barrier = pltpu.get_barrier_semaphore()

    def greet(req, tp):
        pl.semaphore_signal(
            barrier, inc=1, device_id={"req": req, "tp": tp}, device_id_type=MESH
        )

    for hop in (1, 2, 3):
        greet(2 * lax.rem(z + hop, 4) + y, part)
    greet(y_mate, part)
    for hop in (1, 2, 3):
        greet(me, lax.rem(part + hop, 4))
        greet(z_mate, lax.rem(part + hop, 4))
    pl.semaphore_wait(barrier, 10)

    for index in range(AHEAD):
        for hop in (1, 3, 2):
            along(index, hop).start()
    for index in range(PIECES):
        across(index).start()

    gains = jnp.concatenate([gain[i : i + 1, :] for i in range(16)], axis=1).astype(jnp.float32)

    def normalise(quarter):
        load_tokens(quarter).wait()

        def some(step, carry):
            rows = pl.ds(pl.multiple_of(quarter * SPAN + step * 32, 32), 32)
            floats = tok[rows, :].astype(jnp.float32)
            mean = jnp.mean(floats * floats, axis=-1, keepdims=True)
            normed[mine, rows, :] = (floats * lax.rsqrt(mean + norm_eps) * gains).astype(
                jnp.bfloat16
            )
            return carry

        lax.fori_loop(0, SPAN // 32, some, 0)

    normalise(part)
    share_tokens().start()

    segment = segment_in[...].astype(jnp.float32)
    ordinal = lax.broadcasted_iota(jnp.int32, segment.shape, 1).astype(jnp.float32)
    place = jnp.zeros_like(segment)
    start = jnp.zeros_like(segment)
    for request in range(request_position.shape[1]):
        slot = slots[in_use[request_position[0, request]]]
        here = segment == float(request)
        place = jnp.where(here, slot.astype(jnp.float32), place)
        before = jnp.sum(jnp.where(segment < float(request), 1.0, 0.0), axis=1, keepdims=True)
        start = jnp.where(here, before, start)
    info[mine] = jnp.concatenate(
        [segment, place, ordinal - start, jnp.zeros((5, segment.shape[1]), jnp.float32)], axis=0
    )
    share_info().start()
    for index in range(PIECES):
        keep(index).start()
    normalise(lax.rem(part + 1, 4))
    pump(DOWN)
    normalise(lax.rem(part + 2, 4))
    normalise(lax.rem(part + 3, 4))
    pump(QUERY_0)

    def prepare(which):
        facts = info[which]
        columns = facts.T
        for block in range(4):
            first = max(0, block - 2) * SPAN
            width = min(block + 1, 3) * SPAN
            query_segment = columns[block * SPAN : (block + 1) * SPAN, 0:1]
            key_segment = facts[0:1, first : first + width]
            query_order = block * SPAN + lax.broadcasted_iota(jnp.int32, (SPAN, width), 0)
            key_order = first + lax.broadcasted_iota(jnp.int32, (SPAN, width), 1)
            allowed = (query_segment == key_segment) & (key_order <= query_order)
            limit[which, pl.ds(block * SPAN, SPAN), pl.ds(0, width)] = jnp.where(
                allowed, FAR, NEVER
            )
        lane = lax.broadcasted_iota(jnp.int32, (4 * SPAN, REACH), 1).astype(jnp.float32)
        chosen = jnp.where(columns[:, 2:3] == lane, 1.0, 0.0).astype(jnp.bfloat16)
        rotation[which] = jnp.dot(
            chosen, table[0], preferred_element_type=jnp.float32
        ) + jnp.dot(chosen, table[1], preferred_element_type=jnp.float32)

    prepare(mine)
    pump(KEY_0)
    share_info().wait_recv()
    prepare(other)
    tokens_arrived(part)
    spread_tokens(0).start()
    spread_tokens(1).start()
    pump(UP)
    complete(DOWN)

    def shrink(which):
        columns = pl.ds(pl.multiple_of(mine * 1024, 1024), 1024)
        product = lax.dot_general(
            down_all[...].reshape(8 * RANK, 1024),
            normed[which, :, columns],
            NT,
            preferred_element_type=jnp.float32,
        )
        places = info[which][1:2, :]
        total = jnp.zeros((RANK, product.shape[1]), jnp.float32)
        for origin in range(8):
            wanted = (2 * origin + x).astype(jnp.float32)
            total = total + jnp.where(
                places == wanted, product[origin * RANK : (origin + 1) * RANK], 0.0
            )
        at = pl.ds(pl.multiple_of(which * 512, 512), 512)
        shrunk_all[2 * part + mine, :, at] = total.astype(jnp.bfloat16)

    shrink(mine)
    tokens_arrived(x_mate)
    spread_tokens(2).start()
    pump(VALUE_0)
    tokens_arrived(core_mate)
    tokens_arrived(2 * (1 - x) + 1 - core)
    shrink(other)
    for to_mate, hop in shrunk_hops:
        share_shrunk(to_mate, hop).start()

    def projected(which, index):
        return jnp.dot(
            normed[which],
            weight_all[weight_slot[index]].reshape(8 * 256, 128),
            preferred_element_type=jnp.float32,
        )

    def shrunk_of(which, kind):
        at = pl.ds(pl.multiple_of(which * 512, 512), 512)
        total = jnp.zeros((RANK, 512), jnp.float32)
        for slot in range(2):
            for half in range(2):
                total = total + shrunk_all[2 * (2 * slot + kind) + half, :, at].astype(jnp.float32)
        return total

    def lay(which, kind):
        columns = info[which].T
        compact = shrunk_of(which, kind)
        padded = jnp.concatenate(
            [compact, jnp.zeros((128 - RANK, compact.shape[1]), jnp.float32)], axis=0
        ).T
        lane = lax.broadcasted_iota(jnp.int32, (128, PLACES * RANK), 1)
        row = lax.broadcasted_iota(jnp.int32, (128, PLACES * RANK), 0)
        tile = jnp.where(lane % RANK == row, 1.0, 0.0).astype(jnp.bfloat16)
        tiled = jnp.dot(
            padded.astype(jnp.bfloat16), tile, preferred_element_type=jnp.float32
        )
        lanes = lax.broadcasted_iota(jnp.int32, tiled.shape, 1) // RANK
        laid[which, kind] = jnp.where(
            columns[:, 1:2] == lanes.astype(jnp.float32), tiled, 0.0
        ).astype(jnp.bfloat16)

    def change(which, kind, pair):
        ups = up_all[:, :, pl.ds(pair * 128, 128)].reshape(8, 2, 2, RANK, 128)
        return adapter_scale * jnp.dot(
            laid[which, kind],
            ups[:, :, kind].reshape(PLACES * RANK, 128),
            preferred_element_type=jnp.float32,
        )

    def rotated(which, value):
        half = HEAD_WIDTH // 2
        low = lax.broadcasted_iota(jnp.int32, (512, 128), 1) % HEAD_WIDTH < half
        swapped = jnp.where(low, pltpu.roll(value, 128 - half, 1), pltpu.roll(value, half, 1))
        return value * rotation[which, :, 0:128] + swapped * rotation[which, :, 128:256]

    def make_key(pair):
        def one(which, carry):
            key = projected(which, KEY_1 if pair else KEY_0)
            key_heads[which, pair] = rotated(which, key).astype(jnp.bfloat16)
            return carry

        lax.fori_loop(0, 2, one, 0)

    def make_query(pair):
        def one(which, carry):
            query = projected(which, QUERY_1 if pair else QUERY_0) + change(which, 0, pair)
            query_heads[which, pair] = (rotated(which, query) * 0.125).astype(jnp.bfloat16)
            return carry

        lax.fori_loop(0, 2, one, 0)

    def make_value(pair):
        def one(which, carry):
            value = projected(which, VALUE_1 if pair else VALUE_0) + change(which, 1, pair)
            value_heads[which, pair] = value.astype(jnp.bfloat16)
            return carry

        lax.fori_loop(0, 2, one, 0)

    complete(KEY_0)
    make_key(0)
    pump(QUERY_1)
    complete(QUERY_0)
    complete(UP)
    for to_mate, hop in shrunk_hops:
        slot = 2 * lax.rem(part + hop, 4) + (other if to_mate else mine)
        held = shrunk_all.at[slot]
        remote(held, held, shrunk_send.at[0], shrunk_recv.at[slot], req=z_mate).wait_recv()

    def lay_all(which, carry):
        lay(which, 0)
        lay(which, 1)
        return carry

    lax.fori_loop(0, 2, lay_all, 0)
    make_query(0)
    pump(KEY_1)
    complete(VALUE_0)
    make_value(0)

    def attend(which, pair):
        left = lax.broadcasted_iota(jnp.int32, (SPAN, 128), 1) < HEAD_WIDTH
        for part_of in range(4):
            first = max(0, part_of - 2) * SPAN
            width = min(part_of + 1, 3) * SPAN
            rows = pl.ds(part_of * SPAN, SPAN)
            query = query_heads[which, pair, rows, :]
            keys = key_heads[which, pair, pl.ds(first, width), :]
            values = value_heads[which, pair, pl.ds(first, width), :]
            results = []
            for head in range(2):
                own = left if head == 0 else jnp.logical_not(left)
                masked = jnp.where(own, query, jnp.zeros_like(query))
                scores = lax.dot_general(masked, keys, NT, preferred_element_type=jnp.float32)
                scores = jnp.minimum(scores, limit[which, rows, pl.ds(0, width)])
                peak = jnp.max(scores, axis=-1, keepdims=True)
                exponent = jnp.exp(scores - peak)
                total = jnp.sum(exponent, axis=-1, keepdims=True)
                weighed = jnp.dot(
                    exponent.astype(jnp.bfloat16), values, preferred_element_type=jnp.float32
                )
                results.append(weighed / total)
            attended[which, rows, pl.ds(pair * 128, 128)] = jnp.where(
                left, results[0], results[1]
            ).astype(jnp.bfloat16)

    attend(other, 0)
    pump(VALUE_1)
    attend(mine, 0)
    complete(QUERY_1)
    make_query(1)
    complete(KEY_1)
    make_key(1)
    pump(OUTPUT_0)
    complete(VALUE_1)
    make_value(1)
    attend(other, 1)
    pump(OUTPUT_1)
    attend(mine, 1)
    keep(OUTPUT_0).wait()
    keep(OUTPUT_1).wait()

    chunks = sent_core.shape[1]
    rows_of = sent_core.shape[3]

    def product(target, side, which, chunk):
        return jnp.dot(
            attended[which, pl.ds(pl.multiple_of(chunk * rows_of, rows_of), rows_of), :],
            output_all[2 * target + side],
            preferred_element_type=jnp.float32,
        )

    def core_copy(phase, chunk):
        return remote(
            sent_core.at[phase, chunk], got_core.at[phase, chunk],
            reduce_send.at[0, phase, chunk], reduce_recv.at[0, phase, chunk], tp=core_mate,
        )

    def second_copy(phase, chunk):
        to = {"tp": x_mate} if phase == 0 else {"req": z_mate}
        return remote(
            sent_second.at[phase, chunk], got_second.at[phase, chunk],
            reduce_send.at[1, phase, chunk], reduce_recv.at[1, phase, chunk], **to,
        )

    def third_copy(phase, chunk):
        to = {"req": z_mate} if phase == 0 else {"tp": x_mate}
        return remote(
            sent_third.at[phase, chunk], got_third.at[phase, chunk],
            reduce_send.at[2, phase, chunk], reduce_recv.at[2, phase, chunk], **to,
        )

    def side_of(phase):
        return y if phase == 0 else 1 - y

    for phase in range(2):
        if phase == 1:
            for hop in (0, 1, 3, 2):
                arrived(OUTPUT_0, 2 * lax.rem(z + hop, 4) + 1 - y)
                arrived(OUTPUT_1, 2 * lax.rem(z + hop, 4) + 1 - y)
        side = side_of(phase)

        def first(chunk, carry):
            for column in range(2):
                for which in range(2):
                    sent_core[phase, chunk, 2 * column + which] = product(
                        2 * column + 1 - core, side, which, chunk
                    ).astype(jnp.bfloat16)
            core_copy(phase, chunk).start()
            return carry

        lax.fori_loop(0, chunks, first, 0)

    for phase in range(2):
        side = side_of(phase)

        def second(chunk, carry):
            core_copy(phase, chunk).wait_recv()
            for step in range(2):
                column, which = (1 - x, step) if phase == 0 else (step, other)
                sent_second[phase, chunk, step] = (
                    product(2 * column + core, side, which, chunk)
                    + got_core[phase, chunk, 2 * column + which].astype(jnp.float32)
                ).astype(jnp.bfloat16)
            second_copy(phase, chunk).start()
            for step in range(2):
                column, which = (x, step) if phase == 0 else (step, mine)
                kept_second[phase, chunk, step] = product(
                    2 * column + core, side, which, chunk
                ) + got_core[phase, chunk, 2 * column + which].astype(jnp.float32)
            return carry

        lax.fori_loop(0, chunks, second, 0)

    for phase in range(2):

        def third(chunk, carry):
            second_copy(phase, chunk).wait_recv()
            sent, held = (other, mine) if phase == 0 else (1 - x, x)
            sent_third[phase, chunk] = (
                kept_second[phase, chunk, sent]
                + got_second[phase, chunk, sent].astype(jnp.float32)
            ).astype(jnp.bfloat16)
            third_copy(phase, chunk).start()
            kept_third[phase, chunk] = kept_second[phase, chunk, held] + got_second[
                phase, chunk, held
            ].astype(jnp.float32)
            return carry

        lax.fori_loop(0, chunks, third, 0)

    for phase in range(2):
        side = side_of(phase)

        def last(chunk, carry):
            third_copy(phase, chunk).wait_recv()
            rows = pl.ds(pl.multiple_of(chunk * rows_of, rows_of), rows_of)
            residual = tok[rows, pl.ds(pl.multiple_of(part * 512 + side * 256, 256), 256)]
            out[rows, pl.ds(pl.multiple_of(side * 256, 256), 256)] = (
                kept_third[phase, chunk]
                + got_third[phase, chunk].astype(jnp.float32)
                + residual.astype(jnp.float32)
            ).astype(jnp.bfloat16)
            return carry

        lax.fori_loop(0, chunks, last, 0)

    for index in range(PIECES):
        for hop in (1, 2, 3):
            along(index, hop).wait_send()
            onward(index, hop).wait_send()
        across(index).wait_send()
    share_tokens().wait_send()
    for slot in range(3):
        spread_tokens(slot).wait_send()
    share_info().wait_send()
    for to_mate, hop in shrunk_hops:
        share_shrunk(to_mate, hop).wait_send()
    for phase in range(2):
        for chunk in range(chunks):
            core_copy(phase, chunk).wait_send()
            second_copy(phase, chunk).wait_send()
            third_copy(phase, chunk).wait_send()


def fused_layer(
    tokens, segment, request_position, in_use, slots, gain,
    query_weight, key_weight, value_weight, output_weight, down, up,
):
    bf16, f32 = jnp.bfloat16, jnp.float32
    rows, width = tokens.shape
    chunks = 4
    piece = rows // chunks
    hbm = pl.BlockSpec(memory_space=pltpu.HBM)
    vmem = pl.BlockSpec(memory_space=pltpu.VMEM)
    smem = pl.BlockSpec(memory_space=pltpu.SMEM)
    dma = pltpu.SemaphoreType.DMA
    return pl.pallas_call(
        layer_kernel,
        out_shape=jax.ShapeDtypeStruct((rows, 512), bf16),
        in_specs=[hbm, vmem, smem, smem, smem, vmem, vmem] + [hbm] * 6,
        out_specs=vmem,
        scratch_shapes=[
            pltpu.VMEM((rows, width), bf16),
            pltpu.VMEM((2, rows, width), bf16),
            pltpu.VMEM((2, 8, rows), f32),
            pltpu.VMEM((2, rows, 3 * SPAN), f32),
            pltpu.VMEM((2, rows, 256), f32),
            pltpu.VMEM((8, RANK, 1024), bf16),
            pltpu.VMEM((6, 8, 256, 128), bf16),
            pltpu.VMEM((8, 64, 256), bf16),
            pltpu.VMEM((8, 256, 256), bf16),
            pltpu.VMEM((8, RANK, 2 * rows), bf16),
            pltpu.VMEM((2, 2, rows, 256), bf16),
            pltpu.VMEM((2, 2, rows, 128), bf16),
            pltpu.VMEM((2, 2, rows, 128), bf16),
            pltpu.VMEM((2, 2, rows, 128), bf16),
            pltpu.VMEM((2, rows, 256), bf16),
            pltpu.VMEM((2, chunks, 4, piece, 256), bf16),
            pltpu.VMEM((2, chunks, 4, piece, 256), bf16),
            pltpu.VMEM((2, chunks, 2, piece, 256), bf16),
            pltpu.VMEM((2, chunks, 2, piece, 256), bf16),
            pltpu.VMEM((2, chunks, 2, piece, 256), f32),
            pltpu.VMEM((2, chunks, piece, 256), bf16),
            pltpu.VMEM((2, chunks, piece, 256), bf16),
            pltpu.VMEM((2, chunks, piece, 256), f32),
            dma((4,)),
            dma((PIECES, 7)),
            dma((PIECES, 8)),
            dma((PIECES,)),
            dma((4,)),
            dma((4,)),
            dma((2,)),
            dma((8,)),
            dma((8,)),
            dma((3, 2, chunks)),
            dma((3, 2, chunks)),
        ],
        compiler_params=pltpu.CompilerParams(
            collective_id=0, has_side_effects=True, vmem_limit_bytes=56 * 1024 * 1024
        ),
    )(
        tokens, segment, request_position, in_use, slots, gain.reshape(16, 128),
        jnp.asarray(rotation_tables()),
        down.reshape(-1, width), query_weight, key_weight, value_weight,
        up.reshape(-1, up.shape[3]), output_weight,
    )


def active_rows(stored, active_slots):
    slot_total = stored.shape[0]
    held = lax.axis_index("req") * slot_total + jnp.arange(slot_total, dtype=jnp.int32)
    chosen = (active_slots[:, None] == held[None, :]).astype(stored.dtype)
    rows = jnp.einsum(
        "as,srd->ard", chosen, stored, preferred_element_type=jnp.float32
    ).astype(stored.dtype)
    return lax.psum(rows, "req").reshape(-1, stored.shape[2])


def positions_of(segment):
    ordinal = jnp.arange(segment.shape[0], dtype=jnp.int32)
    before = segment[None, :] < segment[:, None]
    return ordinal - jnp.sum(before.astype(jnp.int32), axis=1)


def apply_rotation(values, token_positions):
    half_dim = HEAD_WIDTH // 2
    frequency = rope_base ** (-(jnp.arange(half_dim, dtype=jnp.float32) * 2.0 / HEAD_WIDTH))
    angles = token_positions.astype(jnp.float32)[:, None] * frequency[None, :]
    cosine = jnp.cos(angles)[:, None, :]
    sine_part = jnp.sin(angles)[:, None, :]
    first_half = values[..., :half_dim]
    second_half = values[..., half_dim:]
    return jnp.concatenate(
        [
            first_half * cosine - second_half * sine_part,
            second_half * cosine + first_half * sine_part,
        ],
        axis=-1,
    )


def attend(query_per_head, key_heads, value_per_head, segment):
    scores = (
        jnp.einsum("qhd,khd->hqk", query_per_head, key_heads, preferred_element_type=jnp.float32)
        * 0.125
    )
    ordinal = jnp.arange(segment.shape[0], dtype=jnp.int32)
    allowed = (segment[:, None] == segment[None, :]) & (ordinal[None, :] <= ordinal[:, None])
    scores = jnp.where(allowed[None], scores, jnp.float32(-1e30))
    row_peak = jnp.max(scores, axis=-1, keepdims=True)
    exponent = jnp.where(allowed[None], jnp.exp(scores - row_peak), jnp.float32(0.0))
    weights = (exponent / jnp.sum(exponent, axis=-1, keepdims=True)).astype(jnp.bfloat16)
    return jnp.einsum(
        "hqk,khd->qhd", weights, value_per_head, preferred_element_type=jnp.float32
    ).astype(jnp.bfloat16)


def local(
    tokens,
    token_request_number,
    request_adapter_position,
    adapters_in_use,
    adapter_storage_slot,
    input_norm_gain,
    query_weight,
    key_weight,
    value_weight,
    output_weight,
    adapter_down_weight,
    adapter_up_weight,
):
    if (
        lax.axis_size("req") == 8
        and lax.axis_size("tp") == 4
        and tokens.shape == (512, 2048)
        and adapter_down_weight.shape == (2, 2, 16, 2048)
    ):
        return fused_layer(
            tokens,
            token_request_number,
            request_adapter_position,
            adapters_in_use,
            adapter_storage_slot,
            input_norm_gain,
            query_weight,
            key_weight,
            value_weight,
            output_weight,
            adapter_down_weight,
            adapter_up_weight,
        )
    row_total, model_width = tokens.shape
    local_width = query_weight.shape[1]
    reduced_rows = adapter_down_weight.shape[2]
    slot_total = adapter_down_weight.shape[0]
    segment = token_request_number[0]
    request_adapters = request_adapter_position[0]
    tp_total = lax.axis_size("tp")
    req_total = lax.axis_size("req")
    part_rows = reduced_rows // tp_total
    share = 2 * part_rows
    down_part = lax.dynamic_slice_in_dim(
        adapter_down_weight, lax.axis_index("tp") * part_rows, part_rows, 2
    ).reshape(slot_total, share, model_width)
    up_part = adapter_up_weight.reshape(slot_total, 2 * reduced_rows, local_width)
    active_slots = jnp.take(adapter_storage_slot, adapters_in_use, axis=0)
    place_total = active_slots.shape[0]
    request_places = request_adapters
    member = segment[:, None] == jnp.arange(request_adapters.shape[0], dtype=jnp.int32)[None, :]
    token_place = jnp.sum(
        jnp.where(member, request_places[None, :], jnp.zeros_like(request_places)[None, :]),
        axis=1,
    )
    column = jnp.arange(place_total * share, dtype=jnp.int32)
    mask = (token_place[:, None] == (column // share)[None, :]).astype(jnp.bfloat16)
    lanes = max(128, tp_total * share)
    fold = (lax.axis_index("tp") * share + column % share)[:, None] == jnp.arange(
        lanes, dtype=jnp.int32
    )[None, :]
    fold = fold.astype(jnp.bfloat16)
    floats = tokens.astype(jnp.float32)
    normed = (
        floats
        * lax.rsqrt(jnp.mean(floats * floats, axis=-1, keepdims=True) + norm_eps)
        * input_norm_gain.astype(jnp.float32)
    ).astype(jnp.bfloat16)
    down_all = active_rows(down_part, active_slots)
    up_all = active_rows(up_part, active_slots)
    output_full = lax.all_gather(output_weight, "req", axis=1, tiled=True)
    query_plain, key_base, value_plain = [
        jnp.dot(
            normed,
            lax.all_gather(weight, "req", axis=0, tiled=True),
            preferred_element_type=jnp.float32,
        )
        for weight in (query_weight, key_weight, value_weight)
    ]
    shrunk_all = lax.dot_general(
        normed, down_all, (((1,), (1,)), ((), ())), preferred_element_type=jnp.float32
    ).astype(jnp.bfloat16)
    shrunk = lax.psum(
        jnp.dot(shrunk_all * mask, fold, preferred_element_type=jnp.float32), "tp"
    ).astype(jnp.bfloat16)
    shrunk = shrunk[:, : tp_total * share]
    source = jnp.arange(tp_total * share, dtype=jnp.int32)
    source_kind = (source % share) // part_rows
    source_rank = (source // share) * part_rows + source % part_rows
    target = jnp.arange(place_total * reduced_rows, dtype=jnp.int32)
    mine = token_place[:, None] == (target // reduced_rows)[None, :]
    up_all = up_all.reshape(place_total, 2, reduced_rows, local_width)

    def change_of(kind):
        spread_map = (source_kind == kind)[:, None] & (
            source_rank[:, None] == (target % reduced_rows)[None, :]
        )
        spread = jnp.dot(
            shrunk, spread_map.astype(jnp.bfloat16), preferred_element_type=jnp.float32
        ).astype(jnp.bfloat16)
        spread = jnp.where(mine, spread, jnp.zeros((), jnp.bfloat16))
        return jnp.dot(
            spread,
            up_all[:, kind].reshape(place_total * reduced_rows, local_width),
            preferred_element_type=jnp.float32,
        )

    query_change = change_of(0)
    value_change = change_of(1)
    head_total = local_width // HEAD_WIDTH
    token_positions = positions_of(segment)
    query_per_head = apply_rotation(
        (query_plain + adapter_scale * query_change).reshape(row_total, head_total, HEAD_WIDTH),
        token_positions,
    ).astype(jnp.bfloat16)
    key_heads = apply_rotation(
        key_base.reshape(row_total, head_total, HEAD_WIDTH), token_positions
    ).astype(jnp.bfloat16)
    value_per_head = (
        (value_plain + adapter_scale * value_change)
        .astype(jnp.bfloat16)
        .reshape(row_total, head_total, HEAD_WIDTH)
    )
    attended = attend(query_per_head, key_heads, value_per_head, segment).reshape(
        row_total, local_width
    )
    share_width = model_width // tp_total
    residual_part = lax.dynamic_slice_in_dim(
        tokens, lax.axis_index("tp") * share_width, share_width, 1
    )
    partial_out = jnp.dot(attended, output_full, preferred_element_type=jnp.float32)
    summed = lax.psum_scatter(
        partial_out.astype(jnp.bfloat16), "tp", scatter_dimension=1, tiled=True
    ).astype(jnp.float32)
    return (summed + residual_part.astype(jnp.float32)).astype(jnp.bfloat16)


def solution(mesh):
    in_specs = (
        P("req", None),
        P("req", None),
        P("req", None),
        P(),
        P(),
        P(),
        P("req", "tp"),
        P("req", "tp"),
        P("req", "tp"),
        P("tp", "req"),
        P("req", None, None, None),
        P("req", None, None, "tp"),
    )
    out_specs = P("req", "tp")
    return jax.shard_map(local, mesh=mesh, in_specs=in_specs, out_specs=out_specs, check_vma=False)
```

```python
import functools

import jax
import jax.numpy as jnp
import numpy as np
from jax import lax
from jax.experimental import pallas as pl
from jax.experimental.pallas import tpu as pltpu
from jax.sharding import PartitionSpec as P

HEAD_WIDTH = 64


norm_eps = 1e-05
rope_base = 130000.0
adapter_scale = 2.0

MESH = pl.DeviceIdType.MESH
DOWN, QUERY_0, KEY_0, UP, VALUE_0, QUERY_1, KEY_1, VALUE_1, OUTPUT_0, OUTPUT_1 = range(10)
PIECES = 10
AHEAD = 2
TOKEN_ROWS = 32
SPAN = 128
PLACES = 16
RANK = 16
REACH = 256
FAR = 3.0e38
NEVER = -1.0e30
NT = (((1,), (1,)), ((), ()))
TN = (((0,), (0,)), ((), ()))


def rotation_tables():
    half = HEAD_WIDTH // 2
    lane = np.arange(128)
    frequency = np.float32(rope_base) ** (-(np.arange(half, dtype=np.float32) * 2.0 / HEAD_WIDTH))
    angles = np.arange(REACH, dtype=np.float32)[:, None] * frequency.astype(np.float32)[None, lane % half]
    angles = angles.astype(np.float64)
    sign = np.where(lane % HEAD_WIDTH < half, -1.0, 1.0)
    table = np.concatenate([np.cos(angles), np.sin(angles) * sign], axis=1).astype(np.float32)
    high = table.astype(jnp.bfloat16)
    low = (table - high.astype(np.float32)).astype(jnp.bfloat16)
    return np.stack([high, low])


def layer_kernel(
    tokens, segment_hbm, request_hbm, in_use_hbm, slots_hbm, gain_hbm, table_hbm,
    down, query_weight, key_weight, value_weight, up, output_weight,
    out,
    segment_in, request_position, in_use, slots, gain, table, operand_sems,
    tok, normed, info, limit, rotation,
    down_all, weight_all, up_all, output_all,
    shrunk_all, laid, query_heads, key_heads, value_heads, attended,
    sent_core, got_core, sent_x, got_x, kept, sent_z, got_z,
    token_sems, send_sems, recv_sems, local_sems,
    spread_send, spread_recv, info_sems, shrunk_send, shrunk_recv, attended_send, attended_recv,
    core_send, core_recv, x_send, x_recv, z_send, z_recv,
):
    me = lax.axis_index("req")
    part = lax.axis_index("tp")
    z, y = me // 2, me % 2
    x, core = part // 2, part % 2
    mine = z % 2
    other = 1 - mine
    z_mate = 2 * (z + 1 - 2 * mine) + y
    y_mate = 2 * z + 1 - y
    core_mate = 2 * x + 1 - core
    x_mate = 2 * (1 - x) + core
    weights = {
        QUERY_0: (query_weight, 0), KEY_0: (key_weight, 0), VALUE_0: (value_weight, 0),
        QUERY_1: (query_weight, 1), KEY_1: (key_weight, 1), VALUE_1: (value_weight, 1),
    }
    weight_slot = {name: slot for slot, name in enumerate(weights)}

    def piece(index, half):
        if index == DOWN:
            rows = pl.ds(pl.multiple_of(part * 16, 16), 16)
            return down.at[rows, pl.ds(pl.multiple_of(half * 1024, 1024), 1024)]
        if index == UP:
            return up.at[:, pl.ds(pl.multiple_of(half * 256, 256), 256)]
        if index in weights:
            weight, pair = weights[index]
            return weight.at[:, pl.ds(pl.multiple_of(half * 256 + pair * 128, 128), 128)]
        rows = pl.ds((index - OUTPUT_0) * 256, 256)
        return output_weight.at[rows, pl.ds(pl.multiple_of(half * 128, 128), 128)]

    def block(index, origin):
        if index == DOWN:
            return down_all.at[origin]
        if index == UP:
            return up_all.at[origin]
        if index in weights:
            return weight_all.at[weight_slot[index], origin]
        return output_all.at[origin, pl.ds((index - OUTPUT_0) * 256, 256), :]

    def remote(source, target, send, recv, req=None, tp=None):
        return pltpu.make_async_remote_copy(
            src_ref=source,
            dst_ref=target,
            send_sem=send,
            recv_sem=recv,
            device_id={
                "req": me if req is None else req,
                "tp": part if tp is None else tp,
            },
            device_id_type=MESH,
        )

    def along(index, hop):
        there = lax.rem(z + hop, 4)
        return remote(
            piece(index, there % 2),
            block(index, me),
            send_sems.at[index, hop],
            recv_sems.at[index, me],
            req=2 * there + y,
        )

    def across(index):
        return remote(
            piece(index, mine),
            block(index, me),
            send_sems.at[index, 0],
            recv_sems.at[index, me],
            req=y_mate,
        )

    def onward(index, hop):
        origin = 2 * lax.rem(z + hop, 4) + y
        held = block(index, origin)
        return remote(
            held, held, send_sems.at[index, 3 + hop], recv_sems.at[index, origin], req=y_mate
        )

    def keep(index):
        return pltpu.make_async_copy(piece(index, mine), block(index, me), local_sems.at[index])

    def arrived(index, origin):
        held = block(index, origin)
        remote(
            held, held, send_sems.at[index, 0], recv_sems.at[index, origin], req=y_mate
        ).wait_recv()

    def pump(index, hops=(1, 3, 2)):
        for hop in hops:
            arrived(index, 2 * lax.rem(z + hop, 4) + y)
            onward(index, hop).start()
            if index + AHEAD < PIECES:
                along(index + AHEAD, hop).start()

    def complete(index):
        for hop in (0, 1, 3, 2):
            arrived(index, 2 * lax.rem(z + hop, 4) + 1 - y)
        keep(index).wait()

    def load_tokens(quarter):
        rows = pl.ds(pl.multiple_of(quarter * SPAN, SPAN), SPAN)
        return pltpu.make_async_copy(tokens.at[rows, :], tok.at[rows, :], token_sems.at[quarter])

    def quarters(which, quarter):
        return normed.at[which, pl.ds(pl.multiple_of(quarter * SPAN, SPAN), SPAN), :]

    def token_rows(which, quarter, step):
        first = quarter * SPAN + step * TOKEN_ROWS
        return normed.at[which, pl.ds(pl.multiple_of(first, TOKEN_ROWS), TOKEN_ROWS), :]

    def share_tokens(step):
        held = token_rows(mine, part, step)
        return remote(
            held, held, spread_send.at[0, step], spread_recv.at[part, step], req=z_mate
        )

    def spread_tokens(slot, step):
        quarter = x_mate if slot == 3 else part
        held = token_rows(other, quarter, step)
        return remote(
            held, held, spread_send.at[slot, step], spread_recv.at[quarter, step],
            tp=x_mate if slot == 1 else core_mate,
        )

    def tokens_arrived(quarter, step):
        held = token_rows(other, quarter, step)
        remote(
            held, held, spread_send.at[0, step], spread_recv.at[quarter, step], req=z_mate
        ).wait_recv()

    def spread(step):
        tokens_arrived(part, step)
        spread_tokens(1, step).start()
        spread_tokens(2, step).start()

    def pass_tokens(step):
        tokens_arrived(x_mate, step)
        spread_tokens(3, step).start()

    def share_info():
        held = info.at[mine]
        return remote(held, held, info_sems.at[0], info_sems.at[1], req=z_mate)

    def share_shrunk(to_mate, hop):
        slot = 4 * to_mate + hop
        held = shrunk_all.at[2 * part + mine]
        return remote(
            held,
            held,
            shrunk_send.at[slot],
            shrunk_recv.at[2 * part + mine],
            req=z_mate if to_mate else me,
            tp=lax.rem(part + hop, 4),
        )

    shrunk_hops = [(0, 1), (0, 2), (0, 3), (1, 0), (1, 1), (1, 2), (1, 3)]

    operands = [
        pltpu.make_async_copy(source, target, operand_sems.at[number])
        for number, (source, target) in enumerate(
            [
                (gain_hbm, gain), (segment_hbm, segment_in), (request_hbm, request_position),
                (in_use_hbm, in_use), (slots_hbm, slots), (table_hbm, table),
            ]
        )
    ]
    load_tokens(part).start()
    for operand in operands:
        operand.start()
    for step in range(1, 4):
        load_tokens(lax.rem(part + step, 4)).start()

    barrier = pltpu.get_barrier_semaphore()

    def greet(req, tp):
        pl.semaphore_signal(
            barrier, inc=1, device_id={"req": req, "tp": tp}, device_id_type=MESH
        )

    for hop in (1, 2, 3):
        greet(2 * lax.rem(z + hop, 4) + y, part)
    greet(y_mate, part)
    for hop in (1, 2, 3):
        greet(me, lax.rem(part + hop, 4))
        greet(z_mate, lax.rem(part + hop, 4))
    pl.semaphore_wait(barrier, 10)

    for index in range(AHEAD):
        for hop in (1, 3, 2):
            along(index, hop).start()
    for index in range(PIECES):
        across(index).start()

    operands[0].wait()
    gains = jnp.concatenate([gain[i : i + 1, :] for i in range(16)], axis=1).astype(jnp.float32)

    def normalise(quarter):
        load_tokens(quarter).wait()

        def some(step, carry):
            rows = pl.ds(pl.multiple_of(quarter * SPAN + step * 32, 32), 32)
            floats = tok[rows, :].astype(jnp.float32)
            mean = jnp.mean(floats * floats, axis=-1, keepdims=True)
            normed[mine, rows, :] = (floats * lax.rsqrt(mean + norm_eps) * gains).astype(
                jnp.bfloat16
            )
            return carry

        lax.fori_loop(0, SPAN // 32, some, 0)

    def prepare(which):
        facts = info[which]
        columns = facts.T
        for block in range(4):
            first = max(0, block - 2) * SPAN
            width = min(block + 1, 3) * SPAN
            query_segment = columns[block * SPAN : (block + 1) * SPAN, 0:1]
            key_segment = facts[0:1, first : first + width]
            query_order = block * SPAN + lax.broadcasted_iota(jnp.int32, (SPAN, width), 0)
            key_order = first + lax.broadcasted_iota(jnp.int32, (SPAN, width), 1)
            allowed = (query_segment == key_segment) & (key_order <= query_order)
            limit[which, pl.ds(block * SPAN, SPAN), pl.ds(0, width)] = jnp.where(
                allowed, FAR, NEVER
            )
        lane = lax.broadcasted_iota(jnp.int32, (4 * SPAN, REACH), 1).astype(jnp.float32)
        chosen = jnp.where(columns[:, 2:3] == lane, 1.0, 0.0).astype(jnp.bfloat16)
        rotation[which] = jnp.dot(
            chosen, table[0], preferred_element_type=jnp.float32
        ) + jnp.dot(chosen, table[1], preferred_element_type=jnp.float32)

    def shrink(which):
        columns = pl.ds(pl.multiple_of(mine * 1024, 1024), 1024)
        product = lax.dot_general(
            down_all[...].reshape(8 * RANK, 1024),
            normed[which, :, columns],
            NT,
            preferred_element_type=jnp.float32,
        )
        places = info[which][1:2, :]
        total = jnp.zeros((RANK, product.shape[1]), jnp.float32)
        for origin in range(8):
            wanted = (2 * origin + x).astype(jnp.float32)
            total = total + jnp.where(
                places == wanted, product[origin * RANK : (origin + 1) * RANK], 0.0
            )
        at = pl.ds(pl.multiple_of(which * 512, 512), 512)
        shrunk_all[2 * part + mine, :, at] = total.astype(jnp.bfloat16)

    def projected(which, index):
        return jnp.dot(
            normed[which],
            weight_all[weight_slot[index]].reshape(8 * 256, 128),
            preferred_element_type=jnp.float32,
        )

    def shrunk_of(which, kind):
        at = pl.ds(pl.multiple_of(which * 512, 512), 512)
        total = jnp.zeros((RANK, 512), jnp.float32)
        for slot in range(2):
            for half in range(2):
                total = total + shrunk_all[2 * (2 * slot + kind) + half, :, at].astype(jnp.float32)
        return total

    def lay(which, kind):
        columns = info[which].T
        compact = shrunk_of(which, kind)
        padded = jnp.concatenate(
            [compact, jnp.zeros((128 - RANK, compact.shape[1]), jnp.float32)], axis=0
        ).T
        lane = lax.broadcasted_iota(jnp.int32, (128, PLACES * RANK), 1)
        row = lax.broadcasted_iota(jnp.int32, (128, PLACES * RANK), 0)
        tile = jnp.where(lane % RANK == row, 1.0, 0.0).astype(jnp.bfloat16)
        tiled = jnp.dot(
            padded.astype(jnp.bfloat16), tile, preferred_element_type=jnp.float32
        )
        lanes = lax.broadcasted_iota(jnp.int32, tiled.shape, 1) // RANK
        laid[which, kind] = jnp.where(
            columns[:, 1:2] == lanes.astype(jnp.float32), tiled, 0.0
        ).astype(jnp.bfloat16)

    def change(which, kind, pair):
        ups = up_all[:, :, pl.ds(pair * 128, 128)].reshape(8, 2, 2, RANK, 128)
        return adapter_scale * jnp.dot(
            laid[which, kind],
            ups[:, :, kind].reshape(PLACES * RANK, 128),
            preferred_element_type=jnp.float32,
        )

    def rotated(which, value):
        half = HEAD_WIDTH // 2
        low = lax.broadcasted_iota(jnp.int32, (512, 128), 1) % HEAD_WIDTH < half
        swapped = jnp.where(low, pltpu.roll(value, 128 - half, 1), pltpu.roll(value, half, 1))
        return value * rotation[which, :, 0:128] + swapped * rotation[which, :, 128:256]

    def make_key(pair, which):
        key = projected(which, KEY_1 if pair else KEY_0)
        key_heads[which, pair] = rotated(which, key).astype(jnp.bfloat16)

    def make_query(pair, which):
        query = projected(which, QUERY_1 if pair else QUERY_0) + change(which, 0, pair)
        query_heads[which, pair] = (rotated(which, query) * 0.125).astype(jnp.bfloat16)

    def make_value(pair, which):
        value = projected(which, VALUE_1 if pair else VALUE_0) + change(which, 1, pair)
        value_heads[which, pair] = value.astype(jnp.bfloat16)

    def share_attended(which, pair):
        held = attended.at[mine, pair, which]
        return remote(
            held, held, attended_send.at[pair, which], attended_recv.at[pair, which], req=z_mate
        )

    def attend(which, pair):
        left = lax.broadcasted_iota(jnp.int32, (SPAN, 128), 1) < HEAD_WIDTH
        for part_of in range(4):
            first = max(0, part_of - 2) * SPAN
            width = min(part_of + 1, 3) * SPAN
            rows = pl.ds(part_of * SPAN, SPAN)
            query = query_heads[which, pair, rows, :]
            keys = key_heads[which, pair, pl.ds(first, width), :]
            values = value_heads[which, pair, pl.ds(first, width), :]
            results = []
            for head in range(2):
                own = left if head == 0 else jnp.logical_not(left)
                masked = jnp.where(own, query, jnp.zeros_like(query))
                scores = lax.dot_general(masked, keys, NT, preferred_element_type=jnp.float32)
                scores = jnp.minimum(scores, limit[which, rows, pl.ds(0, width)])
                peak = jnp.max(scores, axis=-1, keepdims=True)
                exponent = jnp.exp(scores - peak)
                total = jnp.sum(exponent, axis=-1, keepdims=True)
                weighed = jnp.dot(
                    exponent.astype(jnp.bfloat16), values, preferred_element_type=jnp.float32
                )
                results.append(weighed / total)
            attended[mine, pair, which, rows, :] = jnp.where(
                left, results[0], results[1]
            ).astype(jnp.bfloat16)
        share_attended(which, pair).start()

    def wait_shrunk():
        for to_mate, hop in shrunk_hops:
            slot = 2 * lax.rem(part + hop, 4) + (other if to_mate else mine)
            held = shrunk_all.at[slot]
            remote(held, held, shrunk_send.at[0], shrunk_recv.at[slot], req=z_mate).wait_recv()

    def lay_all(which, carry):
        lay(which, 0)
        lay(which, 1)
        return carry

    normalise(part)
    for step in range(2):
        share_tokens(step).start()
    for operand in operands[1:]:
        operand.wait()
    segment = segment_in[...].astype(jnp.float32)
    ordinal = lax.broadcasted_iota(jnp.int32, segment.shape, 1).astype(jnp.float32)
    place = jnp.zeros_like(segment)
    start = jnp.zeros_like(segment)
    for request in range(request_position.shape[1]):
        slot = slots[in_use[request_position[0, request]]]
        here = segment == float(request)
        place = jnp.where(here, slot.astype(jnp.float32), place)
        before = jnp.sum(jnp.where(segment < float(request), 1.0, 0.0), axis=1, keepdims=True)
        start = jnp.where(here, before, start)
    info[mine] = jnp.concatenate(
        [segment, place, ordinal - start, jnp.zeros((5, segment.shape[1]), jnp.float32)], axis=0
    )
    share_info().start()
    for index in range(PIECES):
        keep(index).start()
    normalise(lax.rem(part + 1, 4))
    pump(DOWN)
    share_tokens(2).start()
    normalise(lax.rem(part + 2, 4))
    pump(QUERY_0, (1, 3))
    normalise(lax.rem(part + 3, 4))
    pump(QUERY_0, (2,))
    share_tokens(3).start()
    spread(0)
    prepare(mine)
    pump(KEY_0)
    spread(1)
    share_info().wait_recv()
    prepare(other)
    pump(UP)
    spread(2)
    pass_tokens(0)
    complete(DOWN)
    shrink(mine)
    pump(VALUE_0, (1, 3))
    spread(3)
    pass_tokens(1)
    pump(VALUE_0, (2,))
    complete(KEY_0)
    make_key(0, mine)
    pass_tokens(2)
    pass_tokens(3)
    pump(QUERY_1, (1, 3))
    for step in range(SPAN // TOKEN_ROWS):
        tokens_arrived(core_mate, step)
        tokens_arrived(2 * (1 - x) + 1 - core, step)
    shrink(other)
    for to_mate, hop in shrunk_hops:
        share_shrunk(to_mate, hop).start()
    pump(QUERY_1, (2,))
    make_key(0, other)
    complete(QUERY_0)
    complete(UP)
    pump(KEY_1, (1,))
    wait_shrunk()
    lax.fori_loop(0, 2, lay_all, 0)
    pump(KEY_1, (3, 2))
    make_query(0, other)
    make_query(0, mine)
    complete(VALUE_0)
    make_value(0, other)
    pump(VALUE_1, (1,))
    make_value(0, mine)
    attend(other, 0)
    pump(VALUE_1, (3, 2))
    complete(QUERY_1)
    make_query(1, other)
    make_query(1, mine)
    attend(mine, 0)
    pump(OUTPUT_0, (1,))
    complete(KEY_1)
    make_key(1, other)
    make_key(1, mine)
    pump(OUTPUT_0, (3,))
    complete(VALUE_1)
    make_value(1, other)
    attend(other, 1)
    pump(OUTPUT_0, (2,))
    make_value(1, mine)
    attend(mine, 1)
    pump(OUTPUT_1)
    keep(OUTPUT_0).wait()
    keep(OUTPUT_1).wait()

    chunks = sent_core.shape[2]
    rows_of = sent_core.shape[4]

    for pair in range(2):
        for which in range(2):
            held = attended.at[other, pair, which]
            remote(
                held, held, attended_send.at[pair, which], attended_recv.at[pair, which],
                req=z_mate,
            ).wait_recv()

    def rows_at(chunk):
        return pl.ds(pl.multiple_of(chunk * rows_of, rows_of), rows_of)

    def product(side, to_core, which, chunk):
        heads = jnp.concatenate(
            [attended[z_of, pair, which, rows_at(chunk), :] for z_of in range(2) for pair in range(2)],
            axis=1,
        )
        columns = jnp.concatenate(
            [output_all[2 * (2 * x_of + to_core) + side] for x_of in range(2)], axis=1
        )
        return jnp.dot(heads, columns, preferred_element_type=jnp.float32)

    def core_copy(phase, which, chunk):
        return remote(
            sent_core.at[phase, which, chunk], got_core.at[phase, which, chunk],
            core_send.at[phase, which, chunk], core_recv.at[phase, which, chunk], tp=core_mate,
        )

    def x_copy(phase, which, chunk):
        return remote(
            sent_x.at[phase, which, chunk], got_x.at[phase, which, chunk],
            x_send.at[phase, which, chunk], x_recv.at[phase, which, chunk], tp=x_mate,
        )

    def z_copy(phase, chunk):
        return remote(
            sent_z.at[phase, chunk], got_z.at[phase, chunk],
            z_send.at[phase, chunk], z_recv.at[phase, chunk], req=z_mate,
        )

    def write(side, half, chunk, values):
        first = side * 256 + half * 128
        residual = tok[rows_at(chunk), pl.ds(pl.multiple_of(part * 512 + first, 128), 128)]
        out[rows_at(chunk), pl.ds(pl.multiple_of(first, 128), 128)] = (
            values + residual.astype(jnp.float32)
        ).astype(jnp.bfloat16)

    for phase in range(2):
        side = y if phase == 0 else 1 - y
        if phase == 1:
            for hop in (0, 1, 3, 2):
                arrived(OUTPUT_0, 2 * lax.rem(z + hop, 4) + 1 - y)
                arrived(OUTPUT_1, 2 * lax.rem(z + hop, 4) + 1 - y)
        for which in (other, mine):

            def first(chunk, carry):
                share = product(side, 1 - core, which, chunk)
                for x_of in range(2):
                    sent_core[phase, which, chunk, x_of] = share[
                        :, x_of * 128 : (x_of + 1) * 128
                    ].astype(jnp.bfloat16)
                core_copy(phase, which, chunk).start()
                return carry

            lax.fori_loop(0, chunks, first, 0)
        for which in (other, mine):

            def second(chunk, carry):
                share = product(side, core, which, chunk)
                core_copy(phase, which, chunk).wait_recv()
                got = got_core[phase, which, chunk].astype(jnp.float32)
                totals = [share[:, 0:128] + got[0], share[:, 128:256] + got[1]]
                first_x = x == 0
                sent_x[phase, which, chunk] = jnp.where(first_x, totals[1], totals[0]).astype(
                    jnp.bfloat16
                )
                x_copy(phase, which, chunk).start()
                kept[phase, which, chunk] = jnp.where(first_x, totals[0], totals[1])
                return carry

            lax.fori_loop(0, chunks, second, 0)

    for phase in range(2):
        side = y if phase == 0 else 1 - y

        def third(chunk, carry):
            x_copy(phase, other, chunk).wait_recv()
            sent_z[phase, chunk] = (
                kept[phase, other, chunk] + got_x[phase, other, chunk].astype(jnp.float32)
            ).astype(jnp.bfloat16)
            z_copy(phase, chunk).start()
            return carry

        lax.fori_loop(0, chunks, third, 0)

    for phase in range(2):
        side = y if phase == 0 else 1 - y

        def own(chunk, carry):
            x_copy(phase, mine, chunk).wait_recv()
            write(
                side, mine, chunk,
                kept[phase, mine, chunk] + got_x[phase, mine, chunk].astype(jnp.float32),
            )
            return carry

        lax.fori_loop(0, chunks, own, 0)

    for phase in range(2):
        side = y if phase == 0 else 1 - y

        def returned(chunk, carry):
            z_copy(phase, chunk).wait_recv()
            write(side, other, chunk, got_z[phase, chunk].astype(jnp.float32))
            return carry

        lax.fori_loop(0, chunks, returned, 0)

    for index in range(PIECES):
        for hop in (1, 2, 3):
            along(index, hop).wait_send()
            onward(index, hop).wait_send()
        across(index).wait_send()
    for step in range(SPAN // TOKEN_ROWS):
        share_tokens(step).wait_send()
        for slot in (1, 2, 3):
            spread_tokens(slot, step).wait_send()
    share_info().wait_send()
    for to_mate, hop in shrunk_hops:
        share_shrunk(to_mate, hop).wait_send()
    for pair in range(2):
        for which in range(2):
            share_attended(which, pair).wait_send()
    for phase in range(2):
        for chunk in range(chunks):
            for which in range(2):
                core_copy(phase, which, chunk).wait_send()
                x_copy(phase, which, chunk).wait_send()
            z_copy(phase, chunk).wait_send()


def fused_layer(
    tokens, segment, request_position, in_use, slots, gain,
    query_weight, key_weight, value_weight, output_weight, down, up,
):
    bf16, f32 = jnp.bfloat16, jnp.float32
    rows, width = tokens.shape
    chunks = 2
    piece = rows // chunks
    hbm = pl.BlockSpec(memory_space=pltpu.HBM)
    dma = pltpu.SemaphoreType.DMA
    return pl.pallas_call(
        layer_kernel,
        out_shape=jax.ShapeDtypeStruct((rows, 512), bf16),
        in_specs=[hbm] * 13,
        out_specs=pl.BlockSpec(memory_space=pltpu.VMEM),
        scratch_shapes=[
            pltpu.VMEM(segment.shape, jnp.int32),
            pltpu.SMEM(request_position.shape, jnp.int32),
            pltpu.SMEM(in_use.shape, jnp.int32),
            pltpu.SMEM(slots.shape, jnp.int32),
            pltpu.VMEM((16, 128), bf16),
            pltpu.VMEM((2, REACH, 256), bf16),
            dma((6,)),
            pltpu.VMEM((rows, width), bf16),
            pltpu.VMEM((2, rows, width), bf16),
            pltpu.VMEM((2, 8, rows), f32),
            pltpu.VMEM((2, rows, 3 * SPAN), f32),
            pltpu.VMEM((2, rows, 256), f32),
            pltpu.VMEM((8, RANK, 1024), bf16),
            pltpu.VMEM((6, 8, 256, 128), bf16),
            pltpu.VMEM((8, 64, 256), bf16),
            pltpu.VMEM((8, 512, 128), bf16),
            pltpu.VMEM((8, RANK, 2 * rows), bf16),
            pltpu.VMEM((2, 2, rows, 256), bf16),
            pltpu.VMEM((2, 2, rows, 128), bf16),
            pltpu.VMEM((2, 2, rows, 128), bf16),
            pltpu.VMEM((2, 2, rows, 128), bf16),
            pltpu.VMEM((2, 2, 2, rows, 128), bf16),
            pltpu.VMEM((2, 2, chunks, 2, piece, 128), bf16),
            pltpu.VMEM((2, 2, chunks, 2, piece, 128), bf16),
            pltpu.VMEM((2, 2, chunks, piece, 128), bf16),
            pltpu.VMEM((2, 2, chunks, piece, 128), bf16),
            pltpu.VMEM((2, 2, chunks, piece, 128), f32),
            pltpu.VMEM((2, chunks, piece, 128), bf16),
            pltpu.VMEM((2, chunks, piece, 128), bf16),
            dma((4,)),
            dma((PIECES, 7)),
            dma((PIECES, 8)),
            dma((PIECES,)),
            dma((4, SPAN // TOKEN_ROWS)),
            dma((4, SPAN // TOKEN_ROWS)),
            dma((2,)),
            dma((8,)),
            dma((8,)),
            dma((2, 2)),
            dma((2, 2)),
            dma((2, 2, chunks)),
            dma((2, 2, chunks)),
            dma((2, 2, chunks)),
            dma((2, 2, chunks)),
            dma((2, chunks)),
            dma((2, chunks)),
        ],
        compiler_params=pltpu.CompilerParams(
            collective_id=0, has_side_effects=True, vmem_limit_bytes=56 * 1024 * 1024
        ),
    )(
        tokens, segment, request_position, in_use, slots, gain.reshape(16, 128),
        jnp.asarray(rotation_tables()),
        down.reshape(-1, width), query_weight, key_weight, value_weight,
        up.reshape(-1, up.shape[3]), output_weight,
    )


def active_rows(stored, active_slots):
    slot_total = stored.shape[0]
    held = lax.axis_index("req") * slot_total + jnp.arange(slot_total, dtype=jnp.int32)
    chosen = (active_slots[:, None] == held[None, :]).astype(stored.dtype)
    rows = jnp.einsum(
        "as,srd->ard", chosen, stored, preferred_element_type=jnp.float32
    ).astype(stored.dtype)
    return lax.psum(rows, "req").reshape(-1, stored.shape[2])


def positions_of(segment):
    ordinal = jnp.arange(segment.shape[0], dtype=jnp.int32)
    before = segment[None, :] < segment[:, None]
    return ordinal - jnp.sum(before.astype(jnp.int32), axis=1)


def apply_rotation(values, token_positions):
    half_dim = HEAD_WIDTH // 2
    frequency = rope_base ** (-(jnp.arange(half_dim, dtype=jnp.float32) * 2.0 / HEAD_WIDTH))
    angles = token_positions.astype(jnp.float32)[:, None] * frequency[None, :]
    cosine = jnp.cos(angles)[:, None, :]
    sine_part = jnp.sin(angles)[:, None, :]
    first_half = values[..., :half_dim]
    second_half = values[..., half_dim:]
    return jnp.concatenate(
        [
            first_half * cosine - second_half * sine_part,
            second_half * cosine + first_half * sine_part,
        ],
        axis=-1,
    )


def attend(query_per_head, key_heads, value_per_head, segment):
    scores = (
        jnp.einsum("qhd,khd->hqk", query_per_head, key_heads, preferred_element_type=jnp.float32)
        * 0.125
    )
    ordinal = jnp.arange(segment.shape[0], dtype=jnp.int32)
    allowed = (segment[:, None] == segment[None, :]) & (ordinal[None, :] <= ordinal[:, None])
    scores = jnp.where(allowed[None], scores, jnp.float32(-1e30))
    row_peak = jnp.max(scores, axis=-1, keepdims=True)
    exponent = jnp.where(allowed[None], jnp.exp(scores - row_peak), jnp.float32(0.0))
    weights = (exponent / jnp.sum(exponent, axis=-1, keepdims=True)).astype(jnp.bfloat16)
    return jnp.einsum(
        "hqk,khd->qhd", weights, value_per_head, preferred_element_type=jnp.float32
    ).astype(jnp.bfloat16)


def local(
    tokens,
    token_request_number,
    request_adapter_position,
    adapters_in_use,
    adapter_storage_slot,
    input_norm_gain,
    query_weight,
    key_weight,
    value_weight,
    output_weight,
    adapter_down_weight,
    adapter_up_weight,
):
    if (
        lax.axis_size("req") == 8
        and lax.axis_size("tp") == 4
        and tokens.shape == (512, 2048)
        and adapter_down_weight.shape == (2, 2, 16, 2048)
    ):
        return fused_layer(
            tokens,
            token_request_number,
            request_adapter_position,
            adapters_in_use,
            adapter_storage_slot,
            input_norm_gain,
            query_weight,
            key_weight,
            value_weight,
            output_weight,
            adapter_down_weight,
            adapter_up_weight,
        )
    row_total, model_width = tokens.shape
    local_width = query_weight.shape[1]
    reduced_rows = adapter_down_weight.shape[2]
    slot_total = adapter_down_weight.shape[0]
    segment = token_request_number[0]
    request_adapters = request_adapter_position[0]
    tp_total = lax.axis_size("tp")
    req_total = lax.axis_size("req")
    part_rows = reduced_rows // tp_total
    share = 2 * part_rows
    down_part = lax.dynamic_slice_in_dim(
        adapter_down_weight, lax.axis_index("tp") * part_rows, part_rows, 2
    ).reshape(slot_total, share, model_width)
    up_part = adapter_up_weight.reshape(slot_total, 2 * reduced_rows, local_width)
    active_slots = jnp.take(adapter_storage_slot, adapters_in_use, axis=0)
    place_total = active_slots.shape[0]
    request_places = request_adapters
    member = segment[:, None] == jnp.arange(request_adapters.shape[0], dtype=jnp.int32)[None, :]
    token_place = jnp.sum(
        jnp.where(member, request_places[None, :], jnp.zeros_like(request_places)[None, :]),
        axis=1,
    )
    column = jnp.arange(place_total * share, dtype=jnp.int32)
    mask = (token_place[:, None] == (column // share)[None, :]).astype(jnp.bfloat16)
    lanes = max(128, tp_total * share)
    fold = (lax.axis_index("tp") * share + column % share)[:, None] == jnp.arange(
        lanes, dtype=jnp.int32
    )[None, :]
    fold = fold.astype(jnp.bfloat16)
    floats = tokens.astype(jnp.float32)
    normed = (
        floats
        * lax.rsqrt(jnp.mean(floats * floats, axis=-1, keepdims=True) + norm_eps)
        * input_norm_gain.astype(jnp.float32)
    ).astype(jnp.bfloat16)
    down_all = active_rows(down_part, active_slots)
    up_all = active_rows(up_part, active_slots)
    output_full = lax.all_gather(output_weight, "req", axis=1, tiled=True)
    query_plain, key_base, value_plain = [
        jnp.dot(
            normed,
            lax.all_gather(weight, "req", axis=0, tiled=True),
            preferred_element_type=jnp.float32,
        )
        for weight in (query_weight, key_weight, value_weight)
    ]
    shrunk_all = lax.dot_general(
        normed, down_all, (((1,), (1,)), ((), ())), preferred_element_type=jnp.float32
    ).astype(jnp.bfloat16)
    shrunk = lax.psum(
        jnp.dot(shrunk_all * mask, fold, preferred_element_type=jnp.float32), "tp"
    ).astype(jnp.bfloat16)
    shrunk = shrunk[:, : tp_total * share]
    source = jnp.arange(tp_total * share, dtype=jnp.int32)
    source_kind = (source % share) // part_rows
    source_rank = (source // share) * part_rows + source % part_rows
    target = jnp.arange(place_total * reduced_rows, dtype=jnp.int32)
    mine = token_place[:, None] == (target // reduced_rows)[None, :]
    up_all = up_all.reshape(place_total, 2, reduced_rows, local_width)

    def change_of(kind):
        spread_map = (source_kind == kind)[:, None] & (
            source_rank[:, None] == (target % reduced_rows)[None, :]
        )
        spread = jnp.dot(
            shrunk, spread_map.astype(jnp.bfloat16), preferred_element_type=jnp.float32
        ).astype(jnp.bfloat16)
        spread = jnp.where(mine, spread, jnp.zeros((), jnp.bfloat16))
        return jnp.dot(
            spread,
            up_all[:, kind].reshape(place_total * reduced_rows, local_width),
            preferred_element_type=jnp.float32,
        )

    query_change = change_of(0)
    value_change = change_of(1)
    head_total = local_width // HEAD_WIDTH
    token_positions = positions_of(segment)
    query_per_head = apply_rotation(
        (query_plain + adapter_scale * query_change).reshape(row_total, head_total, HEAD_WIDTH),
        token_positions,
    ).astype(jnp.bfloat16)
    key_heads = apply_rotation(
        key_base.reshape(row_total, head_total, HEAD_WIDTH), token_positions
    ).astype(jnp.bfloat16)
    value_per_head = (
        (value_plain + adapter_scale * value_change)
        .astype(jnp.bfloat16)
        .reshape(row_total, head_total, HEAD_WIDTH)
    )
    attended = attend(query_per_head, key_heads, value_per_head, segment).reshape(
        row_total, local_width
    )
    share_width = model_width // tp_total
    residual_part = lax.dynamic_slice_in_dim(
        tokens, lax.axis_index("tp") * share_width, share_width, 1
    )
    partial_out = jnp.dot(attended, output_full, preferred_element_type=jnp.float32)
    summed = lax.psum_scatter(
        partial_out.astype(jnp.bfloat16), "tp", scatter_dimension=1, tiled=True
    ).astype(jnp.float32)
    return (summed + residual_part.astype(jnp.float32)).astype(jnp.bfloat16)


def solution(mesh):
    in_specs = (
        P("req", None),
        P("req", None),
        P("req", None),
        P(),
        P(),
        P(),
        P("req", "tp"),
        P("req", "tp"),
        P("req", "tp"),
        P("tp", "req"),
        P("req", None, None, None),
        P("req", None, None, "tp"),
    )
    out_specs = P("req", "tp")
    return jax.shard_map(local, mesh=mesh, in_specs=in_specs, out_specs=out_specs, check_vma=False)
```

```python
import functools

import jax
import jax.numpy as jnp
import numpy as np
from jax import lax
from jax.experimental import pallas as pl
from jax.experimental.pallas import tpu as pltpu
from jax.sharding import PartitionSpec as P

HEAD_WIDTH = 64


norm_eps = 1e-05
rope_base = 130000.0
adapter_scale = 2.0

MESH = pl.DeviceIdType.MESH
DOWN, QUERY_0, KEY_0, UP, VALUE_0, QUERY_1, KEY_1, VALUE_1, OUTPUT_0, OUTPUT_1 = range(10)
PIECES = 10
AHEAD = 2
TOKEN_ROWS = 32
SPAN = 128
PLACES = 16
RANK = 16
REACH = 256
FAR = 3.0e38
NEVER = -1.0e30
NT = (((1,), (1,)), ((), ()))
TN = (((0,), (0,)), ((), ()))


def rotation_tables():
    half = HEAD_WIDTH // 2
    lane = np.arange(128)
    frequency = np.float32(rope_base) ** (-(np.arange(half, dtype=np.float32) * 2.0 / HEAD_WIDTH))
    angles = np.arange(REACH, dtype=np.float32)[:, None] * frequency.astype(np.float32)[None, lane % half]
    angles = angles.astype(np.float64)
    sign = np.where(lane % HEAD_WIDTH < half, -1.0, 1.0)
    table = np.concatenate([np.cos(angles), np.sin(angles) * sign], axis=1).astype(np.float32)
    high = table.astype(jnp.bfloat16)
    low = (table - high.astype(np.float32)).astype(jnp.bfloat16)
    return np.stack([high, low])


def layer_kernel(
    tokens, segment_hbm, request_hbm, in_use_hbm, slots_hbm, gain_hbm, table_hbm,
    down, query_weight, key_weight, value_weight, up, output_weight,
    out,
    segment_in, request_position, in_use, slots, gain, table, operand_sems,
    tok, normed, info, limit, rotation,
    down_all, weight_all, up_all, output_all,
    shrunk_own, shrunk_got, shrunk_all, laid, query_heads, key_heads, value_heads, attended,
    sent_core, got_core, sent_x, got_x, kept, sent_z, got_z,
    token_sems, send_sems, recv_sems, local_sems,
    spread_send, spread_recv, info_sems, shrunk_send, shrunk_recv, attended_send, attended_recv,
    core_send, core_recv, x_send, x_recv, z_send, z_recv,
):
    me = lax.axis_index("req")
    part = lax.axis_index("tp")
    z, y = me // 2, me % 2
    x, core = part // 2, part % 2
    mine = z % 2
    other = 1 - mine
    z_mate = 2 * (z + 1 - 2 * mine) + y
    y_mate = 2 * z + 1 - y
    core_mate = 2 * x + 1 - core
    x_mate = 2 * (1 - x) + core
    weights = {
        QUERY_0: (query_weight, 0), KEY_0: (key_weight, 0), VALUE_0: (value_weight, 0),
        QUERY_1: (query_weight, 1), KEY_1: (key_weight, 1), VALUE_1: (value_weight, 1),
    }
    weight_slot = {name: slot for slot, name in enumerate(weights)}

    def piece(index, half):
        if index == DOWN:
            rows = pl.ds(pl.multiple_of(part * 16, 16), 16)
            return down.at[rows, pl.ds(pl.multiple_of(half * 1024, 1024), 1024)]
        if index == UP:
            return up.at[:, pl.ds(pl.multiple_of(half * 256, 256), 256)]
        if index in weights:
            weight, pair = weights[index]
            return weight.at[:, pl.ds(pl.multiple_of(half * 256 + pair * 128, 128), 128)]
        rows = pl.ds((index - OUTPUT_0) * 256, 256)
        return output_weight.at[rows, pl.ds(pl.multiple_of(half * 128, 128), 128)]

    def block(index, origin):
        if index == DOWN:
            return down_all.at[origin]
        if index == UP:
            return up_all.at[origin]
        if index in weights:
            return weight_all.at[weight_slot[index], origin]
        return output_all.at[origin, pl.ds((index - OUTPUT_0) * 256, 256), :]

    def remote(source, target, send, recv, req=None, tp=None):
        return pltpu.make_async_remote_copy(
            src_ref=source,
            dst_ref=target,
            send_sem=send,
            recv_sem=recv,
            device_id={
                "req": me if req is None else req,
                "tp": part if tp is None else tp,
            },
            device_id_type=MESH,
        )

    def along(index, hop):
        there = lax.rem(z + hop, 4)
        return remote(
            piece(index, there % 2),
            block(index, me),
            send_sems.at[index, hop],
            recv_sems.at[index, me],
            req=2 * there + y,
        )

    def across(index):
        return remote(
            piece(index, mine),
            block(index, me),
            send_sems.at[index, 0],
            recv_sems.at[index, me],
            req=y_mate,
        )

    def onward(index, hop):
        origin = 2 * lax.rem(z + hop, 4) + y
        held = block(index, origin)
        return remote(
            held, held, send_sems.at[index, 3 + hop], recv_sems.at[index, origin], req=y_mate
        )

    def keep(index):
        return pltpu.make_async_copy(piece(index, mine), block(index, me), local_sems.at[index])

    def arrived(index, origin):
        held = block(index, origin)
        remote(
            held, held, send_sems.at[index, 0], recv_sems.at[index, origin], req=y_mate
        ).wait_recv()

    def pump(index, hops=(1, 3, 2)):
        for hop in hops:
            arrived(index, 2 * lax.rem(z + hop, 4) + y)
            onward(index, hop).start()
            if index + AHEAD < PIECES:
                along(index + AHEAD, hop).start()

    def complete(index):
        for hop in (0, 1, 3, 2):
            arrived(index, 2 * lax.rem(z + hop, 4) + 1 - y)
        keep(index).wait()

    def load_tokens(quarter):
        rows = pl.ds(pl.multiple_of(quarter * SPAN, SPAN), SPAN)
        return pltpu.make_async_copy(tokens.at[rows, :], tok.at[rows, :], token_sems.at[quarter])

    def quarters(which, quarter):
        return normed.at[which, pl.ds(pl.multiple_of(quarter * SPAN, SPAN), SPAN), :]

    def token_rows(which, quarter, step):
        first = quarter * SPAN + step * TOKEN_ROWS
        return normed.at[which, pl.ds(pl.multiple_of(first, TOKEN_ROWS), TOKEN_ROWS), :]

    def share_tokens(step):
        held = token_rows(mine, part, step)
        return remote(
            held, held, spread_send.at[0, step], spread_recv.at[part, step], req=z_mate
        )

    def spread_tokens(slot, step):
        quarter = x_mate if slot == 3 else part
        held = token_rows(other, quarter, step)
        return remote(
            held, held, spread_send.at[slot, step], spread_recv.at[quarter, step],
            tp=x_mate if slot == 1 else core_mate,
        )

    def tokens_arrived(quarter, step):
        held = token_rows(other, quarter, step)
        remote(
            held, held, spread_send.at[0, step], spread_recv.at[quarter, step], req=z_mate
        ).wait_recv()

    def spread(step):
        tokens_arrived(part, step)
        spread_tokens(1, step).start()
        spread_tokens(2, step).start()

    def pass_tokens(step):
        tokens_arrived(x_mate, step)
        spread_tokens(3, step).start()

    def share_info():
        held = info.at[mine]
        return remote(held, held, info_sems.at[0], info_sems.at[1], req=z_mate)

    def share_shrunk(step):
        source = shrunk_all.at[core] if step == 2 else shrunk_own.at[step]
        target = shrunk_all.at[core] if step == 2 else shrunk_got.at[step]
        return remote(
            source, target, shrunk_send.at[step], shrunk_recv.at[step],
            req=z_mate if step == 1 else me,
            tp=(x_mate, part, core_mate)[step],
        )

    def add_shrunk(step):
        share_shrunk(step).wait_recv()
        total = shrunk_own[step].astype(jnp.float32) + shrunk_got[step].astype(jnp.float32)
        if step == 0:
            shrunk_own[1] = total.astype(jnp.bfloat16)
        else:
            shrunk_all[core] = total.astype(jnp.bfloat16)
        share_shrunk(step + 1).start()

    operands = [
        pltpu.make_async_copy(source, target, operand_sems.at[number])
        for number, (source, target) in enumerate(
            [
                (gain_hbm, gain), (segment_hbm, segment_in), (request_hbm, request_position),
                (in_use_hbm, in_use), (slots_hbm, slots), (table_hbm, table),
            ]
        )
    ]
    load_tokens(part).start()
    for operand in operands:
        operand.start()
    for step in range(1, 4):
        load_tokens(lax.rem(part + step, 4)).start()

    barrier = pltpu.get_barrier_semaphore()

    def greet(req, tp):
        pl.semaphore_signal(
            barrier, inc=1, device_id={"req": req, "tp": tp}, device_id_type=MESH
        )

    for hop in (1, 2, 3):
        greet(2 * lax.rem(z + hop, 4) + y, part)
    greet(y_mate, part)
    greet(me, core_mate)
    greet(me, x_mate)
    pl.semaphore_wait(barrier, 6)

    for index in range(AHEAD):
        for hop in (1, 3, 2):
            along(index, hop).start()
    for index in range(PIECES):
        across(index).start()

    operands[0].wait()
    gains = jnp.concatenate([gain[i : i + 1, :] for i in range(16)], axis=1).astype(jnp.float32)

    def normalise(quarter):
        load_tokens(quarter).wait()

        def some(step, carry):
            rows = pl.ds(pl.multiple_of(quarter * SPAN + step * 32, 32), 32)
            floats = tok[rows, :].astype(jnp.float32)
            mean = jnp.mean(floats * floats, axis=-1, keepdims=True)
            normed[mine, rows, :] = (floats * lax.rsqrt(mean + norm_eps) * gains).astype(
                jnp.bfloat16
            )
            return carry

        lax.fori_loop(0, SPAN // 32, some, 0)

    def prepare(which):
        facts = info[which]
        columns = facts.T
        for block in range(4):
            first = max(0, block - 2) * SPAN
            width = min(block + 1, 3) * SPAN
            query_segment = columns[block * SPAN : (block + 1) * SPAN, 0:1]
            key_segment = facts[0:1, first : first + width]
            query_order = block * SPAN + lax.broadcasted_iota(jnp.int32, (SPAN, width), 0)
            key_order = first + lax.broadcasted_iota(jnp.int32, (SPAN, width), 1)
            allowed = (query_segment == key_segment) & (key_order <= query_order)
            limit[which, pl.ds(block * SPAN, SPAN), pl.ds(0, width)] = jnp.where(
                allowed, FAR, NEVER
            )
        lane = lax.broadcasted_iota(jnp.int32, (4 * SPAN, REACH), 1).astype(jnp.float32)
        chosen = jnp.where(columns[:, 2:3] == lane, 1.0, 0.0).astype(jnp.bfloat16)
        rotation[which] = jnp.dot(
            chosen, table[0], preferred_element_type=jnp.float32
        ) + jnp.dot(chosen, table[1], preferred_element_type=jnp.float32)

    def shrink(which):
        columns = pl.ds(pl.multiple_of(mine * 1024, 1024), 1024)
        product = lax.dot_general(
            down_all[...].reshape(8 * RANK, 1024),
            normed[which, :, columns],
            NT,
            preferred_element_type=jnp.float32,
        )
        places = info[which][1:2, :]
        total = jnp.zeros((RANK, product.shape[1]), jnp.float32)
        for origin in range(8):
            wanted = (2 * origin + x).astype(jnp.float32)
            total = total + jnp.where(
                places == wanted, product[origin * RANK : (origin + 1) * RANK], 0.0
            )
        at = pl.ds(pl.multiple_of(which * 512, 512), 512)
        shrunk_own[0, :, at] = total.astype(jnp.bfloat16)

    def projected(which, index):
        return jnp.dot(
            normed[which],
            weight_all[weight_slot[index]].reshape(8 * 256, 128),
            preferred_element_type=jnp.float32,
        )

    def lay(which, kind):
        columns = info[which].T
        at = pl.ds(pl.multiple_of(which * 512, 512), 512)
        compact = shrunk_all[kind, :, at].astype(jnp.float32)
        padded = jnp.concatenate(
            [compact, jnp.zeros((128 - RANK, compact.shape[1]), jnp.float32)], axis=0
        ).T
        lane = lax.broadcasted_iota(jnp.int32, (128, PLACES * RANK), 1)
        row = lax.broadcasted_iota(jnp.int32, (128, PLACES * RANK), 0)
        tile = jnp.where(lane % RANK == row, 1.0, 0.0).astype(jnp.bfloat16)
        tiled = jnp.dot(
            padded.astype(jnp.bfloat16), tile, preferred_element_type=jnp.float32
        )
        lanes = lax.broadcasted_iota(jnp.int32, tiled.shape, 1) // RANK
        laid[which, kind] = jnp.where(
            columns[:, 1:2] == lanes.astype(jnp.float32), tiled, 0.0
        ).astype(jnp.bfloat16)

    def change(which, kind, pair):
        ups = up_all[:, :, pl.ds(pair * 128, 128)].reshape(8, 2, 2, RANK, 128)
        return adapter_scale * jnp.dot(
            laid[which, kind],
            ups[:, :, kind].reshape(PLACES * RANK, 128),
            preferred_element_type=jnp.float32,
        )

    def rotated(which, value):
        half = HEAD_WIDTH // 2
        low = lax.broadcasted_iota(jnp.int32, (512, 128), 1) % HEAD_WIDTH < half
        swapped = jnp.where(low, pltpu.roll(value, 128 - half, 1), pltpu.roll(value, half, 1))
        return value * rotation[which, :, 0:128] + swapped * rotation[which, :, 128:256]

    def make_key(pair, which):
        key = projected(which, KEY_1 if pair else KEY_0)
        key_heads[which, pair] = rotated(which, key).astype(jnp.bfloat16)

    def make_query(pair, which):
        query = projected(which, QUERY_1 if pair else QUERY_0) + change(which, 0, pair)
        query_heads[which, pair] = (rotated(which, query) * 0.125).astype(jnp.bfloat16)

    def make_value(pair, which):
        value = projected(which, VALUE_1 if pair else VALUE_0) + change(which, 1, pair)
        value_heads[which, pair] = value.astype(jnp.bfloat16)

    def share_attended(which, pair):
        held = attended.at[mine, pair, which]
        return remote(
            held, held, attended_send.at[pair, which], attended_recv.at[pair, which], req=z_mate
        )

    def attend(which, pair):
        left = lax.broadcasted_iota(jnp.int32, (SPAN, 128), 1) < HEAD_WIDTH
        spans = [(max(0, number - 2) * SPAN, min(number + 1, 3) * SPAN) for number in range(4)]
        rows = [pl.ds(number * SPAN, SPAN) for number in range(4)]
        scores = []
        for number, (first, width) in enumerate(spans):
            query = query_heads[which, pair, rows[number], :]
            zero = jnp.zeros_like(query)
            both = jnp.concatenate(
                [jnp.where(left, query, zero), jnp.where(left, zero, query)], axis=0
            )
            keys = key_heads[which, pair, pl.ds(first, width), :]
            score = lax.dot_general(both, keys, NT, preferred_element_type=jnp.float32)
            bound = limit[which, rows[number], pl.ds(0, width)]
            scores.append(jnp.minimum(score, jnp.concatenate([bound, bound], axis=0)))
        exponents = [
            jnp.exp(score - jnp.max(score, axis=-1, keepdims=True)).astype(jnp.bfloat16)
            for score in scores
        ]
        results = []
        for (first, width), exponent in zip(spans, exponents):
            values = value_heads[which, pair, pl.ds(first, width), :]
            wide = jnp.concatenate([values, jnp.ones_like(values)], axis=1)
            results.append(jnp.dot(exponent, wide, preferred_element_type=jnp.float32))
        for number, result in enumerate(results):
            divided = result[:, 0:128] / result[:, 128:256]
            attended[mine, pair, which, rows[number], :] = jnp.where(
                left, divided[0:SPAN], divided[SPAN : 2 * SPAN]
            ).astype(jnp.bfloat16)
        share_attended(which, pair).start()

    def lay_all(which, carry):
        lay(which, 0)
        lay(which, 1)
        return carry

    normalise(part)
    for step in range(2):
        share_tokens(step).start()
    for operand in operands[1:]:
        operand.wait()
    segment = segment_in[...].astype(jnp.float32)
    ordinal = lax.broadcasted_iota(jnp.int32, segment.shape, 1).astype(jnp.float32)
    place = jnp.zeros_like(segment)
    start = jnp.zeros_like(segment)
    for request in range(request_position.shape[1]):
        slot = slots[in_use[request_position[0, request]]]
        here = segment == float(request)
        place = jnp.where(here, slot.astype(jnp.float32), place)
        before = jnp.sum(jnp.where(segment < float(request), 1.0, 0.0), axis=1, keepdims=True)
        start = jnp.where(here, before, start)
    info[mine] = jnp.concatenate(
        [segment, place, ordinal - start, jnp.zeros((5, segment.shape[1]), jnp.float32)], axis=0
    )
    share_info().start()
    for index in range(PIECES):
        keep(index).start()
    normalise(lax.rem(part + 1, 4))
    pump(DOWN)
    share_tokens(2).start()
    normalise(lax.rem(part + 2, 4))
    pump(QUERY_0, (1, 3))
    normalise(lax.rem(part + 3, 4))
    pump(QUERY_0, (2,))
    share_tokens(3).start()
    spread(0)
    prepare(mine)
    pump(KEY_0)
    spread(1)
    share_info().wait_recv()
    prepare(other)
    pump(UP)
    spread(2)
    pass_tokens(0)
    complete(DOWN)
    shrink(mine)
    pump(VALUE_0, (1, 3))
    spread(3)
    pass_tokens(1)
    pump(VALUE_0, (2,))
    complete(KEY_0)
    make_key(0, mine)
    pass_tokens(2)
    pass_tokens(3)
    pump(QUERY_1, (1, 3))
    for step in range(SPAN // TOKEN_ROWS):
        tokens_arrived(core_mate, step)
        tokens_arrived(2 * (1 - x) + 1 - core, step)
    shrink(other)
    share_shrunk(0).start()
    pump(QUERY_1, (2,))
    make_key(0, other)
    add_shrunk(0)
    complete(QUERY_0)
    complete(UP)
    add_shrunk(1)
    pump(KEY_1, (1,))
    share_shrunk(2).wait_recv()
    lax.fori_loop(0, 2, lay_all, 0)
    pump(KEY_1, (3, 2))
    make_query(0, other)
    make_query(0, mine)
    complete(VALUE_0)
    make_value(0, other)
    pump(VALUE_1, (1,))
    make_value(0, mine)
    attend(other, 0)
    pump(VALUE_1, (3, 2))
    complete(QUERY_1)
    make_query(1, other)
    make_query(1, mine)
    attend(mine, 0)
    pump(OUTPUT_0, (1,))
    complete(KEY_1)
    make_key(1, other)
    make_key(1, mine)
    pump(OUTPUT_0, (3,))
    complete(VALUE_1)
    make_value(1, other)
    attend(other, 1)
    pump(OUTPUT_0, (2,))
    make_value(1, mine)
    attend(mine, 1)
    pump(OUTPUT_1)
    keep(OUTPUT_0).wait()
    keep(OUTPUT_1).wait()

    chunks = sent_core.shape[2]
    rows_of = sent_core.shape[4]

    for pair in range(2):
        for which in range(2):
            held = attended.at[other, pair, which]
            remote(
                held, held, attended_send.at[pair, which], attended_recv.at[pair, which],
                req=z_mate,
            ).wait_recv()

    def rows_at(chunk):
        return pl.ds(pl.multiple_of(chunk * rows_of, rows_of), rows_of)

    def product(side, to_core, which, chunk):
        heads = jnp.concatenate(
            [attended[z_of, pair, which, rows_at(chunk), :] for z_of in range(2) for pair in range(2)],
            axis=1,
        )
        columns = jnp.concatenate(
            [output_all[2 * (2 * x_of + to_core) + side] for x_of in range(2)], axis=1
        )
        return jnp.dot(heads, columns, preferred_element_type=jnp.float32)

    def core_copy(phase, which, chunk):
        return remote(
            sent_core.at[phase, which, chunk], got_core.at[phase, which, chunk],
            core_send.at[phase, which, chunk], core_recv.at[phase, which, chunk], tp=core_mate,
        )

    def x_copy(phase, which, chunk):
        return remote(
            sent_x.at[phase, which, chunk], got_x.at[phase, which, chunk],
            x_send.at[phase, which, chunk], x_recv.at[phase, which, chunk], tp=x_mate,
        )

    def z_copy(phase, chunk):
        return remote(
            sent_z.at[phase, chunk], got_z.at[phase, chunk],
            z_send.at[phase, chunk], z_recv.at[phase, chunk], req=z_mate,
        )

    def write(side, half, chunk, values):
        first = side * 256 + half * 128
        residual = tok[rows_at(chunk), pl.ds(pl.multiple_of(part * 512 + first, 128), 128)]
        out[rows_at(chunk), pl.ds(pl.multiple_of(first, 128), 128)] = (
            values + residual.astype(jnp.float32)
        ).astype(jnp.bfloat16)

    for phase in range(2):
        side = y if phase == 0 else 1 - y
        if phase == 1:
            for hop in (0, 1, 3, 2):
                arrived(OUTPUT_0, 2 * lax.rem(z + hop, 4) + 1 - y)
                arrived(OUTPUT_1, 2 * lax.rem(z + hop, 4) + 1 - y)
        for which in (other, mine):

            def first(chunk, carry):
                share = product(side, 1 - core, which, chunk)
                for x_of in range(2):
                    sent_core[phase, which, chunk, x_of] = share[
                        :, x_of * 128 : (x_of + 1) * 128
                    ].astype(jnp.bfloat16)
                core_copy(phase, which, chunk).start()
                return carry

            lax.fori_loop(0, chunks, first, 0)
        for which in (other, mine):

            def second(chunk, carry):
                share = product(side, core, which, chunk)
                core_copy(phase, which, chunk).wait_recv()
                got = got_core[phase, which, chunk].astype(jnp.float32)
                totals = [share[:, 0:128] + got[0], share[:, 128:256] + got[1]]
                first_x = x == 0
                sent_x[phase, which, chunk] = jnp.where(first_x, totals[1], totals[0]).astype(
                    jnp.bfloat16
                )
                x_copy(phase, which, chunk).start()
                kept[phase, which, chunk] = jnp.where(first_x, totals[0], totals[1])
                return carry

            lax.fori_loop(0, chunks, second, 0)

    for phase in range(2):
        side = y if phase == 0 else 1 - y

        def third(chunk, carry):
            x_copy(phase, other, chunk).wait_recv()
            sent_z[phase, chunk] = (
                kept[phase, other, chunk] + got_x[phase, other, chunk].astype(jnp.float32)
            ).astype(jnp.bfloat16)
            z_copy(phase, chunk).start()
            return carry

        lax.fori_loop(0, chunks, third, 0)

    for phase in range(2):
        side = y if phase == 0 else 1 - y

        def own(chunk, carry):
            x_copy(phase, mine, chunk).wait_recv()
            write(
                side, mine, chunk,
                kept[phase, mine, chunk] + got_x[phase, mine, chunk].astype(jnp.float32),
            )
            return carry

        lax.fori_loop(0, chunks, own, 0)

    for phase in range(2):
        side = y if phase == 0 else 1 - y

        def returned(chunk, carry):
            z_copy(phase, chunk).wait_recv()
            write(side, other, chunk, got_z[phase, chunk].astype(jnp.float32))
            return carry

        lax.fori_loop(0, chunks, returned, 0)

    for index in range(PIECES):
        for hop in (1, 2, 3):
            along(index, hop).wait_send()
            onward(index, hop).wait_send()
        across(index).wait_send()
    for step in range(SPAN // TOKEN_ROWS):
        share_tokens(step).wait_send()
        for slot in (1, 2, 3):
            spread_tokens(slot, step).wait_send()
    share_info().wait_send()
    for step in range(3):
        share_shrunk(step).wait_send()
    for pair in range(2):
        for which in range(2):
            share_attended(which, pair).wait_send()
    for phase in range(2):
        for chunk in range(chunks):
            for which in range(2):
                core_copy(phase, which, chunk).wait_send()
                x_copy(phase, which, chunk).wait_send()
            z_copy(phase, chunk).wait_send()


def fused_layer(
    tokens, segment, request_position, in_use, slots, gain,
    query_weight, key_weight, value_weight, output_weight, down, up,
):
    bf16, f32 = jnp.bfloat16, jnp.float32
    rows, width = tokens.shape
    chunks = 2
    piece = rows // chunks
    hbm = pl.BlockSpec(memory_space=pltpu.HBM)
    dma = pltpu.SemaphoreType.DMA
    return pl.pallas_call(
        layer_kernel,
        out_shape=jax.ShapeDtypeStruct((rows, 512), bf16),
        in_specs=[hbm] * 13,
        out_specs=pl.BlockSpec(memory_space=pltpu.VMEM),
        scratch_shapes=[
            pltpu.VMEM(segment.shape, jnp.int32),
            pltpu.SMEM(request_position.shape, jnp.int32),
            pltpu.SMEM(in_use.shape, jnp.int32),
            pltpu.SMEM(slots.shape, jnp.int32),
            pltpu.VMEM((16, 128), bf16),
            pltpu.VMEM((2, REACH, 256), bf16),
            dma((6,)),
            pltpu.VMEM((rows, width), bf16),
            pltpu.VMEM((2, rows, width), bf16),
            pltpu.VMEM((2, 8, rows), f32),
            pltpu.VMEM((2, rows, 3 * SPAN), f32),
            pltpu.VMEM((2, rows, 256), f32),
            pltpu.VMEM((8, RANK, 1024), bf16),
            pltpu.VMEM((6, 8, 256, 128), bf16),
            pltpu.VMEM((8, 64, 256), bf16),
            pltpu.VMEM((8, 512, 128), bf16),
            pltpu.VMEM((2, RANK, 2 * rows), bf16),
            pltpu.VMEM((2, RANK, 2 * rows), bf16),
            pltpu.VMEM((2, RANK, 2 * rows), bf16),
            pltpu.VMEM((2, 2, rows, 256), bf16),
            pltpu.VMEM((2, 2, rows, 128), bf16),
            pltpu.VMEM((2, 2, rows, 128), bf16),
            pltpu.VMEM((2, 2, rows, 128), bf16),
            pltpu.VMEM((2, 2, 2, rows, 128), bf16),
            pltpu.VMEM((2, 2, chunks, 2, piece, 128), bf16),
            pltpu.VMEM((2, 2, chunks, 2, piece, 128), bf16),
            pltpu.VMEM((2, 2, chunks, piece, 128), bf16),
            pltpu.VMEM((2, 2, chunks, piece, 128), bf16),
            pltpu.VMEM((2, 2, chunks, piece, 128), f32),
            pltpu.VMEM((2, chunks, piece, 128), bf16),
            pltpu.VMEM((2, chunks, piece, 128), bf16),
            dma((4,)),
            dma((PIECES, 7)),
            dma((PIECES, 8)),
            dma((PIECES,)),
            dma((4, SPAN // TOKEN_ROWS)),
            dma((4, SPAN // TOKEN_ROWS)),
            dma((2,)),
            dma((3,)),
            dma((3,)),
            dma((2, 2)),
            dma((2, 2)),
            dma((2, 2, chunks)),
            dma((2, 2, chunks)),
            dma((2, 2, chunks)),
            dma((2, 2, chunks)),
            dma((2, chunks)),
            dma((2, chunks)),
        ],
        compiler_params=pltpu.CompilerParams(
            collective_id=0, has_side_effects=True, vmem_limit_bytes=56 * 1024 * 1024
        ),
    )(
        tokens, segment, request_position, in_use, slots, gain.reshape(16, 128),
        jnp.asarray(rotation_tables()),
        down.reshape(-1, width), query_weight, key_weight, value_weight,
        up.reshape(-1, up.shape[3]), output_weight,
    )


def active_rows(stored, active_slots):
    slot_total = stored.shape[0]
    held = lax.axis_index("req") * slot_total + jnp.arange(slot_total, dtype=jnp.int32)
    chosen = (active_slots[:, None] == held[None, :]).astype(stored.dtype)
    rows = jnp.einsum(
        "as,srd->ard", chosen, stored, preferred_element_type=jnp.float32
    ).astype(stored.dtype)
    return lax.psum(rows, "req").reshape(-1, stored.shape[2])


def positions_of(segment):
    ordinal = jnp.arange(segment.shape[0], dtype=jnp.int32)
    before = segment[None, :] < segment[:, None]
    return ordinal - jnp.sum(before.astype(jnp.int32), axis=1)


def apply_rotation(values, token_positions):
    half_dim = HEAD_WIDTH // 2
    frequency = rope_base ** (-(jnp.arange(half_dim, dtype=jnp.float32) * 2.0 / HEAD_WIDTH))
    angles = token_positions.astype(jnp.float32)[:, None] * frequency[None, :]
    cosine = jnp.cos(angles)[:, None, :]
    sine_part = jnp.sin(angles)[:, None, :]
    first_half = values[..., :half_dim]
    second_half = values[..., half_dim:]
    return jnp.concatenate(
        [
            first_half * cosine - second_half * sine_part,
            second_half * cosine + first_half * sine_part,
        ],
        axis=-1,
    )


def attend(query_per_head, key_heads, value_per_head, segment):
    scores = (
        jnp.einsum("qhd,khd->hqk", query_per_head, key_heads, preferred_element_type=jnp.float32)
        * 0.125
    )
    ordinal = jnp.arange(segment.shape[0], dtype=jnp.int32)
    allowed = (segment[:, None] == segment[None, :]) & (ordinal[None, :] <= ordinal[:, None])
    scores = jnp.where(allowed[None], scores, jnp.float32(-1e30))
    row_peak = jnp.max(scores, axis=-1, keepdims=True)
    exponent = jnp.where(allowed[None], jnp.exp(scores - row_peak), jnp.float32(0.0))
    weights = (exponent / jnp.sum(exponent, axis=-1, keepdims=True)).astype(jnp.bfloat16)
    return jnp.einsum(
        "hqk,khd->qhd", weights, value_per_head, preferred_element_type=jnp.float32
    ).astype(jnp.bfloat16)


def local(
    tokens,
    token_request_number,
    request_adapter_position,
    adapters_in_use,
    adapter_storage_slot,
    input_norm_gain,
    query_weight,
    key_weight,
    value_weight,
    output_weight,
    adapter_down_weight,
    adapter_up_weight,
):
    if (
        lax.axis_size("req") == 8
        and lax.axis_size("tp") == 4
        and tokens.shape == (512, 2048)
        and adapter_down_weight.shape == (2, 2, 16, 2048)
    ):
        return fused_layer(
            tokens,
            token_request_number,
            request_adapter_position,
            adapters_in_use,
            adapter_storage_slot,
            input_norm_gain,
            query_weight,
            key_weight,
            value_weight,
            output_weight,
            adapter_down_weight,
            adapter_up_weight,
        )
    row_total, model_width = tokens.shape
    local_width = query_weight.shape[1]
    reduced_rows = adapter_down_weight.shape[2]
    slot_total = adapter_down_weight.shape[0]
    segment = token_request_number[0]
    request_adapters = request_adapter_position[0]
    tp_total = lax.axis_size("tp")
    req_total = lax.axis_size("req")
    part_rows = reduced_rows // tp_total
    share = 2 * part_rows
    down_part = lax.dynamic_slice_in_dim(
        adapter_down_weight, lax.axis_index("tp") * part_rows, part_rows, 2
    ).reshape(slot_total, share, model_width)
    up_part = adapter_up_weight.reshape(slot_total, 2 * reduced_rows, local_width)
    active_slots = jnp.take(adapter_storage_slot, adapters_in_use, axis=0)
    place_total = active_slots.shape[0]
    request_places = request_adapters
    member = segment[:, None] == jnp.arange(request_adapters.shape[0], dtype=jnp.int32)[None, :]
    token_place = jnp.sum(
        jnp.where(member, request_places[None, :], jnp.zeros_like(request_places)[None, :]),
        axis=1,
    )
    column = jnp.arange(place_total * share, dtype=jnp.int32)
    mask = (token_place[:, None] == (column // share)[None, :]).astype(jnp.bfloat16)
    lanes = max(128, tp_total * share)
    fold = (lax.axis_index("tp") * share + column % share)[:, None] == jnp.arange(
        lanes, dtype=jnp.int32
    )[None, :]
    fold = fold.astype(jnp.bfloat16)
    floats = tokens.astype(jnp.float32)
    normed = (
        floats
        * lax.rsqrt(jnp.mean(floats * floats, axis=-1, keepdims=True) + norm_eps)
        * input_norm_gain.astype(jnp.float32)
    ).astype(jnp.bfloat16)
    down_all = active_rows(down_part, active_slots)
    up_all = active_rows(up_part, active_slots)
    output_full = lax.all_gather(output_weight, "req", axis=1, tiled=True)
    query_plain, key_base, value_plain = [
        jnp.dot(
            normed,
            lax.all_gather(weight, "req", axis=0, tiled=True),
            preferred_element_type=jnp.float32,
        )
        for weight in (query_weight, key_weight, value_weight)
    ]
    shrunk_all = lax.dot_general(
        normed, down_all, (((1,), (1,)), ((), ())), preferred_element_type=jnp.float32
    ).astype(jnp.bfloat16)
    shrunk = lax.psum(
        jnp.dot(shrunk_all * mask, fold, preferred_element_type=jnp.float32), "tp"
    ).astype(jnp.bfloat16)
    shrunk = shrunk[:, : tp_total * share]
    source = jnp.arange(tp_total * share, dtype=jnp.int32)
    source_kind = (source % share) // part_rows
    source_rank = (source // share) * part_rows + source % part_rows
    target = jnp.arange(place_total * reduced_rows, dtype=jnp.int32)
    mine = token_place[:, None] == (target // reduced_rows)[None, :]
    up_all = up_all.reshape(place_total, 2, reduced_rows, local_width)

    def change_of(kind):
        spread_map = (source_kind == kind)[:, None] & (
            source_rank[:, None] == (target % reduced_rows)[None, :]
        )
        spread = jnp.dot(
            shrunk, spread_map.astype(jnp.bfloat16), preferred_element_type=jnp.float32
        ).astype(jnp.bfloat16)
        spread = jnp.where(mine, spread, jnp.zeros((), jnp.bfloat16))
        return jnp.dot(
            spread,
            up_all[:, kind].reshape(place_total * reduced_rows, local_width),
            preferred_element_type=jnp.float32,
        )

    query_change = change_of(0)
    value_change = change_of(1)
    head_total = local_width // HEAD_WIDTH
    token_positions = positions_of(segment)
    query_per_head = apply_rotation(
        (query_plain + adapter_scale * query_change).reshape(row_total, head_total, HEAD_WIDTH),
        token_positions,
    ).astype(jnp.bfloat16)
    key_heads = apply_rotation(
        key_base.reshape(row_total, head_total, HEAD_WIDTH), token_positions
    ).astype(jnp.bfloat16)
    value_per_head = (
        (value_plain + adapter_scale * value_change)
        .astype(jnp.bfloat16)
        .reshape(row_total, head_total, HEAD_WIDTH)
    )
    attended = attend(query_per_head, key_heads, value_per_head, segment).reshape(
        row_total, local_width
    )
    share_width = model_width // tp_total
    residual_part = lax.dynamic_slice_in_dim(
        tokens, lax.axis_index("tp") * share_width, share_width, 1
    )
    partial_out = jnp.dot(attended, output_full, preferred_element_type=jnp.float32)
    summed = lax.psum_scatter(
        partial_out.astype(jnp.bfloat16), "tp", scatter_dimension=1, tiled=True
    ).astype(jnp.float32)
    return (summed + residual_part.astype(jnp.float32)).astype(jnp.bfloat16)


def solution(mesh):
    in_specs = (
        P("req", None),
        P("req", None),
        P("req", None),
        P(),
        P(),
        P(),
        P("req", "tp"),
        P("req", "tp"),
        P("req", "tp"),
        P("tp", "req"),
        P("req", None, None, None),
        P("req", None, None, "tp"),
    )
    out_specs = P("req", "tp")
    return jax.shard_map(local, mesh=mesh, in_specs=in_specs, out_specs=out_specs, check_vma=False)
```

```python
import functools

import jax
import jax.numpy as jnp
import numpy as np
from jax import lax
from jax.experimental import pallas as pl
from jax.experimental.pallas import tpu as pltpu
from jax.sharding import PartitionSpec as P

HEAD_WIDTH = 64


norm_eps = 1e-05
rope_base = 130000.0
adapter_scale = 2.0

MESH = pl.DeviceIdType.MESH
DOWN, QUERY_0, KEY_0, UP, VALUE_0, QUERY_1, KEY_1, VALUE_1, OUTPUT_0, OUTPUT_1 = range(10)
PIECES = 10
AHEAD = 2
TOKEN_ROWS = 32
SPAN = 128
PLACES = 16
RANK = 16
REACH = 256
FAR = 3.0e38
NEVER = -1.0e30
NT = (((1,), (1,)), ((), ()))
TN = (((0,), (0,)), ((), ()))


def rotation_tables():
    half = HEAD_WIDTH // 2
    lane = np.arange(128)
    frequency = np.float32(rope_base) ** (-(np.arange(half, dtype=np.float32) * 2.0 / HEAD_WIDTH))
    angles = np.arange(REACH, dtype=np.float32)[:, None] * frequency.astype(np.float32)[None, lane % half]
    angles = angles.astype(np.float64)
    sign = np.where(lane % HEAD_WIDTH < half, -1.0, 1.0)
    table = np.concatenate([np.cos(angles), np.sin(angles) * sign], axis=1).astype(np.float32)
    high = table.astype(jnp.bfloat16)
    low = (table - high.astype(np.float32)).astype(jnp.bfloat16)
    return np.stack([high, low])


def layer_kernel(
    tokens, segment_hbm, request_hbm, in_use_hbm, slots_hbm, gain_hbm, table_hbm,
    down, query_weight, key_weight, value_weight, up, output_weight,
    out,
    segment_in, request_position, in_use, slots, gain, table, operand_sems,
    tok, normed, info, limit, rotation,
    down_all, weight_all, up_all, output_all,
    shrunk_own, shrunk_got, shrunk_all, laid, query_heads, key_heads, value_heads, attended,
    sent_core, got_core, sent_x, got_x, kept, sent_z, got_z,
    token_sems, send_sems, recv_sems, local_sems,
    spread_send, spread_recv, info_sems, shrunk_send, shrunk_recv, attended_send, attended_recv,
    core_send, core_recv, x_send, x_recv, z_send, z_recv,
):
    me = lax.axis_index("req")
    part = lax.axis_index("tp")
    z, y = me // 2, me % 2
    x, core = part // 2, part % 2
    mine = z % 2
    other = 1 - mine
    z_mate = 2 * (z + 1 - 2 * mine) + y
    y_mate = 2 * z + 1 - y
    near, cross = 1 + 2 * mine, 3 - 2 * mine
    real = {1: cross, 3: 2, 2: near}
    core_mate = 2 * x + 1 - core
    x_mate = 2 * (1 - x) + core
    weights = {
        QUERY_0: (query_weight, 0), KEY_0: (key_weight, 0), VALUE_0: (value_weight, 0),
        QUERY_1: (query_weight, 1), KEY_1: (key_weight, 1), VALUE_1: (value_weight, 1),
    }
    weight_slot = {name: slot for slot, name in enumerate(weights)}

    def piece(index, half):
        if index == DOWN:
            rows = pl.ds(pl.multiple_of(part * 16, 16), 16)
            return down.at[rows, pl.ds(pl.multiple_of(half * 1024, 1024), 1024)]
        if index == UP:
            return up.at[:, pl.ds(pl.multiple_of(half * 256, 256), 256)]
        if index in weights:
            weight, pair = weights[index]
            return weight.at[:, pl.ds(pl.multiple_of(half * 256 + pair * 128, 128), 128)]
        rows = pl.ds((index - OUTPUT_0) * 256, 256)
        return output_weight.at[rows, pl.ds(pl.multiple_of(half * 128, 128), 128)]

    def block(index, origin):
        if index == DOWN:
            return down_all.at[origin]
        if index == UP:
            return up_all.at[origin]
        if index in weights:
            return weight_all.at[weight_slot[index], origin]
        return output_all.at[origin, pl.ds((index - OUTPUT_0) * 256, 256), :]

    def remote(source, target, send, recv, req=None, tp=None):
        return pltpu.make_async_remote_copy(
            src_ref=source,
            dst_ref=target,
            send_sem=send,
            recv_sem=recv,
            device_id={
                "req": me if req is None else req,
                "tp": part if tp is None else tp,
            },
            device_id_type=MESH,
        )

    def along(index, hop):
        there = lax.rem(z + real[hop], 4)
        return remote(
            piece(index, there % 2),
            block(index, me),
            send_sems.at[index, hop],
            recv_sems.at[index, me],
            req=2 * there + y,
        )

    def across(index):
        return remote(
            piece(index, mine),
            block(index, me),
            send_sems.at[index, 0],
            recv_sems.at[index, me],
            req=y_mate,
        )

    def onward(index, hop):
        origin = 2 * lax.rem(z + real[hop], 4) + y
        held = block(index, origin)
        return remote(
            held, held, send_sems.at[index, 3 + hop], recv_sems.at[index, origin], req=y_mate
        )

    def keep(index):
        return pltpu.make_async_copy(piece(index, mine), block(index, me), local_sems.at[index])

    def arrived(index, origin):
        held = block(index, origin)
        remote(
            held, held, send_sems.at[index, 0], recv_sems.at[index, origin], req=y_mate
        ).wait_recv()

    def pump(index, hops=(1, 3, 2)):
        for hop in hops:
            arrived(index, 2 * lax.rem(z + real[hop], 4) + y)
            onward(index, hop).start()
            if index + AHEAD < PIECES:
                along(index + AHEAD, hop).start()

    def complete(index):
        for hop in (0, 1, 3, 2):
            arrived(index, 2 * lax.rem(z + hop, 4) + 1 - y)
        keep(index).wait()

    def load_tokens(quarter):
        rows = pl.ds(pl.multiple_of(quarter * SPAN, SPAN), SPAN)
        return pltpu.make_async_copy(tokens.at[rows, :], tok.at[rows, :], token_sems.at[quarter])

    def quarters(which, quarter):
        return normed.at[which, pl.ds(pl.multiple_of(quarter * SPAN, SPAN), SPAN), :]

    def token_rows(which, quarter, step):
        first = quarter * SPAN + step * TOKEN_ROWS
        return normed.at[which, pl.ds(pl.multiple_of(first, TOKEN_ROWS), TOKEN_ROWS), :]

    def share_tokens(step):
        held = token_rows(mine, part, step)
        return remote(
            held, held, spread_send.at[0, step], spread_recv.at[part, step], req=z_mate
        )

    def spread_tokens(slot, step):
        quarter = x_mate if slot == 3 else part
        held = token_rows(other, quarter, step)
        return remote(
            held, held, spread_send.at[slot, step], spread_recv.at[quarter, step],
            tp=x_mate if slot == 1 else core_mate,
        )

    def tokens_arrived(quarter, step):
        held = token_rows(other, quarter, step)
        remote(
            held, held, spread_send.at[0, step], spread_recv.at[quarter, step], req=z_mate
        ).wait_recv()

    def spread(step):
        tokens_arrived(part, step)
        spread_tokens(1, step).start()
        spread_tokens(2, step).start()

    def pass_tokens(step):
        tokens_arrived(x_mate, step)
        spread_tokens(3, step).start()

    def share_info():
        held = info.at[mine]
        return remote(held, held, info_sems.at[0], info_sems.at[1], req=z_mate)

    def share_shrunk(step):
        source = shrunk_all.at[core] if step == 2 else shrunk_own.at[step]
        target = shrunk_all.at[core] if step == 2 else shrunk_got.at[step]
        return remote(
            source, target, shrunk_send.at[step], shrunk_recv.at[step],
            req=z_mate if step == 1 else me,
            tp=(x_mate, part, core_mate)[step],
        )

    def add_shrunk(step):
        share_shrunk(step).wait_recv()
        total = shrunk_own[step].astype(jnp.float32) + shrunk_got[step].astype(jnp.float32)
        if step == 0:
            shrunk_own[1] = total.astype(jnp.bfloat16)
        else:
            shrunk_all[core] = total.astype(jnp.bfloat16)
        share_shrunk(step + 1).start()

    operands = [
        pltpu.make_async_copy(source, target, operand_sems.at[number])
        for number, (source, target) in enumerate(
            [
                (gain_hbm, gain), (segment_hbm, segment_in), (request_hbm, request_position),
                (in_use_hbm, in_use), (slots_hbm, slots), (table_hbm, table),
            ]
        )
    ]
    load_tokens(part).start()
    for operand in operands:
        operand.start()
    for step in range(1, 4):
        load_tokens(lax.rem(part + step, 4)).start()

    barrier = pltpu.get_barrier_semaphore()

    def greet(req, tp):
        pl.semaphore_signal(
            barrier, inc=1, device_id={"req": req, "tp": tp}, device_id_type=MESH
        )

    for hop in (1, 2, 3):
        greet(2 * lax.rem(z + hop, 4) + y, part)
    greet(y_mate, part)
    greet(me, core_mate)
    greet(me, x_mate)
    pl.semaphore_wait(barrier, 6)

    for index in range(AHEAD):
        for hop in (1, 3, 2):
            along(index, hop).start()
    for index in range(PIECES):
        across(index).start()

    operands[0].wait()
    gains = jnp.concatenate([gain[i : i + 1, :] for i in range(16)], axis=1).astype(jnp.float32)

    def normalise(quarter):
        load_tokens(quarter).wait()

        def some(step, carry):
            rows = pl.ds(pl.multiple_of(quarter * SPAN + step * 32, 32), 32)
            floats = tok[rows, :].astype(jnp.float32)
            mean = jnp.mean(floats * floats, axis=-1, keepdims=True)
            normed[mine, rows, :] = (floats * lax.rsqrt(mean + norm_eps) * gains).astype(
                jnp.bfloat16
            )
            return carry

        lax.fori_loop(0, SPAN // 32, some, 0)

    def prepare(which):
        facts = info[which]
        columns = facts.T
        for block in range(4):
            first = max(0, block - 2) * SPAN
            width = min(block + 1, 3) * SPAN
            query_segment = columns[block * SPAN : (block + 1) * SPAN, 0:1]
            key_segment = facts[0:1, first : first + width]
            query_order = block * SPAN + lax.broadcasted_iota(jnp.int32, (SPAN, width), 0)
            key_order = first + lax.broadcasted_iota(jnp.int32, (SPAN, width), 1)
            allowed = (query_segment == key_segment) & (key_order <= query_order)
            limit[which, pl.ds(block * SPAN, SPAN), pl.ds(0, width)] = jnp.where(
                allowed, FAR, NEVER
            )
        lane = lax.broadcasted_iota(jnp.int32, (4 * SPAN, REACH), 1).astype(jnp.float32)
        chosen = jnp.where(columns[:, 2:3] == lane, 1.0, 0.0).astype(jnp.bfloat16)
        rotation[which] = jnp.dot(
            chosen, table[0], preferred_element_type=jnp.float32
        ) + jnp.dot(chosen, table[1], preferred_element_type=jnp.float32)

    def shrink(which):
        columns = pl.ds(pl.multiple_of(mine * 1024, 1024), 1024)
        product = lax.dot_general(
            down_all[...].reshape(8 * RANK, 1024),
            normed[which, :, columns],
            NT,
            preferred_element_type=jnp.float32,
        )
        places = info[which][1:2, :]
        total = jnp.zeros((RANK, product.shape[1]), jnp.float32)
        for origin in range(8):
            wanted = (2 * origin + x).astype(jnp.float32)
            total = total + jnp.where(
                places == wanted, product[origin * RANK : (origin + 1) * RANK], 0.0
            )
        at = pl.ds(pl.multiple_of(which * 512, 512), 512)
        shrunk_own[0, :, at] = total.astype(jnp.bfloat16)

    def projected(which, index):
        return jnp.dot(
            normed[which],
            weight_all[weight_slot[index]].reshape(8 * 256, 128),
            preferred_element_type=jnp.float32,
        )

    def lay(which, kind):
        columns = info[which].T
        at = pl.ds(pl.multiple_of(which * 512, 512), 512)
        compact = shrunk_all[kind, :, at].astype(jnp.float32)
        padded = jnp.concatenate(
            [compact, jnp.zeros((128 - RANK, compact.shape[1]), jnp.float32)], axis=0
        ).T
        lane = lax.broadcasted_iota(jnp.int32, (128, PLACES * RANK), 1)
        row = lax.broadcasted_iota(jnp.int32, (128, PLACES * RANK), 0)
        tile = jnp.where(lane % RANK == row, 1.0, 0.0).astype(jnp.bfloat16)
        tiled = jnp.dot(
            padded.astype(jnp.bfloat16), tile, preferred_element_type=jnp.float32
        )
        lanes = lax.broadcasted_iota(jnp.int32, tiled.shape, 1) // RANK
        laid[which, kind] = jnp.where(
            columns[:, 1:2] == lanes.astype(jnp.float32), tiled, 0.0
        ).astype(jnp.bfloat16)

    def change(which, kind, pair):
        ups = up_all[:, :, pl.ds(pair * 128, 128)].reshape(8, 2, 2, RANK, 128)
        return adapter_scale * jnp.dot(
            laid[which, kind],
            ups[:, :, kind].reshape(PLACES * RANK, 128),
            preferred_element_type=jnp.float32,
        )

    def rotated(which, value):
        half = HEAD_WIDTH // 2
        low = lax.broadcasted_iota(jnp.int32, (512, 128), 1) % HEAD_WIDTH < half
        swapped = jnp.where(low, pltpu.roll(value, 128 - half, 1), pltpu.roll(value, half, 1))
        return value * rotation[which, :, 0:128] + swapped * rotation[which, :, 128:256]

    def make_key(pair, which):
        key = projected(which, KEY_1 if pair else KEY_0)
        key_heads[which, pair] = rotated(which, key).astype(jnp.bfloat16)

    def make_query(pair, which):
        query = projected(which, QUERY_1 if pair else QUERY_0) + change(which, 0, pair)
        query_heads[which, pair] = (rotated(which, query) * 0.125).astype(jnp.bfloat16)

    def make_value(pair, which):
        value = projected(which, VALUE_1 if pair else VALUE_0) + change(which, 1, pair)
        value_heads[which, pair] = value.astype(jnp.bfloat16)

    def share_attended(which, pair):
        held = attended.at[mine, pair, which]
        return remote(
            held, held, attended_send.at[pair, which], attended_recv.at[pair, which], req=z_mate
        )

    def attend(which, pair):
        left = lax.broadcasted_iota(jnp.int32, (SPAN, 128), 1) < HEAD_WIDTH
        spans = [(max(0, number - 2) * SPAN, min(number + 1, 3) * SPAN) for number in range(4)]
        rows = [pl.ds(number * SPAN, SPAN) for number in range(4)]
        scores = []
        for number, (first, width) in enumerate(spans):
            query = query_heads[which, pair, rows[number], :]
            zero = jnp.zeros_like(query)
            both = jnp.concatenate(
                [jnp.where(left, query, zero), jnp.where(left, zero, query)], axis=0
            )
            keys = key_heads[which, pair, pl.ds(first, width), :]
            score = lax.dot_general(both, keys, NT, preferred_element_type=jnp.float32)
            bound = limit[which, rows[number], pl.ds(0, width)]
            scores.append(jnp.minimum(score, jnp.concatenate([bound, bound], axis=0)))
        exponents = [
            jnp.exp(score - jnp.max(score, axis=-1, keepdims=True)).astype(jnp.bfloat16)
            for score in scores
        ]
        results = []
        for (first, width), exponent in zip(spans, exponents):
            values = value_heads[which, pair, pl.ds(first, width), :]
            wide = jnp.concatenate([values, jnp.ones_like(values)], axis=1)
            results.append(jnp.dot(exponent, wide, preferred_element_type=jnp.float32))
        for number, result in enumerate(results):
            divided = result[:, 0:128] / result[:, 128:256]
            attended[mine, pair, which, rows[number], :] = jnp.where(
                left, divided[0:SPAN], divided[SPAN : 2 * SPAN]
            ).astype(jnp.bfloat16)
        share_attended(which, pair).start()

    def lay_all(which, carry):
        lay(which, 0)
        lay(which, 1)
        return carry

    normalise(part)
    for step in range(2):
        share_tokens(step).start()
    for operand in operands[1:]:
        operand.wait()
    segment = segment_in[...].astype(jnp.float32)
    ordinal = lax.broadcasted_iota(jnp.int32, segment.shape, 1).astype(jnp.float32)
    place = jnp.zeros_like(segment)
    start = jnp.zeros_like(segment)
    for request in range(request_position.shape[1]):
        slot = slots[in_use[request_position[0, request]]]
        here = segment == float(request)
        place = jnp.where(here, slot.astype(jnp.float32), place)
        before = jnp.sum(jnp.where(segment < float(request), 1.0, 0.0), axis=1, keepdims=True)
        start = jnp.where(here, before, start)
    info[mine] = jnp.concatenate(
        [segment, place, ordinal - start, jnp.zeros((5, segment.shape[1]), jnp.float32)], axis=0
    )
    share_info().start()
    for index in range(PIECES):
        keep(index).start()
    normalise(lax.rem(part + 1, 4))
    pump(DOWN)
    share_tokens(2).start()
    normalise(lax.rem(part + 2, 4))
    pump(QUERY_0, (1, 3))
    normalise(lax.rem(part + 3, 4))
    pump(QUERY_0, (2,))
    share_tokens(3).start()
    spread(0)
    prepare(mine)
    pump(KEY_0)
    spread(1)
    share_info().wait_recv()
    prepare(other)
    pump(UP)
    spread(2)
    pass_tokens(0)
    complete(DOWN)
    shrink(mine)
    pump(VALUE_0, (1, 3))
    spread(3)
    pass_tokens(1)
    pump(VALUE_0, (2,))
    complete(KEY_0)
    make_key(0, mine)
    pass_tokens(2)
    pass_tokens(3)
    pump(QUERY_1, (1, 3))
    for step in range(SPAN // TOKEN_ROWS):
        tokens_arrived(core_mate, step)
        tokens_arrived(2 * (1 - x) + 1 - core, step)
    shrink(other)
    share_shrunk(0).start()
    pump(QUERY_1, (2,))
    make_key(0, other)
    add_shrunk(0)
    complete(QUERY_0)
    complete(UP)
    add_shrunk(1)
    pump(KEY_1, (1,))
    share_shrunk(2).wait_recv()
    lax.fori_loop(0, 2, lay_all, 0)
    pump(KEY_1, (3, 2))
    make_query(0, other)
    make_query(0, mine)
    complete(VALUE_0)
    make_value(0, other)
    pump(VALUE_1, (1,))
    make_value(0, mine)
    attend(other, 0)
    pump(VALUE_1, (3, 2))
    complete(QUERY_1)
    make_query(1, other)
    make_query(1, mine)
    attend(mine, 0)
    pump(OUTPUT_0, (1,))
    complete(KEY_1)
    make_key(1, other)
    make_key(1, mine)
    pump(OUTPUT_0, (3,))
    complete(VALUE_1)
    make_value(1, other)
    attend(other, 1)
    pump(OUTPUT_0, (2,))
    make_value(1, mine)
    attend(mine, 1)
    pump(OUTPUT_1)
    keep(OUTPUT_0).wait()
    keep(OUTPUT_1).wait()

    chunks = sent_core.shape[2]
    rows_of = sent_core.shape[4]

    for pair in range(2):
        for which in range(2):
            held = attended.at[other, pair, which]
            remote(
                held, held, attended_send.at[pair, which], attended_recv.at[pair, which],
                req=z_mate,
            ).wait_recv()

    def rows_at(chunk):
        return pl.ds(pl.multiple_of(chunk * rows_of, rows_of), rows_of)

    def product(side, to_core, which, chunk):
        heads = jnp.concatenate(
            [attended[z_of, pair, which, rows_at(chunk), :] for z_of in range(2) for pair in range(2)],
            axis=1,
        )
        columns = jnp.concatenate(
            [output_all[2 * (2 * x_of + to_core) + side] for x_of in range(2)], axis=1
        )
        return jnp.dot(heads, columns, preferred_element_type=jnp.float32)

    def core_copy(phase, which, chunk):
        return remote(
            sent_core.at[phase, which, chunk], got_core.at[phase, which, chunk],
            core_send.at[phase, which, chunk], core_recv.at[phase, which, chunk], tp=core_mate,
        )

    def x_copy(phase, which, chunk):
        return remote(
            sent_x.at[phase, which, chunk], got_x.at[phase, which, chunk],
            x_send.at[phase, which, chunk], x_recv.at[phase, which, chunk], tp=x_mate,
        )

    def z_copy(phase, chunk):
        return remote(
            sent_z.at[phase, chunk], got_z.at[phase, chunk],
            z_send.at[phase, chunk], z_recv.at[phase, chunk], req=z_mate,
        )

    def write(side, half, chunk, values):
        first = side * 256 + half * 128
        residual = tok[rows_at(chunk), pl.ds(pl.multiple_of(part * 512 + first, 128), 128)]
        out[rows_at(chunk), pl.ds(pl.multiple_of(first, 128), 128)] = (
            values + residual.astype(jnp.float32)
        ).astype(jnp.bfloat16)

    for phase in range(2):
        side = y if phase == 0 else 1 - y
        if phase == 1:
            for hop in (0, 1, 3, 2):
                arrived(OUTPUT_0, 2 * lax.rem(z + hop, 4) + 1 - y)
                arrived(OUTPUT_1, 2 * lax.rem(z + hop, 4) + 1 - y)
        for which in (other, mine):

            def first(chunk, carry):
                share = product(side, 1 - core, which, chunk)
                for x_of in range(2):
                    sent_core[phase, which, chunk, x_of] = share[
                        :, x_of * 128 : (x_of + 1) * 128
                    ].astype(jnp.bfloat16)
                core_copy(phase, which, chunk).start()
                return carry

            lax.fori_loop(0, chunks, first, 0)

            def second(chunk, carry):
                share = product(side, core, which, chunk)
                core_copy(phase, which, chunk).wait_recv()
                got = got_core[phase, which, chunk].astype(jnp.float32)
                totals = [share[:, 0:128] + got[0], share[:, 128:256] + got[1]]
                first_x = x == 0
                sent_x[phase, which, chunk] = jnp.where(first_x, totals[1], totals[0]).astype(
                    jnp.bfloat16
                )
                x_copy(phase, which, chunk).start()
                kept[phase, which, chunk] = jnp.where(first_x, totals[0], totals[1])
                return carry

            lax.fori_loop(0, chunks, second, 0)

    for phase in range(2):
        side = y if phase == 0 else 1 - y

        def third(chunk, carry):
            x_copy(phase, other, chunk).wait_recv()
            sent_z[phase, chunk] = (
                kept[phase, other, chunk] + got_x[phase, other, chunk].astype(jnp.float32)
            ).astype(jnp.bfloat16)
            z_copy(phase, chunk).start()
            return carry

        lax.fori_loop(0, chunks, third, 0)

    for phase in range(2):
        side = y if phase == 0 else 1 - y

        def own(chunk, carry):
            x_copy(phase, mine, chunk).wait_recv()
            write(
                side, mine, chunk,
                kept[phase, mine, chunk] + got_x[phase, mine, chunk].astype(jnp.float32),
            )
            return carry

        lax.fori_loop(0, chunks, own, 0)

    for phase in range(2):
        side = y if phase == 0 else 1 - y

        def returned(chunk, carry):
            z_copy(phase, chunk).wait_recv()
            write(side, other, chunk, got_z[phase, chunk].astype(jnp.float32))
            return carry

        lax.fori_loop(0, chunks, returned, 0)

    for index in range(PIECES):
        for hop in (1, 2, 3):
            along(index, hop).wait_send()
            onward(index, hop).wait_send()
        across(index).wait_send()
    for step in range(SPAN // TOKEN_ROWS):
        share_tokens(step).wait_send()
        for slot in (1, 2, 3):
            spread_tokens(slot, step).wait_send()
    share_info().wait_send()
    for step in range(3):
        share_shrunk(step).wait_send()
    for pair in range(2):
        for which in range(2):
            share_attended(which, pair).wait_send()
    for phase in range(2):
        for chunk in range(chunks):
            for which in range(2):
                core_copy(phase, which, chunk).wait_send()
                x_copy(phase, which, chunk).wait_send()
            z_copy(phase, chunk).wait_send()


def fused_layer(
    tokens, segment, request_position, in_use, slots, gain,
    query_weight, key_weight, value_weight, output_weight, down, up,
):
    bf16, f32 = jnp.bfloat16, jnp.float32
    rows, width = tokens.shape
    chunks = 2
    piece = rows // chunks
    hbm = pl.BlockSpec(memory_space=pltpu.HBM)
    dma = pltpu.SemaphoreType.DMA
    return pl.pallas_call(
        layer_kernel,
        out_shape=jax.ShapeDtypeStruct((rows, 512), bf16),
        in_specs=[hbm] * 13,
        out_specs=pl.BlockSpec(memory_space=pltpu.VMEM),
        scratch_shapes=[
            pltpu.VMEM(segment.shape, jnp.int32),
            pltpu.SMEM(request_position.shape, jnp.int32),
            pltpu.SMEM(in_use.shape, jnp.int32),
            pltpu.SMEM(slots.shape, jnp.int32),
            pltpu.VMEM((16, 128), bf16),
            pltpu.VMEM((2, REACH, 256), bf16),
            dma((6,)),
            pltpu.VMEM((rows, width), bf16),
            pltpu.VMEM((2, rows, width), bf16),
            pltpu.VMEM((2, 8, rows), f32),
            pltpu.VMEM((2, rows, 3 * SPAN), f32),
            pltpu.VMEM((2, rows, 256), f32),
            pltpu.VMEM((8, RANK, 1024), bf16),
            pltpu.VMEM((6, 8, 256, 128), bf16),
            pltpu.VMEM((8, 64, 256), bf16),
            pltpu.VMEM((8, 512, 128), bf16),
            pltpu.VMEM((2, RANK, 2 * rows), bf16),
            pltpu.VMEM((2, RANK, 2 * rows), bf16),
            pltpu.VMEM((2, RANK, 2 * rows), bf16),
            pltpu.VMEM((2, 2, rows, 256), bf16),
            pltpu.VMEM((2, 2, rows, 128), bf16),
            pltpu.VMEM((2, 2, rows, 128), bf16),
            pltpu.VMEM((2, 2, rows, 128), bf16),
            pltpu.VMEM((2, 2, 2, rows, 128), bf16),
            pltpu.VMEM((2, 2, chunks, 2, piece, 128), bf16),
            pltpu.VMEM((2, 2, chunks, 2, piece, 128), bf16),
            pltpu.VMEM((2, 2, chunks, piece, 128), bf16),
            pltpu.VMEM((2, 2, chunks, piece, 128), bf16),
            pltpu.VMEM((2, 2, chunks, piece, 128), f32),
            pltpu.VMEM((2, chunks, piece, 128), bf16),
            pltpu.VMEM((2, chunks, piece, 128), bf16),
            dma((4,)),
            dma((PIECES, 7)),
            dma((PIECES, 8)),
            dma((PIECES,)),
            dma((4, SPAN // TOKEN_ROWS)),
            dma((4, SPAN // TOKEN_ROWS)),
            dma((2,)),
            dma((3,)),
            dma((3,)),
            dma((2, 2)),
            dma((2, 2)),
            dma((2, 2, chunks)),
            dma((2, 2, chunks)),
            dma((2, 2, chunks)),
            dma((2, 2, chunks)),
            dma((2, chunks)),
            dma((2, chunks)),
        ],
        compiler_params=pltpu.CompilerParams(
            collective_id=0, has_side_effects=True, vmem_limit_bytes=56 * 1024 * 1024
        ),
    )(
        tokens, segment, request_position, in_use, slots, gain.reshape(16, 128),
        jnp.asarray(rotation_tables()),
        down.reshape(-1, width), query_weight, key_weight, value_weight,
        up.reshape(-1, up.shape[3]), output_weight,
    )


def active_rows(stored, active_slots):
    slot_total = stored.shape[0]
    held = lax.axis_index("req") * slot_total + jnp.arange(slot_total, dtype=jnp.int32)
    chosen = (active_slots[:, None] == held[None, :]).astype(stored.dtype)
    rows = jnp.einsum(
        "as,srd->ard", chosen, stored, preferred_element_type=jnp.float32
    ).astype(stored.dtype)
    return lax.psum(rows, "req").reshape(-1, stored.shape[2])


def positions_of(segment):
    ordinal = jnp.arange(segment.shape[0], dtype=jnp.int32)
    before = segment[None, :] < segment[:, None]
    return ordinal - jnp.sum(before.astype(jnp.int32), axis=1)


def apply_rotation(values, token_positions):
    half_dim = HEAD_WIDTH // 2
    frequency = rope_base ** (-(jnp.arange(half_dim, dtype=jnp.float32) * 2.0 / HEAD_WIDTH))
    angles = token_positions.astype(jnp.float32)[:, None] * frequency[None, :]
    cosine = jnp.cos(angles)[:, None, :]
    sine_part = jnp.sin(angles)[:, None, :]
    first_half = values[..., :half_dim]
    second_half = values[..., half_dim:]
    return jnp.concatenate(
        [
            first_half * cosine - second_half * sine_part,
            second_half * cosine + first_half * sine_part,
        ],
        axis=-1,
    )


def attend(query_per_head, key_heads, value_per_head, segment):
    scores = (
        jnp.einsum("qhd,khd->hqk", query_per_head, key_heads, preferred_element_type=jnp.float32)
        * 0.125
    )
    ordinal = jnp.arange(segment.shape[0], dtype=jnp.int32)
    allowed = (segment[:, None] == segment[None, :]) & (ordinal[None, :] <= ordinal[:, None])
    scores = jnp.where(allowed[None], scores, jnp.float32(-1e30))
    row_peak = jnp.max(scores, axis=-1, keepdims=True)
    exponent = jnp.where(allowed[None], jnp.exp(scores - row_peak), jnp.float32(0.0))
    weights = (exponent / jnp.sum(exponent, axis=-1, keepdims=True)).astype(jnp.bfloat16)
    return jnp.einsum(
        "hqk,khd->qhd", weights, value_per_head, preferred_element_type=jnp.float32
    ).astype(jnp.bfloat16)


def local(
    tokens,
    token_request_number,
    request_adapter_position,
    adapters_in_use,
    adapter_storage_slot,
    input_norm_gain,
    query_weight,
    key_weight,
    value_weight,
    output_weight,
    adapter_down_weight,
    adapter_up_weight,
):
    if (
        lax.axis_size("req") == 8
        and lax.axis_size("tp") == 4
        and tokens.shape == (512, 2048)
        and adapter_down_weight.shape == (2, 2, 16, 2048)
    ):
        return fused_layer(
            tokens,
            token_request_number,
            request_adapter_position,
            adapters_in_use,
            adapter_storage_slot,
            input_norm_gain,
            query_weight,
            key_weight,
            value_weight,
            output_weight,
            adapter_down_weight,
            adapter_up_weight,
        )
    row_total, model_width = tokens.shape
    local_width = query_weight.shape[1]
    reduced_rows = adapter_down_weight.shape[2]
    slot_total = adapter_down_weight.shape[0]
    segment = token_request_number[0]
    request_adapters = request_adapter_position[0]
    tp_total = lax.axis_size("tp")
    req_total = lax.axis_size("req")
    part_rows = reduced_rows // tp_total
    share = 2 * part_rows
    down_part = lax.dynamic_slice_in_dim(
        adapter_down_weight, lax.axis_index("tp") * part_rows, part_rows, 2
    ).reshape(slot_total, share, model_width)
    up_part = adapter_up_weight.reshape(slot_total, 2 * reduced_rows, local_width)
    active_slots = jnp.take(adapter_storage_slot, adapters_in_use, axis=0)
    place_total = active_slots.shape[0]
    request_places = request_adapters
    member = segment[:, None] == jnp.arange(request_adapters.shape[0], dtype=jnp.int32)[None, :]
    token_place = jnp.sum(
        jnp.where(member, request_places[None, :], jnp.zeros_like(request_places)[None, :]),
        axis=1,
    )
    column = jnp.arange(place_total * share, dtype=jnp.int32)
    mask = (token_place[:, None] == (column // share)[None, :]).astype(jnp.bfloat16)
    lanes = max(128, tp_total * share)
    fold = (lax.axis_index("tp") * share + column % share)[:, None] == jnp.arange(
        lanes, dtype=jnp.int32
    )[None, :]
    fold = fold.astype(jnp.bfloat16)
    floats = tokens.astype(jnp.float32)
    normed = (
        floats
        * lax.rsqrt(jnp.mean(floats * floats, axis=-1, keepdims=True) + norm_eps)
        * input_norm_gain.astype(jnp.float32)
    ).astype(jnp.bfloat16)
    down_all = active_rows(down_part, active_slots)
    up_all = active_rows(up_part, active_slots)
    output_full = lax.all_gather(output_weight, "req", axis=1, tiled=True)
    query_plain, key_base, value_plain = [
        jnp.dot(
            normed,
            lax.all_gather(weight, "req", axis=0, tiled=True),
            preferred_element_type=jnp.float32,
        )
        for weight in (query_weight, key_weight, value_weight)
    ]
    shrunk_all = lax.dot_general(
        normed, down_all, (((1,), (1,)), ((), ())), preferred_element_type=jnp.float32
    ).astype(jnp.bfloat16)
    shrunk = lax.psum(
        jnp.dot(shrunk_all * mask, fold, preferred_element_type=jnp.float32), "tp"
    ).astype(jnp.bfloat16)
    shrunk = shrunk[:, : tp_total * share]
    source = jnp.arange(tp_total * share, dtype=jnp.int32)
    source_kind = (source % share) // part_rows
    source_rank = (source // share) * part_rows + source % part_rows
    target = jnp.arange(place_total * reduced_rows, dtype=jnp.int32)
    mine = token_place[:, None] == (target // reduced_rows)[None, :]
    up_all = up_all.reshape(place_total, 2, reduced_rows, local_width)

    def change_of(kind):
        spread_map = (source_kind == kind)[:, None] & (
            source_rank[:, None] == (target % reduced_rows)[None, :]
        )
        spread = jnp.dot(
            shrunk, spread_map.astype(jnp.bfloat16), preferred_element_type=jnp.float32
        ).astype(jnp.bfloat16)
        spread = jnp.where(mine, spread, jnp.zeros((), jnp.bfloat16))
        return jnp.dot(
            spread,
            up_all[:, kind].reshape(place_total * reduced_rows, local_width),
            preferred_element_type=jnp.float32,
        )

    query_change = change_of(0)
    value_change = change_of(1)
    head_total = local_width // HEAD_WIDTH
    token_positions = positions_of(segment)
    query_per_head = apply_rotation(
        (query_plain + adapter_scale * query_change).reshape(row_total, head_total, HEAD_WIDTH),
        token_positions,
    ).astype(jnp.bfloat16)
    key_heads = apply_rotation(
        key_base.reshape(row_total, head_total, HEAD_WIDTH), token_positions
    ).astype(jnp.bfloat16)
    value_per_head = (
        (value_plain + adapter_scale * value_change)
        .astype(jnp.bfloat16)
        .reshape(row_total, head_total, HEAD_WIDTH)
    )
    attended = attend(query_per_head, key_heads, value_per_head, segment).reshape(
        row_total, local_width
    )
    share_width = model_width // tp_total
    residual_part = lax.dynamic_slice_in_dim(
        tokens, lax.axis_index("tp") * share_width, share_width, 1
    )
    partial_out = jnp.dot(attended, output_full, preferred_element_type=jnp.float32)
    summed = lax.psum_scatter(
        partial_out.astype(jnp.bfloat16), "tp", scatter_dimension=1, tiled=True
    ).astype(jnp.float32)
    return (summed + residual_part.astype(jnp.float32)).astype(jnp.bfloat16)


def solution(mesh):
    in_specs = (
        P("req", None),
        P("req", None),
        P("req", None),
        P(),
        P(),
        P(),
        P("req", "tp"),
        P("req", "tp"),
        P("req", "tp"),
        P("tp", "req"),
        P("req", None, None, None),
        P("req", None, None, "tp"),
    )
    out_specs = P("req", "tp")
    return jax.shard_map(local, mesh=mesh, in_specs=in_specs, out_specs=out_specs, check_vma=False)
```

```python
import functools

import jax
import jax.numpy as jnp
import numpy as np
from jax import lax
from jax.experimental import pallas as pl
from jax.experimental.pallas import tpu as pltpu
from jax.sharding import PartitionSpec as P

HEAD_WIDTH = 64


norm_eps = 1e-05
rope_base = 130000.0
adapter_scale = 2.0

MESH = pl.DeviceIdType.MESH
DOWN, QUERY_0, KEY_0, UP, VALUE_0, QUERY_1, KEY_1, VALUE_1, OUTPUT_0, OUTPUT_1 = range(10)
PIECES = 10
AHEAD = 2
TOKEN_ROWS = 32
SPAN = 128
PLACES = 16
RANK = 16
REACH = 256
FAR = 3.0e38
NEVER = -1.0e30
NT = (((1,), (1,)), ((), ()))
TN = (((0,), (0,)), ((), ()))


def rotation_tables():
    half = HEAD_WIDTH // 2
    lane = np.arange(128)
    frequency = np.float32(rope_base) ** (-(np.arange(half, dtype=np.float32) * 2.0 / HEAD_WIDTH))
    angles = np.arange(REACH, dtype=np.float32)[:, None] * frequency.astype(np.float32)[None, lane % half]
    angles = angles.astype(np.float64)
    sign = np.where(lane % HEAD_WIDTH < half, -1.0, 1.0)
    table = np.concatenate([np.cos(angles), np.sin(angles) * sign], axis=1).astype(np.float32)
    high = table.astype(jnp.bfloat16)
    low = (table - high.astype(np.float32)).astype(jnp.bfloat16)
    return np.stack([high, low])


def layer_kernel(
    tokens, segment_hbm, request_hbm, in_use_hbm, slots_hbm, gain_hbm, table_hbm,
    down, query_weight, key_weight, value_weight, up, output_weight,
    out,
    segment_in, request_position, in_use, slots, gain, table, operand_sems,
    tok, normed, info, limit, rotation,
    down_all, weight_all, up_all, output_all,
    shrunk_own, shrunk_got, shrunk_all, laid, query_heads, key_heads, value_heads, attended,
    sent_core, got_core, sent_x, got_x, kept, sent_z, got_z,
    token_sems, send_sems, recv_sems, local_sems,
    spread_send, spread_recv, info_sems, shrunk_send, shrunk_recv, attended_send, attended_recv,
    core_send, core_recv, x_send, x_recv, z_send, z_recv,
):
    me = lax.axis_index("req")
    part = lax.axis_index("tp")
    z, y = me // 2, me % 2
    x, core = part // 2, part % 2
    mine = z % 2
    other = 1 - mine
    z_mate = 2 * (z + 1 - 2 * mine) + y
    y_mate = 2 * z + 1 - y
    near, cross = 1 + 2 * mine, 3 - 2 * mine
    real = {1: cross, 3: 2, 2: near}
    core_mate = 2 * x + 1 - core
    x_mate = 2 * (1 - x) + core
    weights = {
        QUERY_0: (query_weight, 0), KEY_0: (key_weight, 0), VALUE_0: (value_weight, 0),
        QUERY_1: (query_weight, 1), KEY_1: (key_weight, 1), VALUE_1: (value_weight, 1),
    }
    weight_slot = {name: slot for slot, name in enumerate(weights)}

    def piece(index, half):
        if index == DOWN:
            rows = pl.ds(pl.multiple_of(part * 16, 16), 16)
            return down.at[rows, pl.ds(pl.multiple_of(half * 1024, 1024), 1024)]
        if index == UP:
            return up.at[:, pl.ds(pl.multiple_of(half * 256, 256), 256)]
        if index in weights:
            weight, pair = weights[index]
            return weight.at[:, pl.ds(pl.multiple_of(half * 256 + pair * 128, 128), 128)]
        rows = pl.ds((index - OUTPUT_0) * 256, 256)
        return output_weight.at[rows, pl.ds(pl.multiple_of(half * 128, 128), 128)]

    def block(index, origin):
        if index == DOWN:
            return down_all.at[origin]
        if index == UP:
            return up_all.at[origin]
        if index in weights:
            return weight_all.at[weight_slot[index], origin]
        return output_all.at[origin, pl.ds((index - OUTPUT_0) * 256, 256), :]

    def remote(source, target, send, recv, req=None, tp=None):
        return pltpu.make_async_remote_copy(
            src_ref=source,
            dst_ref=target,
            send_sem=send,
            recv_sem=recv,
            device_id={
                "req": me if req is None else req,
                "tp": part if tp is None else tp,
            },
            device_id_type=MESH,
        )

    def along(index, hop):
        there = lax.rem(z + real[hop], 4)
        return remote(
            piece(index, there % 2),
            block(index, me),
            send_sems.at[index, hop],
            recv_sems.at[index, me],
            req=2 * there + y,
        )

    def across(index):
        return remote(
            piece(index, mine),
            block(index, me),
            send_sems.at[index, 0],
            recv_sems.at[index, me],
            req=y_mate,
        )

    def onward(index, hop):
        origin = 2 * lax.rem(z + real[hop], 4) + y
        held = block(index, origin)
        return remote(
            held, held, send_sems.at[index, 3 + hop], recv_sems.at[index, origin], req=y_mate
        )

    def keep(index):
        return pltpu.make_async_copy(piece(index, mine), block(index, me), local_sems.at[index])

    def arrived(index, origin):
        held = block(index, origin)
        remote(
            held, held, send_sems.at[index, 0], recv_sems.at[index, origin], req=y_mate
        ).wait_recv()

    def pump(index, hops=(1, 3, 2)):
        for hop in hops:
            arrived(index, 2 * lax.rem(z + real[hop], 4) + y)
            onward(index, hop).start()
            if index + AHEAD < PIECES:
                along(index + AHEAD, hop).start()

    def complete(index):
        for hop in (0, 1, 3, 2):
            arrived(index, 2 * lax.rem(z + hop, 4) + 1 - y)
        keep(index).wait()

    def load_tokens(quarter):
        rows = pl.ds(pl.multiple_of(quarter * SPAN, SPAN), SPAN)
        return pltpu.make_async_copy(tokens.at[rows, :], tok.at[rows, :], token_sems.at[quarter])

    def quarters(which, quarter):
        return normed.at[which, pl.ds(pl.multiple_of(quarter * SPAN, SPAN), SPAN), :]

    def token_rows(which, quarter, step):
        first = quarter * SPAN + step * TOKEN_ROWS
        return normed.at[which, pl.ds(pl.multiple_of(first, TOKEN_ROWS), TOKEN_ROWS), :]

    def share_tokens(step):
        held = token_rows(mine, part, step)
        return remote(
            held, held, spread_send.at[0, step], spread_recv.at[part, step], req=z_mate
        )

    def spread_tokens(slot, step):
        quarter = x_mate if slot == 3 else part
        held = token_rows(other, quarter, step)
        return remote(
            held, held, spread_send.at[slot, step], spread_recv.at[quarter, step],
            tp=x_mate if slot == 1 else core_mate,
        )

    def tokens_arrived(quarter, step):
        held = token_rows(other, quarter, step)
        remote(
            held, held, spread_send.at[0, step], spread_recv.at[quarter, step], req=z_mate
        ).wait_recv()

    def spread(step):
        tokens_arrived(part, step)
        spread_tokens(1, step).start()
        spread_tokens(2, step).start()

    def pass_tokens(step):
        tokens_arrived(x_mate, step)
        spread_tokens(3, step).start()

    def share_info():
        held = info.at[mine]
        return remote(held, held, info_sems.at[0], info_sems.at[1], req=z_mate)

    def share_shrunk(step):
        source = shrunk_all.at[core] if step == 2 else shrunk_own.at[step]
        target = shrunk_all.at[core] if step == 2 else shrunk_got.at[step]
        return remote(
            source, target, shrunk_send.at[step], shrunk_recv.at[step],
            req=z_mate if step == 1 else me,
            tp=(x_mate, part, core_mate)[step],
        )

    def add_shrunk(step):
        share_shrunk(step).wait_recv()
        total = shrunk_own[step].astype(jnp.float32) + shrunk_got[step].astype(jnp.float32)
        if step == 0:
            shrunk_own[1] = total.astype(jnp.bfloat16)
        else:
            shrunk_all[core] = total.astype(jnp.bfloat16)
        share_shrunk(step + 1).start()

    operands = [
        pltpu.make_async_copy(source, target, operand_sems.at[number])
        for number, (source, target) in enumerate(
            [
                (gain_hbm, gain), (segment_hbm, segment_in), (request_hbm, request_position),
                (in_use_hbm, in_use), (slots_hbm, slots), (table_hbm, table),
            ]
        )
    ]
    load_tokens(part).start()
    for operand in operands:
        operand.start()
    for step in range(1, 4):
        load_tokens(lax.rem(part + step, 4)).start()

    barrier = pltpu.get_barrier_semaphore()

    def greet(req, tp):
        pl.semaphore_signal(
            barrier, inc=1, device_id={"req": req, "tp": tp}, device_id_type=MESH
        )

    for hop in (1, 2, 3):
        greet(2 * lax.rem(z + hop, 4) + y, part)
    greet(y_mate, part)
    greet(me, core_mate)
    greet(me, x_mate)
    pl.semaphore_wait(barrier, 6)

    for index in range(AHEAD):
        for hop in (1, 3, 2):
            along(index, hop).start()
    for index in range(PIECES):
        across(index).start()

    operands[0].wait()
    gains = jnp.concatenate([gain[i : i + 1, :] for i in range(16)], axis=1).astype(jnp.float32)

    def normalise(quarter):
        load_tokens(quarter).wait()

        def some(step, carry):
            rows = pl.ds(pl.multiple_of(quarter * SPAN + step * 32, 32), 32)
            floats = tok[rows, :].astype(jnp.float32)
            mean = jnp.mean(floats * floats, axis=-1, keepdims=True)
            normed[mine, rows, :] = (floats * lax.rsqrt(mean + norm_eps) * gains).astype(
                jnp.bfloat16
            )
            return carry

        lax.fori_loop(0, SPAN // 32, some, 0)

    def prepare(which):
        facts = info[which]
        columns = facts.T
        for block in range(4):
            first = max(0, block - 2) * SPAN
            width = min(block + 1, 3) * SPAN
            query_segment = columns[block * SPAN : (block + 1) * SPAN, 0:1]
            key_segment = facts[0:1, first : first + width]
            query_order = block * SPAN + lax.broadcasted_iota(jnp.int32, (SPAN, width), 0)
            key_order = first + lax.broadcasted_iota(jnp.int32, (SPAN, width), 1)
            allowed = (query_segment == key_segment) & (key_order <= query_order)
            limit[which, pl.ds(block * SPAN, SPAN), pl.ds(0, width)] = jnp.where(
                allowed, FAR, NEVER
            )
        lane = lax.broadcasted_iota(jnp.int32, (4 * SPAN, REACH), 1).astype(jnp.float32)
        chosen = jnp.where(columns[:, 2:3] == lane, 1.0, 0.0).astype(jnp.bfloat16)
        rotation[which] = jnp.dot(
            chosen, table[0], preferred_element_type=jnp.float32
        ) + jnp.dot(chosen, table[1], preferred_element_type=jnp.float32)

    def shrink(which):
        columns = pl.ds(pl.multiple_of(mine * 1024, 1024), 1024)
        product = lax.dot_general(
            down_all[...].reshape(8 * RANK, 1024),
            normed[which, :, columns],
            NT,
            preferred_element_type=jnp.float32,
        )
        places = info[which][1:2, :]
        total = jnp.zeros((RANK, product.shape[1]), jnp.float32)
        for origin in range(8):
            wanted = (2 * origin + x).astype(jnp.float32)
            total = total + jnp.where(
                places == wanted, product[origin * RANK : (origin + 1) * RANK], 0.0
            )
        at = pl.ds(pl.multiple_of(which * 512, 512), 512)
        shrunk_own[0, :, at] = total.astype(jnp.bfloat16)

    def projected(which, index):
        return jnp.dot(
            normed[which],
            weight_all[weight_slot[index]].reshape(8 * 256, 128),
            preferred_element_type=jnp.float32,
        )

    def lay(which, kind):
        columns = info[which].T
        at = pl.ds(pl.multiple_of(which * 512, 512), 512)
        compact = shrunk_all[kind, :, at].astype(jnp.float32)
        padded = jnp.concatenate(
            [compact, jnp.zeros((128 - RANK, compact.shape[1]), jnp.float32)], axis=0
        ).T
        lane = lax.broadcasted_iota(jnp.int32, (128, PLACES * RANK), 1)
        row = lax.broadcasted_iota(jnp.int32, (128, PLACES * RANK), 0)
        tile = jnp.where(lane % RANK == row, 1.0, 0.0).astype(jnp.bfloat16)
        tiled = jnp.dot(
            padded.astype(jnp.bfloat16), tile, preferred_element_type=jnp.float32
        )
        lanes = lax.broadcasted_iota(jnp.int32, tiled.shape, 1) // RANK
        laid[which, kind] = jnp.where(
            columns[:, 1:2] == lanes.astype(jnp.float32), tiled, 0.0
        ).astype(jnp.bfloat16)

    def change(which, kind, pair):
        ups = up_all[:, :, pl.ds(pair * 128, 128)].reshape(8, 2, 2, RANK, 128)
        return adapter_scale * jnp.dot(
            laid[which, kind],
            ups[:, :, kind].reshape(PLACES * RANK, 128),
            preferred_element_type=jnp.float32,
        )

    def rotated(which, value):
        half = HEAD_WIDTH // 2
        low = lax.broadcasted_iota(jnp.int32, (512, 128), 1) % HEAD_WIDTH < half
        swapped = jnp.where(low, pltpu.roll(value, 128 - half, 1), pltpu.roll(value, half, 1))
        return value * rotation[which, :, 0:128] + swapped * rotation[which, :, 128:256]

    def make_key(pair, which):
        key = projected(which, KEY_1 if pair else KEY_0)
        key_heads[which, pair] = rotated(which, key).astype(jnp.bfloat16)

    def make_query(pair, which):
        query = projected(which, QUERY_1 if pair else QUERY_0) + change(which, 0, pair)
        query_heads[which, pair] = (rotated(which, query) * 0.125).astype(jnp.bfloat16)

    def make_value(pair, which):
        value = projected(which, VALUE_1 if pair else VALUE_0) + change(which, 1, pair)
        value_heads[which, pair] = value.astype(jnp.bfloat16)

    def share_attended(which, pair):
        held = attended.at[mine, pair, which]
        return remote(
            held, held, attended_send.at[pair, which], attended_recv.at[pair, which], req=z_mate
        )

    def attend(which, pair):
        left = lax.broadcasted_iota(jnp.int32, (SPAN, 128), 1) < HEAD_WIDTH
        spans = [(max(0, number - 2) * SPAN, min(number + 1, 3) * SPAN) for number in range(4)]
        rows = [pl.ds(number * SPAN, SPAN) for number in range(4)]
        scores = []
        for number, (first, width) in enumerate(spans):
            query = query_heads[which, pair, rows[number], :]
            zero = jnp.zeros_like(query)
            both = jnp.concatenate(
                [jnp.where(left, query, zero), jnp.where(left, zero, query)], axis=0
            )
            keys = key_heads[which, pair, pl.ds(first, width), :]
            score = lax.dot_general(both, keys, NT, preferred_element_type=jnp.float32)
            bound = limit[which, rows[number], pl.ds(0, width)]
            scores.append(jnp.minimum(score, jnp.concatenate([bound, bound], axis=0)))
        exponents = [
            jnp.exp(score - jnp.max(score, axis=-1, keepdims=True)).astype(jnp.bfloat16)
            for score in scores
        ]
        results = []
        for (first, width), exponent in zip(spans, exponents):
            values = value_heads[which, pair, pl.ds(first, width), :]
            wide = jnp.concatenate([values, jnp.ones_like(values)], axis=1)
            results.append(jnp.dot(exponent, wide, preferred_element_type=jnp.float32))
        for number, result in enumerate(results):
            divided = result[:, 0:128] / result[:, 128:256]
            attended[mine, pair, which, rows[number], :] = jnp.where(
                left, divided[0:SPAN], divided[SPAN : 2 * SPAN]
            ).astype(jnp.bfloat16)
        share_attended(which, pair).start()

    def lay_all(which, carry):
        lay(which, 0)
        lay(which, 1)
        return carry

    normalise(part)
    for step in range(2):
        share_tokens(step).start()
    for operand in operands[1:]:
        operand.wait()
    segment = segment_in[...].astype(jnp.float32)
    ordinal = lax.broadcasted_iota(jnp.int32, segment.shape, 1).astype(jnp.float32)
    place = jnp.zeros_like(segment)
    start = jnp.zeros_like(segment)
    for request in range(request_position.shape[1]):
        slot = slots[in_use[request_position[0, request]]]
        here = segment == float(request)
        place = jnp.where(here, slot.astype(jnp.float32), place)
        before = jnp.sum(jnp.where(segment < float(request), 1.0, 0.0), axis=1, keepdims=True)
        start = jnp.where(here, before, start)
    info[mine] = jnp.concatenate(
        [segment, place, ordinal - start, jnp.zeros((5, segment.shape[1]), jnp.float32)], axis=0
    )
    share_info().start()
    for index in range(PIECES):
        keep(index).start()
    normalise(lax.rem(part + 1, 4))
    pump(DOWN)
    share_tokens(2).start()
    normalise(lax.rem(part + 2, 4))
    pump(QUERY_0, (1, 3))
    normalise(lax.rem(part + 3, 4))
    pump(QUERY_0, (2,))
    share_tokens(3).start()
    spread(0)
    prepare(mine)
    pump(KEY_0)
    spread(1)
    share_info().wait_recv()
    prepare(other)
    pump(UP)
    spread(2)
    pass_tokens(0)
    complete(DOWN)
    shrink(mine)
    pump(VALUE_0, (1, 3))
    spread(3)
    pass_tokens(1)
    pump(VALUE_0, (2,))
    complete(KEY_0)
    make_key(0, mine)
    pass_tokens(2)
    pass_tokens(3)
    pump(QUERY_1, (1, 3))
    for step in range(SPAN // TOKEN_ROWS):
        tokens_arrived(core_mate, step)
        tokens_arrived(2 * (1 - x) + 1 - core, step)
    shrink(other)
    share_shrunk(0).start()
    pump(QUERY_1, (2,))
    make_key(0, other)
    add_shrunk(0)
    complete(QUERY_0)
    complete(UP)
    add_shrunk(1)
    pump(KEY_1, (1,))
    share_shrunk(2).wait_recv()
    lax.fori_loop(0, 2, lay_all, 0)
    pump(KEY_1, (3, 2))
    make_query(0, other)
    make_query(0, mine)
    complete(VALUE_0)
    make_value(0, other)
    pump(VALUE_1, (1,))
    make_value(0, mine)
    attend(other, 0)
    pump(VALUE_1, (3, 2))
    complete(QUERY_1)
    make_query(1, other)
    make_query(1, mine)
    attend(mine, 0)
    pump(OUTPUT_0, (1,))
    complete(KEY_1)
    make_key(1, other)
    make_key(1, mine)
    pump(OUTPUT_0, (3,))
    complete(VALUE_1)
    make_value(1, other)
    attend(other, 1)
    make_value(1, mine)
    attend(mine, 1)
    pump(OUTPUT_0, (2,))
    pump(OUTPUT_1)
    keep(OUTPUT_0).wait()
    keep(OUTPUT_1).wait()

    chunks = sent_core.shape[2]
    rows_of = sent_core.shape[4]

    for pair in range(2):
        for which in range(2):
            held = attended.at[other, pair, which]
            remote(
                held, held, attended_send.at[pair, which], attended_recv.at[pair, which],
                req=z_mate,
            ).wait_recv()

    def rows_at(chunk):
        return pl.ds(pl.multiple_of(chunk * rows_of, rows_of), rows_of)

    def product(side, to_core, which, chunk):
        heads = jnp.concatenate(
            [attended[z_of, pair, which, rows_at(chunk), :] for z_of in range(2) for pair in range(2)],
            axis=1,
        )
        columns = jnp.concatenate(
            [output_all[2 * (2 * x_of + to_core) + side] for x_of in range(2)], axis=1
        )
        return jnp.dot(heads, columns, preferred_element_type=jnp.float32)

    def core_copy(phase, which, chunk):
        return remote(
            sent_core.at[phase, which, chunk], got_core.at[phase, which, chunk],
            core_send.at[phase, which, chunk], core_recv.at[phase, which, chunk], tp=core_mate,
        )

    def x_copy(phase, which, chunk):
        return remote(
            sent_x.at[phase, which, chunk], got_x.at[phase, which, chunk],
            x_send.at[phase, which, chunk], x_recv.at[phase, which, chunk], tp=x_mate,
        )

    def z_copy(phase, chunk):
        return remote(
            sent_z.at[phase, chunk], got_z.at[phase, chunk],
            z_send.at[phase, chunk], z_recv.at[phase, chunk], req=z_mate,
        )

    def write(side, half, chunk, values):
        first = side * 256 + half * 128
        residual = tok[rows_at(chunk), pl.ds(pl.multiple_of(part * 512 + first, 128), 128)]
        out[rows_at(chunk), pl.ds(pl.multiple_of(first, 128), 128)] = (
            values + residual.astype(jnp.float32)
        ).astype(jnp.bfloat16)

    for phase in range(2):
        side = y if phase == 0 else 1 - y
        if phase == 1:
            for hop in (0, 1, 3, 2):
                arrived(OUTPUT_0, 2 * lax.rem(z + hop, 4) + 1 - y)
                arrived(OUTPUT_1, 2 * lax.rem(z + hop, 4) + 1 - y)
        for which in (other, mine):

            def first(chunk, carry):
                share = product(side, 1 - core, which, chunk)
                for x_of in range(2):
                    sent_core[phase, which, chunk, x_of] = share[
                        :, x_of * 128 : (x_of + 1) * 128
                    ].astype(jnp.bfloat16)
                core_copy(phase, which, chunk).start()
                return carry

            lax.fori_loop(0, chunks, first, 0)

            def second(chunk, carry):
                share = product(side, core, which, chunk)
                core_copy(phase, which, chunk).wait_recv()
                got = got_core[phase, which, chunk].astype(jnp.float32)
                totals = [share[:, 0:128] + got[0], share[:, 128:256] + got[1]]
                first_x = x == 0
                sent_x[phase, which, chunk] = jnp.where(first_x, totals[1], totals[0]).astype(
                    jnp.bfloat16
                )
                x_copy(phase, which, chunk).start()
                kept[phase, which, chunk] = jnp.where(first_x, totals[0], totals[1])
                return carry

            lax.fori_loop(0, chunks, second, 0)

    for phase in range(2):
        side = y if phase == 0 else 1 - y

        def third(chunk, carry):
            x_copy(phase, other, chunk).wait_recv()
            sent_z[phase, chunk] = (
                kept[phase, other, chunk] + got_x[phase, other, chunk].astype(jnp.float32)
            ).astype(jnp.bfloat16)
            z_copy(phase, chunk).start()
            return carry

        lax.fori_loop(0, chunks, third, 0)

    for phase in range(2):
        side = y if phase == 0 else 1 - y

        def own(chunk, carry):
            x_copy(phase, mine, chunk).wait_recv()
            write(
                side, mine, chunk,
                kept[phase, mine, chunk] + got_x[phase, mine, chunk].astype(jnp.float32),
            )
            return carry

        lax.fori_loop(0, chunks, own, 0)

    for phase in range(2):
        side = y if phase == 0 else 1 - y

        def returned(chunk, carry):
            z_copy(phase, chunk).wait_recv()
            write(side, other, chunk, got_z[phase, chunk].astype(jnp.float32))
            return carry

        lax.fori_loop(0, chunks, returned, 0)

    for index in range(PIECES):
        for hop in (1, 2, 3):
            along(index, hop).wait_send()
            onward(index, hop).wait_send()
        across(index).wait_send()
    for step in range(SPAN // TOKEN_ROWS):
        share_tokens(step).wait_send()
        for slot in (1, 2, 3):
            spread_tokens(slot, step).wait_send()
    share_info().wait_send()
    for step in range(3):
        share_shrunk(step).wait_send()
    for pair in range(2):
        for which in range(2):
            share_attended(which, pair).wait_send()
    for phase in range(2):
        for chunk in range(chunks):
            for which in range(2):
                core_copy(phase, which, chunk).wait_send()
                x_copy(phase, which, chunk).wait_send()
            z_copy(phase, chunk).wait_send()


def fused_layer(
    tokens, segment, request_position, in_use, slots, gain,
    query_weight, key_weight, value_weight, output_weight, down, up,
):
    bf16, f32 = jnp.bfloat16, jnp.float32
    rows, width = tokens.shape
    chunks = 2
    piece = rows // chunks
    hbm = pl.BlockSpec(memory_space=pltpu.HBM)
    dma = pltpu.SemaphoreType.DMA
    return pl.pallas_call(
        layer_kernel,
        out_shape=jax.ShapeDtypeStruct((rows, 512), bf16),
        in_specs=[hbm] * 13,
        out_specs=pl.BlockSpec(memory_space=pltpu.VMEM),
        scratch_shapes=[
            pltpu.VMEM(segment.shape, jnp.int32),
            pltpu.SMEM(request_position.shape, jnp.int32),
            pltpu.SMEM(in_use.shape, jnp.int32),
            pltpu.SMEM(slots.shape, jnp.int32),
            pltpu.VMEM((16, 128), bf16),
            pltpu.VMEM((2, REACH, 256), bf16),
            dma((6,)),
            pltpu.VMEM((rows, width), bf16),
            pltpu.VMEM((2, rows, width), bf16),
            pltpu.VMEM((2, 8, rows), f32),
            pltpu.VMEM((2, rows, 3 * SPAN), f32),
            pltpu.VMEM((2, rows, 256), f32),
            pltpu.VMEM((8, RANK, 1024), bf16),
            pltpu.VMEM((6, 8, 256, 128), bf16),
            pltpu.VMEM((8, 64, 256), bf16),
            pltpu.VMEM((8, 512, 128), bf16),
            pltpu.VMEM((2, RANK, 2 * rows), bf16),
            pltpu.VMEM((2, RANK, 2 * rows), bf16),
            pltpu.VMEM((2, RANK, 2 * rows), bf16),
            pltpu.VMEM((2, 2, rows, 256), bf16),
            pltpu.VMEM((2, 2, rows, 128), bf16),
            pltpu.VMEM((2, 2, rows, 128), bf16),
            pltpu.VMEM((2, 2, rows, 128), bf16),
            pltpu.VMEM((2, 2, 2, rows, 128), bf16),
            pltpu.VMEM((2, 2, chunks, 2, piece, 128), bf16),
            pltpu.VMEM((2, 2, chunks, 2, piece, 128), bf16),
            pltpu.VMEM((2, 2, chunks, piece, 128), bf16),
            pltpu.VMEM((2, 2, chunks, piece, 128), bf16),
            pltpu.VMEM((2, 2, chunks, piece, 128), f32),
            pltpu.VMEM((2, chunks, piece, 128), bf16),
            pltpu.VMEM((2, chunks, piece, 128), bf16),
            dma((4,)),
            dma((PIECES, 7)),
            dma((PIECES, 8)),
            dma((PIECES,)),
            dma((4, SPAN // TOKEN_ROWS)),
            dma((4, SPAN // TOKEN_ROWS)),
            dma((2,)),
            dma((3,)),
            dma((3,)),
            dma((2, 2)),
            dma((2, 2)),
            dma((2, 2, chunks)),
            dma((2, 2, chunks)),
            dma((2, 2, chunks)),
            dma((2, 2, chunks)),
            dma((2, chunks)),
            dma((2, chunks)),
        ],
        compiler_params=pltpu.CompilerParams(
            collective_id=0, has_side_effects=True, vmem_limit_bytes=56 * 1024 * 1024
        ),
    )(
        tokens, segment, request_position, in_use, slots, gain.reshape(16, 128),
        jnp.asarray(rotation_tables()),
        down.reshape(-1, width), query_weight, key_weight, value_weight,
        up.reshape(-1, up.shape[3]), output_weight,
    )


def active_rows(stored, active_slots):
    slot_total = stored.shape[0]
    held = lax.axis_index("req") * slot_total + jnp.arange(slot_total, dtype=jnp.int32)
    chosen = (active_slots[:, None] == held[None, :]).astype(stored.dtype)
    rows = jnp.einsum(
        "as,srd->ard", chosen, stored, preferred_element_type=jnp.float32
    ).astype(stored.dtype)
    return lax.psum(rows, "req").reshape(-1, stored.shape[2])


def positions_of(segment):
    ordinal = jnp.arange(segment.shape[0], dtype=jnp.int32)
    before = segment[None, :] < segment[:, None]
    return ordinal - jnp.sum(before.astype(jnp.int32), axis=1)


def apply_rotation(values, token_positions):
    half_dim = HEAD_WIDTH // 2
    frequency = rope_base ** (-(jnp.arange(half_dim, dtype=jnp.float32) * 2.0 / HEAD_WIDTH))
    angles = token_positions.astype(jnp.float32)[:, None] * frequency[None, :]
    cosine = jnp.cos(angles)[:, None, :]
    sine_part = jnp.sin(angles)[:, None, :]
    first_half = values[..., :half_dim]
    second_half = values[..., half_dim:]
    return jnp.concatenate(
        [
            first_half * cosine - second_half * sine_part,
            second_half * cosine + first_half * sine_part,
        ],
        axis=-1,
    )


def attend(query_per_head, key_heads, value_per_head, segment):
    scores = (
        jnp.einsum("qhd,khd->hqk", query_per_head, key_heads, preferred_element_type=jnp.float32)
        * 0.125
    )
    ordinal = jnp.arange(segment.shape[0], dtype=jnp.int32)
    allowed = (segment[:, None] == segment[None, :]) & (ordinal[None, :] <= ordinal[:, None])
    scores = jnp.where(allowed[None], scores, jnp.float32(-1e30))
    row_peak = jnp.max(scores, axis=-1, keepdims=True)
    exponent = jnp.where(allowed[None], jnp.exp(scores - row_peak), jnp.float32(0.0))
    weights = (exponent / jnp.sum(exponent, axis=-1, keepdims=True)).astype(jnp.bfloat16)
    return jnp.einsum(
        "hqk,khd->qhd", weights, value_per_head, preferred_element_type=jnp.float32
    ).astype(jnp.bfloat16)


def local(
    tokens,
    token_request_number,
    request_adapter_position,
    adapters_in_use,
    adapter_storage_slot,
    input_norm_gain,
    query_weight,
    key_weight,
    value_weight,
    output_weight,
    adapter_down_weight,
    adapter_up_weight,
):
    if (
        lax.axis_size("req") == 8
        and lax.axis_size("tp") == 4
        and tokens.shape == (512, 2048)
        and adapter_down_weight.shape == (2, 2, 16, 2048)
    ):
        return fused_layer(
            tokens,
            token_request_number,
            request_adapter_position,
            adapters_in_use,
            adapter_storage_slot,
            input_norm_gain,
            query_weight,
            key_weight,
            value_weight,
            output_weight,
            adapter_down_weight,
            adapter_up_weight,
        )
    row_total, model_width = tokens.shape
    local_width = query_weight.shape[1]
    reduced_rows = adapter_down_weight.shape[2]
    slot_total = adapter_down_weight.shape[0]
    segment = token_request_number[0]
    request_adapters = request_adapter_position[0]
    tp_total = lax.axis_size("tp")
    req_total = lax.axis_size("req")
    part_rows = reduced_rows // tp_total
    share = 2 * part_rows
    down_part = lax.dynamic_slice_in_dim(
        adapter_down_weight, lax.axis_index("tp") * part_rows, part_rows, 2
    ).reshape(slot_total, share, model_width)
    up_part = adapter_up_weight.reshape(slot_total, 2 * reduced_rows, local_width)
    active_slots = jnp.take(adapter_storage_slot, adapters_in_use, axis=0)
    place_total = active_slots.shape[0]
    request_places = request_adapters
    member = segment[:, None] == jnp.arange(request_adapters.shape[0], dtype=jnp.int32)[None, :]
    token_place = jnp.sum(
        jnp.where(member, request_places[None, :], jnp.zeros_like(request_places)[None, :]),
        axis=1,
    )
    column = jnp.arange(place_total * share, dtype=jnp.int32)
    mask = (token_place[:, None] == (column // share)[None, :]).astype(jnp.bfloat16)
    lanes = max(128, tp_total * share)
    fold = (lax.axis_index("tp") * share + column % share)[:, None] == jnp.arange(
        lanes, dtype=jnp.int32
    )[None, :]
    fold = fold.astype(jnp.bfloat16)
    floats = tokens.astype(jnp.float32)
    normed = (
        floats
        * lax.rsqrt(jnp.mean(floats * floats, axis=-1, keepdims=True) + norm_eps)
        * input_norm_gain.astype(jnp.float32)
    ).astype(jnp.bfloat16)
    down_all = active_rows(down_part, active_slots)
    up_all = active_rows(up_part, active_slots)
    output_full = lax.all_gather(output_weight, "req", axis=1, tiled=True)
    query_plain, key_base, value_plain = [
        jnp.dot(
            normed,
            lax.all_gather(weight, "req", axis=0, tiled=True),
            preferred_element_type=jnp.float32,
        )
        for weight in (query_weight, key_weight, value_weight)
    ]
    shrunk_all = lax.dot_general(
        normed, down_all, (((1,), (1,)), ((), ())), preferred_element_type=jnp.float32
    ).astype(jnp.bfloat16)
    shrunk = lax.psum(
        jnp.dot(shrunk_all * mask, fold, preferred_element_type=jnp.float32), "tp"
    ).astype(jnp.bfloat16)
    shrunk = shrunk[:, : tp_total * share]
    source = jnp.arange(tp_total * share, dtype=jnp.int32)
    source_kind = (source % share) // part_rows
    source_rank = (source // share) * part_rows + source % part_rows
    target = jnp.arange(place_total * reduced_rows, dtype=jnp.int32)
    mine = token_place[:, None] == (target // reduced_rows)[None, :]
    up_all = up_all.reshape(place_total, 2, reduced_rows, local_width)

    def change_of(kind):
        spread_map = (source_kind == kind)[:, None] & (
            source_rank[:, None] == (target % reduced_rows)[None, :]
        )
        spread = jnp.dot(
            shrunk, spread_map.astype(jnp.bfloat16), preferred_element_type=jnp.float32
        ).astype(jnp.bfloat16)
        spread = jnp.where(mine, spread, jnp.zeros((), jnp.bfloat16))
        return jnp.dot(
            spread,
            up_all[:, kind].reshape(place_total * reduced_rows, local_width),
            preferred_element_type=jnp.float32,
        )

    query_change = change_of(0)
    value_change = change_of(1)
    head_total = local_width // HEAD_WIDTH
    token_positions = positions_of(segment)
    query_per_head = apply_rotation(
        (query_plain + adapter_scale * query_change).reshape(row_total, head_total, HEAD_WIDTH),
        token_positions,
    ).astype(jnp.bfloat16)
    key_heads = apply_rotation(
        key_base.reshape(row_total, head_total, HEAD_WIDTH), token_positions
    ).astype(jnp.bfloat16)
    value_per_head = (
        (value_plain + adapter_scale * value_change)
        .astype(jnp.bfloat16)
        .reshape(row_total, head_total, HEAD_WIDTH)
    )
    attended = attend(query_per_head, key_heads, value_per_head, segment).reshape(
        row_total, local_width
    )
    share_width = model_width // tp_total
    residual_part = lax.dynamic_slice_in_dim(
        tokens, lax.axis_index("tp") * share_width, share_width, 1
    )
    partial_out = jnp.dot(attended, output_full, preferred_element_type=jnp.float32)
    summed = lax.psum_scatter(
        partial_out.astype(jnp.bfloat16), "tp", scatter_dimension=1, tiled=True
    ).astype(jnp.float32)
    return (summed + residual_part.astype(jnp.float32)).astype(jnp.bfloat16)


def solution(mesh):
    in_specs = (
        P("req", None),
        P("req", None),
        P("req", None),
        P(),
        P(),
        P(),
        P("req", "tp"),
        P("req", "tp"),
        P("req", "tp"),
        P("tp", "req"),
        P("req", None, None, None),
        P("req", None, None, "tp"),
    )
    out_specs = P("req", "tp")
    return jax.shard_map(local, mesh=mesh, in_specs=in_specs, out_specs=out_specs, check_vma=False)
```

```python
import functools

import jax
import jax.numpy as jnp
import numpy as np
from jax import lax
from jax.experimental import pallas as pl
from jax.experimental.pallas import tpu as pltpu
from jax.sharding import PartitionSpec as P

HEAD_WIDTH = 64


norm_eps = 1e-05
rope_base = 130000.0
adapter_scale = 2.0

MESH = pl.DeviceIdType.MESH
DOWN, QUERY_0, KEY_0, UP, VALUE_0, QUERY_1, KEY_1, VALUE_1, OUTPUT_0, OUTPUT_1 = range(10)
PIECES = 10
AHEAD = 2
TOKEN_ROWS = 32
SPAN = 128
PLACES = 16
RANK = 16
REACH = 256
FAR = 3.0e38
NEVER = -1.0e30
NT = (((1,), (1,)), ((), ()))
TN = (((0,), (0,)), ((), ()))


def rotation_tables():
    half = HEAD_WIDTH // 2
    lane = np.arange(128)
    frequency = np.float32(rope_base) ** (-(np.arange(half, dtype=np.float32) * 2.0 / HEAD_WIDTH))
    angles = np.arange(REACH, dtype=np.float32)[:, None] * frequency.astype(np.float32)[None, lane % half]
    angles = angles.astype(np.float64)
    sign = np.where(lane % HEAD_WIDTH < half, -1.0, 1.0)
    table = np.concatenate([np.cos(angles), np.sin(angles) * sign], axis=1).astype(np.float32)
    high = table.astype(jnp.bfloat16)
    low = (table - high.astype(np.float32)).astype(jnp.bfloat16)
    return np.stack([high, low])


def layer_kernel(
    tokens, segment_hbm, request_hbm, in_use_hbm, slots_hbm, gain_hbm, table_hbm,
    down, query_weight, key_weight, value_weight, up, output_weight,
    out,
    segment_in, request_position, in_use, slots, gain, table, operand_sems,
    tok, normed, info, limit, rotation,
    down_all, weight_all, up_all, output_all,
    shrunk_own, shrunk_got, shrunk_all, laid, query_heads, key_heads, value_heads, attended,
    sent_core, got_core, sent_x, got_x, kept, sent_z, got_z,
    token_sems, send_sems, recv_sems, local_sems,
    spread_send, spread_recv, info_sems, shrunk_send, shrunk_recv, attended_send, attended_recv,
    core_send, core_recv, x_send, x_recv, z_send, z_recv,
):
    me = lax.axis_index("req")
    part = lax.axis_index("tp")
    z, y = me // 2, me % 2
    x, core = part // 2, part % 2
    mine = z % 2
    other = 1 - mine
    z_mate = 2 * (z + 1 - 2 * mine) + y
    y_mate = 2 * z + 1 - y
    near, cross = 1 + 2 * mine, 3 - 2 * mine
    real = {1: cross, 3: 2, 2: near}
    core_mate = 2 * x + 1 - core
    x_mate = 2 * (1 - x) + core
    weights = {
        QUERY_0: (query_weight, 0), KEY_0: (key_weight, 0), VALUE_0: (value_weight, 0),
        QUERY_1: (query_weight, 1), KEY_1: (key_weight, 1), VALUE_1: (value_weight, 1),
    }
    weight_slot = {name: slot for slot, name in enumerate(weights)}

    def piece(index, half):
        if index == DOWN:
            rows = pl.ds(pl.multiple_of(part * 16, 16), 16)
            return down.at[rows, pl.ds(pl.multiple_of(half * 1024, 1024), 1024)]
        if index == UP:
            return up.at[:, pl.ds(pl.multiple_of(half * 256, 256), 256)]
        if index in weights:
            weight, pair = weights[index]
            return weight.at[:, pl.ds(pl.multiple_of(half * 256 + pair * 128, 128), 128)]
        rows = pl.ds((index - OUTPUT_0) * 256, 256)
        return output_weight.at[rows, pl.ds(pl.multiple_of(half * 128, 128), 128)]

    def block(index, origin):
        if index == DOWN:
            return down_all.at[origin]
        if index == UP:
            return up_all.at[origin]
        if index in weights:
            return weight_all.at[weight_slot[index], origin]
        return output_all.at[origin, pl.ds((index - OUTPUT_0) * 256, 256), :]

    def remote(source, target, send, recv, req=None, tp=None):
        return pltpu.make_async_remote_copy(
            src_ref=source,
            dst_ref=target,
            send_sem=send,
            recv_sem=recv,
            device_id={
                "req": me if req is None else req,
                "tp": part if tp is None else tp,
            },
            device_id_type=MESH,
        )

    def along(index, hop):
        there = lax.rem(z + real[hop], 4)
        return remote(
            piece(index, there % 2),
            block(index, me),
            send_sems.at[index, hop],
            recv_sems.at[index, me],
            req=2 * there + y,
        )

    def across(index):
        return remote(
            piece(index, mine),
            block(index, me),
            send_sems.at[index, 0],
            recv_sems.at[index, me],
            req=y_mate,
        )

    def onward(index, hop):
        origin = 2 * lax.rem(z + real[hop], 4) + y
        held = block(index, origin)
        return remote(
            held, held, send_sems.at[index, 3 + hop], recv_sems.at[index, origin], req=y_mate
        )

    def keep(index):
        return pltpu.make_async_copy(piece(index, mine), block(index, me), local_sems.at[index])

    def arrived(index, origin):
        held = block(index, origin)
        remote(
            held, held, send_sems.at[index, 0], recv_sems.at[index, origin], req=y_mate
        ).wait_recv()

    def pump(index, hops=(1, 3, 2)):
        for hop in hops:
            arrived(index, 2 * lax.rem(z + real[hop], 4) + y)
            onward(index, hop).start()
            if index + AHEAD < PIECES:
                along(index + AHEAD, hop).start()

    def complete(index):
        for hop in (0, 1, 3, 2):
            arrived(index, 2 * lax.rem(z + hop, 4) + 1 - y)
        keep(index).wait()

    def load_tokens(quarter):
        rows = pl.ds(pl.multiple_of(quarter * SPAN, SPAN), SPAN)
        return pltpu.make_async_copy(tokens.at[rows, :], tok.at[rows, :], token_sems.at[quarter])

    def quarters(which, quarter):
        return normed.at[which, pl.ds(pl.multiple_of(quarter * SPAN, SPAN), SPAN), :]

    def token_rows(which, quarter, step):
        first = quarter * SPAN + step * TOKEN_ROWS
        return normed.at[which, pl.ds(pl.multiple_of(first, TOKEN_ROWS), TOKEN_ROWS), :]

    def share_tokens(step):
        held = token_rows(mine, part, step)
        return remote(
            held, held, spread_send.at[0, step], spread_recv.at[part, step], req=z_mate
        )

    def spread_tokens(slot, step):
        quarter = x_mate if slot == 3 else part
        held = token_rows(other, quarter, step)
        return remote(
            held, held, spread_send.at[slot, step], spread_recv.at[quarter, step],
            tp=x_mate if slot == 1 else core_mate,
        )

    def tokens_arrived(quarter, step):
        held = token_rows(other, quarter, step)
        remote(
            held, held, spread_send.at[0, step], spread_recv.at[quarter, step], req=z_mate
        ).wait_recv()

    def spread(step):
        tokens_arrived(part, step)
        spread_tokens(1, step).start()
        spread_tokens(2, step).start()

    def pass_tokens(step):
        tokens_arrived(x_mate, step)
        spread_tokens(3, step).start()

    def share_info():
        held = info.at[mine]
        return remote(held, held, info_sems.at[0], info_sems.at[1], req=z_mate)

    def share_shrunk(step):
        source = shrunk_all.at[core] if step == 2 else shrunk_own.at[step]
        target = shrunk_all.at[core] if step == 2 else shrunk_got.at[step]
        return remote(
            source, target, shrunk_send.at[step], shrunk_recv.at[step],
            req=z_mate if step == 1 else me,
            tp=(x_mate, part, core_mate)[step],
        )

    def add_shrunk(step):
        share_shrunk(step).wait_recv()
        total = shrunk_own[step].astype(jnp.float32) + shrunk_got[step].astype(jnp.float32)
        if step == 0:
            shrunk_own[1] = total.astype(jnp.bfloat16)
        else:
            shrunk_all[core] = total.astype(jnp.bfloat16)
        share_shrunk(step + 1).start()

    operands = [
        pltpu.make_async_copy(source, target, operand_sems.at[number])
        for number, (source, target) in enumerate(
            [
                (gain_hbm, gain), (segment_hbm, segment_in), (request_hbm, request_position),
                (in_use_hbm, in_use), (slots_hbm, slots), (table_hbm, table),
            ]
        )
    ]
    load_tokens(part).start()
    for operand in operands:
        operand.start()
    for step in range(1, 4):
        load_tokens(lax.rem(part + step, 4)).start()

    barrier = pltpu.get_barrier_semaphore()

    def greet(req, tp):
        pl.semaphore_signal(
            barrier, inc=1, device_id={"req": req, "tp": tp}, device_id_type=MESH
        )

    for hop in (1, 2, 3):
        greet(2 * lax.rem(z + hop, 4) + y, part)
    greet(y_mate, part)
    greet(me, core_mate)
    greet(me, x_mate)
    pl.semaphore_wait(barrier, 6)

    for index in range(AHEAD):
        for hop in (1, 3, 2):
            along(index, hop).start()
    for index in range(PIECES):
        across(index).start()

    operands[0].wait()
    gains = jnp.concatenate([gain[i : i + 1, :] for i in range(16)], axis=1).astype(jnp.float32)

    def normalise(quarter):
        load_tokens(quarter).wait()

        def some(step, carry):
            rows = pl.ds(pl.multiple_of(quarter * SPAN + step * 32, 32), 32)
            floats = tok[rows, :].astype(jnp.float32)
            mean = jnp.mean(floats * floats, axis=-1, keepdims=True)
            normed[mine, rows, :] = (floats * lax.rsqrt(mean + norm_eps) * gains).astype(
                jnp.bfloat16
            )
            return carry

        lax.fori_loop(0, SPAN // 32, some, 0)

    def prepare(which):
        facts = info[which]
        columns = facts.T
        for block in range(4):
            first = max(0, block - 2) * SPAN
            width = min(block + 1, 3) * SPAN
            query_segment = columns[block * SPAN : (block + 1) * SPAN, 0:1]
            key_segment = facts[0:1, first : first + width]
            query_order = block * SPAN + lax.broadcasted_iota(jnp.int32, (SPAN, width), 0)
            key_order = first + lax.broadcasted_iota(jnp.int32, (SPAN, width), 1)
            allowed = (query_segment == key_segment) & (key_order <= query_order)
            limit[which, pl.ds(block * SPAN, SPAN), pl.ds(0, width)] = jnp.where(
                allowed, FAR, NEVER
            )
        lane = lax.broadcasted_iota(jnp.int32, (4 * SPAN, REACH), 1).astype(jnp.float32)
        chosen = jnp.where(columns[:, 2:3] == lane, 1.0, 0.0).astype(jnp.bfloat16)
        rotation[which] = jnp.dot(
            chosen, table[0], preferred_element_type=jnp.float32
        ) + jnp.dot(chosen, table[1], preferred_element_type=jnp.float32)

    def shrink(which):
        columns = pl.ds(pl.multiple_of(mine * 1024, 1024), 1024)
        product = lax.dot_general(
            down_all[...].reshape(8 * RANK, 1024),
            normed[which, :, columns],
            NT,
            preferred_element_type=jnp.float32,
        )
        places = info[which][1:2, :]
        total = jnp.zeros((RANK, product.shape[1]), jnp.float32)
        for origin in range(8):
            wanted = (2 * origin + x).astype(jnp.float32)
            total = total + jnp.where(
                places == wanted, product[origin * RANK : (origin + 1) * RANK], 0.0
            )
        at = pl.ds(pl.multiple_of(which * 512, 512), 512)
        shrunk_own[0, :, at] = total.astype(jnp.bfloat16)

    def projected(which, index):
        return jnp.dot(
            normed[which],
            weight_all[weight_slot[index]].reshape(8 * 256, 128),
            preferred_element_type=jnp.float32,
        )

    def lay(which, kind):
        columns = info[which].T
        at = pl.ds(pl.multiple_of(which * 512, 512), 512)
        compact = shrunk_all[kind, :, at].astype(jnp.float32)
        padded = jnp.concatenate(
            [compact, jnp.zeros((128 - RANK, compact.shape[1]), jnp.float32)], axis=0
        ).T
        lane = lax.broadcasted_iota(jnp.int32, (128, PLACES * RANK), 1)
        row = lax.broadcasted_iota(jnp.int32, (128, PLACES * RANK), 0)
        tile = jnp.where(lane % RANK == row, 1.0, 0.0).astype(jnp.bfloat16)
        tiled = jnp.dot(
            padded.astype(jnp.bfloat16), tile, preferred_element_type=jnp.float32
        )
        lanes = lax.broadcasted_iota(jnp.int32, tiled.shape, 1) // RANK
        laid[which, kind] = jnp.where(
            columns[:, 1:2] == lanes.astype(jnp.float32), tiled, 0.0
        ).astype(jnp.bfloat16)

    def change(which, kind, pair):
        ups = up_all[:, :, pl.ds(pair * 128, 128)].reshape(8, 2, 2, RANK, 128)
        return adapter_scale * jnp.dot(
            laid[which, kind],
            ups[:, :, kind].reshape(PLACES * RANK, 128),
            preferred_element_type=jnp.float32,
        )

    def rotated(which, value):
        half = HEAD_WIDTH // 2
        low = lax.broadcasted_iota(jnp.int32, (512, 128), 1) % HEAD_WIDTH < half
        swapped = jnp.where(low, pltpu.roll(value, 128 - half, 1), pltpu.roll(value, half, 1))
        return value * rotation[which, :, 0:128] + swapped * rotation[which, :, 128:256]

    def make_key(pair, which):
        key = projected(which, KEY_1 if pair else KEY_0)
        key_heads[which, pair] = rotated(which, key).astype(jnp.bfloat16)

    def make_query(pair, which):
        query = projected(which, QUERY_1 if pair else QUERY_0) + change(which, 0, pair)
        query_heads[which, pair] = (rotated(which, query) * 0.125).astype(jnp.bfloat16)

    def make_value(pair, which):
        value = projected(which, VALUE_1 if pair else VALUE_0) + change(which, 1, pair)
        value_heads[which, pair] = value.astype(jnp.bfloat16)

    def share_attended(which, pair):
        held = attended.at[mine, pair, which]
        return remote(
            held, held, attended_send.at[pair, which], attended_recv.at[pair, which], req=z_mate
        )

    def attend(which, pair):
        left = lax.broadcasted_iota(jnp.int32, (SPAN, 128), 1) < HEAD_WIDTH
        spans = [(max(0, number - 2) * SPAN, min(number + 1, 3) * SPAN) for number in range(4)]
        rows = [pl.ds(number * SPAN, SPAN) for number in range(4)]
        scores = []
        for number, (first, width) in enumerate(spans):
            query = query_heads[which, pair, rows[number], :]
            zero = jnp.zeros_like(query)
            both = jnp.concatenate(
                [jnp.where(left, query, zero), jnp.where(left, zero, query)], axis=0
            )
            keys = key_heads[which, pair, pl.ds(first, width), :]
            score = lax.dot_general(both, keys, NT, preferred_element_type=jnp.float32)
            bound = limit[which, rows[number], pl.ds(0, width)]
            scores.append(jnp.minimum(score, jnp.concatenate([bound, bound], axis=0)))
        exponents = [
            jnp.exp(score - jnp.max(score, axis=-1, keepdims=True)).astype(jnp.bfloat16)
            for score in scores
        ]
        results = []
        for (first, width), exponent in zip(spans, exponents):
            values = value_heads[which, pair, pl.ds(first, width), :]
            wide = jnp.concatenate([values, jnp.ones_like(values)], axis=1)
            results.append(jnp.dot(exponent, wide, preferred_element_type=jnp.float32))
        for number, result in enumerate(results):
            divided = result[:, 0:128] / result[:, 128:256]
            attended[mine, pair, which, rows[number], :] = jnp.where(
                left, divided[0:SPAN], divided[SPAN : 2 * SPAN]
            ).astype(jnp.bfloat16)
        share_attended(which, pair).start()

    def lay_all(which, carry):
        lay(which, 0)
        lay(which, 1)
        return carry

    normalise(part)
    share_tokens(0).start()
    for operand in operands[1:]:
        operand.wait()
    segment = segment_in[...].astype(jnp.float32)
    ordinal = lax.broadcasted_iota(jnp.int32, segment.shape, 1).astype(jnp.float32)
    place = jnp.zeros_like(segment)
    start = jnp.zeros_like(segment)
    for request in range(request_position.shape[1]):
        slot = slots[in_use[request_position[0, request]]]
        here = segment == float(request)
        place = jnp.where(here, slot.astype(jnp.float32), place)
        before = jnp.sum(jnp.where(segment < float(request), 1.0, 0.0), axis=1, keepdims=True)
        start = jnp.where(here, before, start)
    info[mine] = jnp.concatenate(
        [segment, place, ordinal - start, jnp.zeros((5, segment.shape[1]), jnp.float32)], axis=0
    )
    share_info().start()
    for index in range(PIECES):
        keep(index).start()
    normalise(lax.rem(part + 1, 4))
    pump(DOWN)
    share_tokens(1).start()
    normalise(lax.rem(part + 2, 4))
    pump(QUERY_0, (1, 3))
    normalise(lax.rem(part + 3, 4))
    pump(QUERY_0, (2,))
    share_tokens(2).start()
    share_tokens(3).start()
    spread(0)
    prepare(mine)
    pump(KEY_0)
    spread(1)
    share_info().wait_recv()
    prepare(other)
    pump(UP)
    spread(2)
    pass_tokens(0)
    complete(DOWN)
    shrink(mine)
    pump(VALUE_0, (1, 3))
    spread(3)
    pass_tokens(1)
    pump(VALUE_0, (2,))
    complete(KEY_0)
    make_key(0, mine)
    pass_tokens(2)
    pass_tokens(3)
    pump(QUERY_1, (1, 3))
    for step in range(SPAN // TOKEN_ROWS):
        tokens_arrived(core_mate, step)
        tokens_arrived(2 * (1 - x) + 1 - core, step)
    shrink(other)
    share_shrunk(0).start()
    pump(QUERY_1, (2,))
    make_key(0, other)
    add_shrunk(0)
    complete(QUERY_0)
    complete(UP)
    add_shrunk(1)
    pump(KEY_1, (1,))
    share_shrunk(2).wait_recv()
    lax.fori_loop(0, 2, lay_all, 0)
    pump(KEY_1, (3, 2))
    make_query(0, other)
    make_query(0, mine)
    complete(VALUE_0)
    make_value(0, other)
    pump(VALUE_1, (1,))
    make_value(0, mine)
    attend(other, 0)
    pump(VALUE_1, (3, 2))
    complete(QUERY_1)
    make_query(1, other)
    make_query(1, mine)
    attend(mine, 0)
    pump(OUTPUT_0, (1,))
    complete(KEY_1)
    make_key(1, other)
    make_key(1, mine)
    pump(OUTPUT_0, (3,))
    complete(VALUE_1)
    make_value(1, other)
    attend(other, 1)
    make_value(1, mine)
    attend(mine, 1)
    pump(OUTPUT_0, (2,))
    pump(OUTPUT_1)
    keep(OUTPUT_0).wait()
    keep(OUTPUT_1).wait()

    chunks = sent_core.shape[2]
    rows_of = sent_core.shape[4]

    for pair in range(2):
        for which in range(2):
            held = attended.at[other, pair, which]
            remote(
                held, held, attended_send.at[pair, which], attended_recv.at[pair, which],
                req=z_mate,
            ).wait_recv()

    def rows_at(chunk):
        return pl.ds(pl.multiple_of(chunk * rows_of, rows_of), rows_of)

    def product(side, to_core, which, chunk):
        heads = jnp.concatenate(
            [attended[z_of, pair, which, rows_at(chunk), :] for z_of in range(2) for pair in range(2)],
            axis=1,
        )
        columns = jnp.concatenate(
            [output_all[2 * (2 * x_of + to_core) + side] for x_of in range(2)], axis=1
        )
        return jnp.dot(heads, columns, preferred_element_type=jnp.float32)

    def core_copy(phase, which, chunk):
        return remote(
            sent_core.at[phase, which, chunk], got_core.at[phase, which, chunk],
            core_send.at[phase, which, chunk], core_recv.at[phase, which, chunk], tp=core_mate,
        )

    def x_copy(phase, which, chunk):
        return remote(
            sent_x.at[phase, which, chunk], got_x.at[phase, which, chunk],
            x_send.at[phase, which, chunk], x_recv.at[phase, which, chunk], tp=x_mate,
        )

    def z_copy(phase, chunk):
        return remote(
            sent_z.at[phase, chunk], got_z.at[phase, chunk],
            z_send.at[phase, chunk], z_recv.at[phase, chunk], req=z_mate,
        )

    def write(side, half, chunk, values):
        first = side * 256 + half * 128
        residual = tok[rows_at(chunk), pl.ds(pl.multiple_of(part * 512 + first, 128), 128)]
        out[rows_at(chunk), pl.ds(pl.multiple_of(first, 128), 128)] = (
            values + residual.astype(jnp.float32)
        ).astype(jnp.bfloat16)

    for phase in range(2):
        side = y if phase == 0 else 1 - y
        if phase == 1:
            for hop in (0, 1, 3, 2):
                arrived(OUTPUT_0, 2 * lax.rem(z + hop, 4) + 1 - y)
                arrived(OUTPUT_1, 2 * lax.rem(z + hop, 4) + 1 - y)
        for which in (other, mine):

            def first(chunk, carry):
                share = product(side, 1 - core, which, chunk)
                for x_of in range(2):
                    sent_core[phase, which, chunk, x_of] = share[
                        :, x_of * 128 : (x_of + 1) * 128
                    ].astype(jnp.bfloat16)
                core_copy(phase, which, chunk).start()
                return carry

            lax.fori_loop(0, chunks, first, 0)

            def second(chunk, carry):
                share = product(side, core, which, chunk)
                core_copy(phase, which, chunk).wait_recv()
                got = got_core[phase, which, chunk].astype(jnp.float32)
                totals = [share[:, 0:128] + got[0], share[:, 128:256] + got[1]]
                first_x = x == 0
                sent_x[phase, which, chunk] = jnp.where(first_x, totals[1], totals[0]).astype(
                    jnp.bfloat16
                )
                x_copy(phase, which, chunk).start()
                kept[phase, which, chunk] = jnp.where(first_x, totals[0], totals[1])
                return carry

            lax.fori_loop(0, chunks, second, 0)

    for phase in range(2):
        side = y if phase == 0 else 1 - y

        def third(chunk, carry):
            x_copy(phase, other, chunk).wait_recv()
            sent_z[phase, chunk] = (
                kept[phase, other, chunk] + got_x[phase, other, chunk].astype(jnp.float32)
            ).astype(jnp.bfloat16)
            z_copy(phase, chunk).start()
            return carry

        lax.fori_loop(0, chunks, third, 0)

    for phase in range(2):
        side = y if phase == 0 else 1 - y

        def own(chunk, carry):
            x_copy(phase, mine, chunk).wait_recv()
            write(
                side, mine, chunk,
                kept[phase, mine, chunk] + got_x[phase, mine, chunk].astype(jnp.float32),
            )
            return carry

        lax.fori_loop(0, chunks, own, 0)

    for phase in range(2):
        side = y if phase == 0 else 1 - y

        def returned(chunk, carry):
            z_copy(phase, chunk).wait_recv()
            write(side, other, chunk, got_z[phase, chunk].astype(jnp.float32))
            return carry

        lax.fori_loop(0, chunks, returned, 0)

    for index in range(PIECES):
        for hop in (1, 2, 3):
            along(index, hop).wait_send()
            onward(index, hop).wait_send()
        across(index).wait_send()
    for step in range(SPAN // TOKEN_ROWS):
        share_tokens(step).wait_send()
        for slot in (1, 2, 3):
            spread_tokens(slot, step).wait_send()
    share_info().wait_send()
    for step in range(3):
        share_shrunk(step).wait_send()
    for pair in range(2):
        for which in range(2):
            share_attended(which, pair).wait_send()
    for phase in range(2):
        for chunk in range(chunks):
            for which in range(2):
                core_copy(phase, which, chunk).wait_send()
                x_copy(phase, which, chunk).wait_send()
            z_copy(phase, chunk).wait_send()


def fused_layer(
    tokens, segment, request_position, in_use, slots, gain,
    query_weight, key_weight, value_weight, output_weight, down, up,
):
    bf16, f32 = jnp.bfloat16, jnp.float32
    rows, width = tokens.shape
    chunks = 2
    piece = rows // chunks
    hbm = pl.BlockSpec(memory_space=pltpu.HBM)
    dma = pltpu.SemaphoreType.DMA
    return pl.pallas_call(
        layer_kernel,
        out_shape=jax.ShapeDtypeStruct((rows, 512), bf16),
        in_specs=[hbm] * 13,
        out_specs=pl.BlockSpec(memory_space=pltpu.VMEM),
        scratch_shapes=[
            pltpu.VMEM(segment.shape, jnp.int32),
            pltpu.SMEM(request_position.shape, jnp.int32),
            pltpu.SMEM(in_use.shape, jnp.int32),
            pltpu.SMEM(slots.shape, jnp.int32),
            pltpu.VMEM((16, 128), bf16),
            pltpu.VMEM((2, REACH, 256), bf16),
            dma((6,)),
            pltpu.VMEM((rows, width), bf16),
            pltpu.VMEM((2, rows, width), bf16),
            pltpu.VMEM((2, 8, rows), f32),
            pltpu.VMEM((2, rows, 3 * SPAN), f32),
            pltpu.VMEM((2, rows, 256), f32),
            pltpu.VMEM((8, RANK, 1024), bf16),
            pltpu.VMEM((6, 8, 256, 128), bf16),
            pltpu.VMEM((8, 64, 256), bf16),
            pltpu.VMEM((8, 512, 128), bf16),
            pltpu.VMEM((2, RANK, 2 * rows), bf16),
            pltpu.VMEM((2, RANK, 2 * rows), bf16),
            pltpu.VMEM((2, RANK, 2 * rows), bf16),
            pltpu.VMEM((2, 2, rows, 256), bf16),
            pltpu.VMEM((2, 2, rows, 128), bf16),
            pltpu.VMEM((2, 2, rows, 128), bf16),
            pltpu.VMEM((2, 2, rows, 128), bf16),
            pltpu.VMEM((2, 2, 2, rows, 128), bf16),
            pltpu.VMEM((2, 2, chunks, 2, piece, 128), bf16),
            pltpu.VMEM((2, 2, chunks, 2, piece, 128), bf16),
            pltpu.VMEM((2, 2, chunks, piece, 128), bf16),
            pltpu.VMEM((2, 2, chunks, piece, 128), bf16),
            pltpu.VMEM((2, 2, chunks, piece, 128), f32),
            pltpu.VMEM((2, chunks, piece, 128), bf16),
            pltpu.VMEM((2, chunks, piece, 128), bf16),
            dma((4,)),
            dma((PIECES, 7)),
            dma((PIECES, 8)),
            dma((PIECES,)),
            dma((4, SPAN // TOKEN_ROWS)),
            dma((4, SPAN // TOKEN_ROWS)),
            dma((2,)),
            dma((3,)),
            dma((3,)),
            dma((2, 2)),
            dma((2, 2)),
            dma((2, 2, chunks)),
            dma((2, 2, chunks)),
            dma((2, 2, chunks)),
            dma((2, 2, chunks)),
            dma((2, chunks)),
            dma((2, chunks)),
        ],
        compiler_params=pltpu.CompilerParams(
            collective_id=0, has_side_effects=True, vmem_limit_bytes=56 * 1024 * 1024
        ),
    )(
        tokens, segment, request_position, in_use, slots, gain.reshape(16, 128),
        jnp.asarray(rotation_tables()),
        down.reshape(-1, width), query_weight, key_weight, value_weight,
        up.reshape(-1, up.shape[3]), output_weight,
    )


def active_rows(stored, active_slots):
    slot_total = stored.shape[0]
    held = lax.axis_index("req") * slot_total + jnp.arange(slot_total, dtype=jnp.int32)
    chosen = (active_slots[:, None] == held[None, :]).astype(stored.dtype)
    rows = jnp.einsum(
        "as,srd->ard", chosen, stored, preferred_element_type=jnp.float32
    ).astype(stored.dtype)
    return lax.psum(rows, "req").reshape(-1, stored.shape[2])


def positions_of(segment):
    ordinal = jnp.arange(segment.shape[0], dtype=jnp.int32)
    before = segment[None, :] < segment[:, None]
    return ordinal - jnp.sum(before.astype(jnp.int32), axis=1)


def apply_rotation(values, token_positions):
    half_dim = HEAD_WIDTH // 2
    frequency = rope_base ** (-(jnp.arange(half_dim, dtype=jnp.float32) * 2.0 / HEAD_WIDTH))
    angles = token_positions.astype(jnp.float32)[:, None] * frequency[None, :]
    cosine = jnp.cos(angles)[:, None, :]
    sine_part = jnp.sin(angles)[:, None, :]
    first_half = values[..., :half_dim]
    second_half = values[..., half_dim:]
    return jnp.concatenate(
        [
            first_half * cosine - second_half * sine_part,
            second_half * cosine + first_half * sine_part,
        ],
        axis=-1,
    )


def attend(query_per_head, key_heads, value_per_head, segment):
    scores = (
        jnp.einsum("qhd,khd->hqk", query_per_head, key_heads, preferred_element_type=jnp.float32)
        * 0.125
    )
    ordinal = jnp.arange(segment.shape[0], dtype=jnp.int32)
    allowed = (segment[:, None] == segment[None, :]) & (ordinal[None, :] <= ordinal[:, None])
    scores = jnp.where(allowed[None], scores, jnp.float32(-1e30))
    row_peak = jnp.max(scores, axis=-1, keepdims=True)
    exponent = jnp.where(allowed[None], jnp.exp(scores - row_peak), jnp.float32(0.0))
    weights = (exponent / jnp.sum(exponent, axis=-1, keepdims=True)).astype(jnp.bfloat16)
    return jnp.einsum(
        "hqk,khd->qhd", weights, value_per_head, preferred_element_type=jnp.float32
    ).astype(jnp.bfloat16)


def local(
    tokens,
    token_request_number,
    request_adapter_position,
    adapters_in_use,
    adapter_storage_slot,
    input_norm_gain,
    query_weight,
    key_weight,
    value_weight,
    output_weight,
    adapter_down_weight,
    adapter_up_weight,
):
    if (
        lax.axis_size("req") == 8
        and lax.axis_size("tp") == 4
        and tokens.shape == (512, 2048)
        and adapter_down_weight.shape == (2, 2, 16, 2048)
    ):
        return fused_layer(
            tokens,
            token_request_number,
            request_adapter_position,
            adapters_in_use,
            adapter_storage_slot,
            input_norm_gain,
            query_weight,
            key_weight,
            value_weight,
            output_weight,
            adapter_down_weight,
            adapter_up_weight,
        )
    row_total, model_width = tokens.shape
    local_width = query_weight.shape[1]
    reduced_rows = adapter_down_weight.shape[2]
    slot_total = adapter_down_weight.shape[0]
    segment = token_request_number[0]
    request_adapters = request_adapter_position[0]
    tp_total = lax.axis_size("tp")
    req_total = lax.axis_size("req")
    part_rows = reduced_rows // tp_total
    share = 2 * part_rows
    down_part = lax.dynamic_slice_in_dim(
        adapter_down_weight, lax.axis_index("tp") * part_rows, part_rows, 2
    ).reshape(slot_total, share, model_width)
    up_part = adapter_up_weight.reshape(slot_total, 2 * reduced_rows, local_width)
    active_slots = jnp.take(adapter_storage_slot, adapters_in_use, axis=0)
    place_total = active_slots.shape[0]
    request_places = request_adapters
    member = segment[:, None] == jnp.arange(request_adapters.shape[0], dtype=jnp.int32)[None, :]
    token_place = jnp.sum(
        jnp.where(member, request_places[None, :], jnp.zeros_like(request_places)[None, :]),
        axis=1,
    )
    column = jnp.arange(place_total * share, dtype=jnp.int32)
    mask = (token_place[:, None] == (column // share)[None, :]).astype(jnp.bfloat16)
    lanes = max(128, tp_total * share)
    fold = (lax.axis_index("tp") * share + column % share)[:, None] == jnp.arange(
        lanes, dtype=jnp.int32
    )[None, :]
    fold = fold.astype(jnp.bfloat16)
    floats = tokens.astype(jnp.float32)
    normed = (
        floats
        * lax.rsqrt(jnp.mean(floats * floats, axis=-1, keepdims=True) + norm_eps)
        * input_norm_gain.astype(jnp.float32)
    ).astype(jnp.bfloat16)
    down_all = active_rows(down_part, active_slots)
    up_all = active_rows(up_part, active_slots)
    output_full = lax.all_gather(output_weight, "req", axis=1, tiled=True)
    query_plain, key_base, value_plain = [
        jnp.dot(
            normed,
            lax.all_gather(weight, "req", axis=0, tiled=True),
            preferred_element_type=jnp.float32,
        )
        for weight in (query_weight, key_weight, value_weight)
    ]
    shrunk_all = lax.dot_general(
        normed, down_all, (((1,), (1,)), ((), ())), preferred_element_type=jnp.float32
    ).astype(jnp.bfloat16)
    shrunk = lax.psum(
        jnp.dot(shrunk_all * mask, fold, preferred_element_type=jnp.float32), "tp"
    ).astype(jnp.bfloat16)
    shrunk = shrunk[:, : tp_total * share]
    source = jnp.arange(tp_total * share, dtype=jnp.int32)
    source_kind = (source % share) // part_rows
    source_rank = (source // share) * part_rows + source % part_rows
    target = jnp.arange(place_total * reduced_rows, dtype=jnp.int32)
    mine = token_place[:, None] == (target // reduced_rows)[None, :]
    up_all = up_all.reshape(place_total, 2, reduced_rows, local_width)

    def change_of(kind):
        spread_map = (source_kind == kind)[:, None] & (
            source_rank[:, None] == (target % reduced_rows)[None, :]
        )
        spread = jnp.dot(
            shrunk, spread_map.astype(jnp.bfloat16), preferred_element_type=jnp.float32
        ).astype(jnp.bfloat16)
        spread = jnp.where(mine, spread, jnp.zeros((), jnp.bfloat16))
        return jnp.dot(
            spread,
            up_all[:, kind].reshape(place_total * reduced_rows, local_width),
            preferred_element_type=jnp.float32,
        )

    query_change = change_of(0)
    value_change = change_of(1)
    head_total = local_width // HEAD_WIDTH
    token_positions = positions_of(segment)
    query_per_head = apply_rotation(
        (query_plain + adapter_scale * query_change).reshape(row_total, head_total, HEAD_WIDTH),
        token_positions,
    ).astype(jnp.bfloat16)
    key_heads = apply_rotation(
        key_base.reshape(row_total, head_total, HEAD_WIDTH), token_positions
    ).astype(jnp.bfloat16)
    value_per_head = (
        (value_plain + adapter_scale * value_change)
        .astype(jnp.bfloat16)
        .reshape(row_total, head_total, HEAD_WIDTH)
    )
    attended = attend(query_per_head, key_heads, value_per_head, segment).reshape(
        row_total, local_width
    )
    share_width = model_width // tp_total
    residual_part = lax.dynamic_slice_in_dim(
        tokens, lax.axis_index("tp") * share_width, share_width, 1
    )
    partial_out = jnp.dot(attended, output_full, preferred_element_type=jnp.float32)
    summed = lax.psum_scatter(
        partial_out.astype(jnp.bfloat16), "tp", scatter_dimension=1, tiled=True
    ).astype(jnp.float32)
    return (summed + residual_part.astype(jnp.float32)).astype(jnp.bfloat16)


def solution(mesh):
    in_specs = (
        P("req", None),
        P("req", None),
        P("req", None),
        P(),
        P(),
        P(),
        P("req", "tp"),
        P("req", "tp"),
        P("req", "tp"),
        P("tp", "req"),
        P("req", None, None, None),
        P("req", None, None, "tp"),
    )
    out_specs = P("req", "tp")
    return jax.shard_map(local, mesh=mesh, in_specs=in_specs, out_specs=out_specs, check_vma=False)
```
